128 devices in a mesh: seq: 4 (over z_lo, core), res: 32 (over y, x, z_hi).
Axes of the slice: x: 4, y: 4, z: 4 (z_hi: 2, z_lo: 2; z = z_hi * 2 + z_lo), core: 2. Of those that a mesh axis runs over, the one named last changes fastest.
Arguments:
- homolog_embedding: bfloat16 [16, 2048, 256], P('seq', 'res'), may hold values from -6 to 6
- pair_input_rows: bfloat16 [2048, 2048, 128], P('res', 'seq'), may hold values from -256 to 256
- incoming_slope: bfloat16 [16, 2048, 256], P('seq', 'res'), may hold values from -6 to 6
- rescale_factor: float32 [256], replicated, may hold values from 0.25 to 1.75
- probe_weights: bfloat16 [256, 256], replicated, may hold values from -0.375 to 0.375
- lookup_weights: bfloat16 [256, 256], replicated, may hold values from -0.375 to 0.375
- content_weights: bfloat16 [256, 256], replicated, may hold values from -0.375 to 0.375
- sigmoid_weights: bfloat16 [256, 256], replicated, may hold values from -0.375 to 0.375
- final_projection: bfloat16 [256, 256], replicated, may hold values from -0.375 to 0.375
- pair_bias_matrix: bfloat16 [128, 8], replicated, may hold values from -1 to 1
Outputs:
- alignment_rows_gradient: bfloat16 [16, 2048, 256], P('seq', 'res')
- pair_input_gradient: bfloat16 [2048, 2048, 128], P('res', 'seq')
- layer_gain_gradient: float32 [256], replicated
- query_matrix_gradient: float32 [256, 256], replicated
- key_matrix_gradient: float32 [256, 256], replicated
- value_matrix_gradient: float32 [256, 256], replicated
- gate_matrix_gradient: float32 [256, 256], replicated
- final_projection_slope: float32 [256, 256], replicated
- pair_bias_matrix_gradient: float32 [128, 8], replicated
The draws below stay inside these ranges and needn't reach their ends.
All inputs are finite; a program needn't handle non-finite values.
Results may differ from the reference program's by a relative error of at most 0.0034.
The reference program's roundings to bfloat16 on the way count: a program that leaves them out, or rounds other values in their place, can miss the bound.
Values may be sent and summed in bfloat16 or wider, within the bound.
A program may use at most 128 MiB of HBM per device.

```python
import functools
import math
import jax
import jax.numpy as jnp
from jax import lax

FEATURE_DEPTH = 256
H = 8
CZ = 128
HOMOLOG_NUMBER = 16
CHAIN_LENGTH = 2048


def bias_weight_values(key):
    raw_values = jax.random.normal(jax.random.fold_in(key, 101), (CZ, H), jnp.float32) / math.sqrt(CZ)
    return jnp.clip(raw_values, -1.0, 1.0).astype(jnp.bfloat16).astype(jnp.float32)


def draw_pair_bias_matrix(key, part):
    return bias_weight_values(key).astype(jnp.bfloat16)


def draw_pair_input_rows(key, part):
    result = jnp.clip(jax.random.normal(jax.random.fold_in(key, 206), (CHAIN_LENGTH, CHAIN_LENGTH, CZ), jnp.float32), -6.0, 6.0)
    return jnp.clip(result, -256.0, 256.0).astype(jnp.bfloat16)


def shard_levels(own_key, dims, pieces, low, high):
    loudness = 1.0
    for position, parts in pieces:
        draws = jax.random.uniform(jax.random.fold_in(jax.random.fold_in(own_key, 6), position), (parts,), jnp.float32, low / len(pieces), high / len(pieces))
        loudness = loudness * jnp.repeat(jnp.exp(draws), dims[position] // parts).reshape((-1,) + (1,) * (len(dims) - 1 - position))
    return loudness


def centred(rng, dims, spread, reach, shards=(), held_as=jnp.bfloat16):
    gain = shard_levels(rng, dims, shards, -0.22, 0.18) if shards else 1.0
    entries = jax.random.normal(rng, dims, jnp.float32) * spread * gain
    return jnp.minimum(jnp.maximum(entries, -reach), reach).astype(held_as)


def setup_inputs(seed: int = 0) -> dict:
    streams_of = jax.random.split(jax.random.key(seed), 11)
    homolog_embedding = centred(streams_of[0], (HOMOLOG_NUMBER, CHAIN_LENGTH, FEATURE_DEPTH), 1.0, 6.0, ((0, 4), (1, 32)))
    pair_input_rows = draw_pair_input_rows(jax.random.fold_in(streams_of[10], 71), 0)
    incoming_slope = centred(streams_of[2], (HOMOLOG_NUMBER, CHAIN_LENGTH, FEATURE_DEPTH), 1.0, 6.0, ((0, 4), (1, 32)))
    rescale_factor = jnp.clip(1.0 + 0.15 * jax.random.normal(streams_of[3], (FEATURE_DEPTH,), jnp.float32), 0.25, 1.75)
    probe_weights = centred(streams_of[4], (FEATURE_DEPTH, FEATURE_DEPTH), FEATURE_DEPTH ** -0.5, 0.375)
    lookup_weights = centred(streams_of[5], (FEATURE_DEPTH, FEATURE_DEPTH), FEATURE_DEPTH ** -0.5, 0.375)
    content_weights = centred(streams_of[6], (FEATURE_DEPTH, FEATURE_DEPTH), FEATURE_DEPTH ** -0.5, 0.375)
    sigmoid_weights = centred(streams_of[7], (FEATURE_DEPTH, FEATURE_DEPTH), FEATURE_DEPTH ** -0.5, 0.375)
    final_projection = centred(streams_of[8], (FEATURE_DEPTH, FEATURE_DEPTH), FEATURE_DEPTH ** -0.5, 0.375)
    pair_bias_matrix = draw_pair_bias_matrix(jax.random.fold_in(streams_of[10], 71), 0)
    return dict(homolog_embedding=homolog_embedding, pair_input_rows=pair_input_rows, incoming_slope=incoming_slope, rescale_factor=rescale_factor, probe_weights=probe_weights, lookup_weights=lookup_weights, content_weights=content_weights, sigmoid_weights=sigmoid_weights, final_projection=final_projection, pair_bias_matrix=pair_bias_matrix)


def layer_norm_rows(alignment_block):
    content_vectors = alignment_block.astype(jnp.float32)
    centered = content_vectors - lax.optimization_barrier(jnp.mean(content_vectors, axis=-1, keepdims=True))
    inverse_deviation = lax.rsqrt(lax.optimization_barrier(jnp.mean(centered * centered, axis=-1, keepdims=True)) + 1e-05)
    return (centered * inverse_deviation, inverse_deviation)

def row_backward(bias_full, head_count, dbias_total, row_inputs):
    probe_vectors, keys_row, values_row, gate_row, derivative_modulated = row_inputs
    query_total, channel_width = probe_vectors.shape
    key_count = keys_row.shape[0]
    head_width = channel_width // head_count
    softmax_scale = 1.0 / math.sqrt(head_width)
    query_heads = probe_vectors.reshape(query_total, head_count, head_width).astype(jnp.float32)
    key_heads = keys_row.reshape(key_count, head_count, head_width).astype(jnp.float32)
    value_heads = values_row.reshape(key_count, head_count, head_width).astype(jnp.float32)
    scores = jnp.einsum('ihd,jhd->hij', query_heads, key_heads) * softmax_scale + bias_full.astype(jnp.float32)
    weights_soft = jax.nn.softmax(scores, axis=-1)
    weights_half = weights_soft.astype(jnp.bfloat16)
    attended = jnp.einsum('hij,jhd->ihd', weights_half.astype(jnp.float32), value_heads).reshape(query_total, channel_width)
    modulated_result = (gate_row * attended).astype(jnp.bfloat16)
    grad_attended = (derivative_modulated * gate_row).astype(jnp.bfloat16)
    derivative_logits_sigmoid = (derivative_modulated * attended * gate_row * (1.0 - gate_row)).astype(jnp.bfloat16)
    grad_heads = grad_attended.reshape(query_total, head_count, head_width).astype(jnp.float32)
    grad_weights = jnp.einsum('ihd,jhd->hij', grad_heads, value_heads)
    row_inner = lax.optimization_barrier(jnp.sum(weights_soft * grad_weights, axis=-1, keepdims=True))
    grad_scores = weights_soft * (grad_weights - row_inner)
    scores_half = grad_scores.astype(jnp.bfloat16).astype(jnp.float32)
    derivative_probe_weights = (jnp.einsum('hij,jhd->ihd', scores_half, key_heads) * softmax_scale).astype(jnp.bfloat16)
    derivative_lookup_weights = jnp.einsum('hij,ihd->jhd', scores_half, query_heads) * softmax_scale
    derivative_content_weights = jnp.einsum('hij,ihd->jhd', weights_half.astype(jnp.float32), grad_heads)
    outputs = (modulated_result, derivative_logits_sigmoid, derivative_probe_weights.reshape(query_total, channel_width), derivative_lookup_weights.reshape(key_count, channel_width), derivative_content_weights.reshape(key_count, channel_width))
    return (dbias_total + grad_scores, outputs)

def reference(homolog_embedding, pair_input_rows, incoming_slope, rescale_factor, probe_weights, lookup_weights, content_weights, sigmoid_weights, final_projection, pair_bias_matrix):
    highest = lax.Precision.HIGHEST
    standardized_rows, inverse_deviation = layer_norm_rows(homolog_embedding)
    rescaled_embedding = (standardized_rows * rescale_factor).astype(jnp.bfloat16)
    rescaled_plain = rescaled_embedding.reshape(-1, FEATURE_DEPTH)
    probe_vectors = jnp.dot(rescaled_plain, probe_weights, preferred_element_type=jnp.float32).astype(jnp.bfloat16).reshape(HOMOLOG_NUMBER, CHAIN_LENGTH, FEATURE_DEPTH)
    lookup_vectors = jnp.dot(rescaled_plain, lookup_weights, preferred_element_type=jnp.float32).astype(jnp.bfloat16).reshape(HOMOLOG_NUMBER, CHAIN_LENGTH, FEATURE_DEPTH)
    content_vectors = jnp.dot(rescaled_plain, content_weights, preferred_element_type=jnp.float32).astype(jnp.bfloat16).reshape(HOMOLOG_NUMBER, CHAIN_LENGTH, FEATURE_DEPTH)
    sigmoid_factors = jax.nn.sigmoid(jnp.dot(rescaled_plain, sigmoid_weights, preferred_element_type=jnp.float32)).reshape(HOMOLOG_NUMBER, CHAIN_LENGTH, FEATURE_DEPTH)
    incoming_slope_plain = incoming_slope.reshape(-1, FEATURE_DEPTH)
    derivative_modulated = jnp.dot(incoming_slope_plain, final_projection.T, preferred_element_type=jnp.float32).reshape(HOMOLOG_NUMBER, CHAIN_LENGTH, FEATURE_DEPTH)
    bias_flat = jnp.dot(pair_input_rows.reshape(-1, CZ), pair_bias_matrix, preferred_element_type=jnp.float32).astype(jnp.bfloat16)
    bias_full = jnp.transpose(bias_flat.reshape(CHAIN_LENGTH, CHAIN_LENGTH, H), (2, 0, 1))
    dbias_init = jnp.zeros((H, CHAIN_LENGTH, CHAIN_LENGTH), jnp.float32)
    dbias_total, row_results = lax.scan(functools.partial(row_backward, bias_full, H), dbias_init, (probe_vectors, lookup_vectors, content_vectors, sigmoid_factors, derivative_modulated))
    modulated_result, derivative_logits_sigmoid, derivative_probe_weights, derivative_lookup_weights, derivative_content_weights = row_results
    probe_plain = derivative_probe_weights.reshape(-1, FEATURE_DEPTH)
    sigmoid_factor_plain = derivative_logits_sigmoid.reshape(-1, FEATURE_DEPTH)
    lookup_plain = derivative_lookup_weights.reshape(-1, FEATURE_DEPTH)
    content_plain = derivative_content_weights.reshape(-1, FEATURE_DEPTH)
    final_projection_slope = jnp.dot(modulated_result.reshape(-1, FEATURE_DEPTH).T, incoming_slope_plain, preferred_element_type=jnp.float32)
    query_matrix_gradient = jnp.dot(rescaled_plain.T, probe_plain, preferred_element_type=jnp.float32)
    gate_matrix_gradient = jnp.dot(rescaled_plain.T, sigmoid_factor_plain, preferred_element_type=jnp.float32)
    normed_wide = rescaled_plain.astype(jnp.float32)
    key_matrix_gradient = jnp.dot(normed_wide.T, lookup_plain, precision=highest)
    value_matrix_gradient = jnp.dot(normed_wide.T, content_plain, precision=highest)
    derivative_rescaled = jnp.dot(probe_plain, probe_weights.T, preferred_element_type=jnp.float32) + jnp.dot(sigmoid_factor_plain, sigmoid_weights.T, preferred_element_type=jnp.float32) + jnp.dot(lookup_plain, lookup_weights.astype(jnp.float32).T, precision=highest) + jnp.dot(content_plain, content_weights.astype(jnp.float32).T, precision=highest)
    derivative_rescaled = derivative_rescaled.reshape(HOMOLOG_NUMBER, CHAIN_LENGTH, FEATURE_DEPTH)
    layer_gain_gradient = lax.optimization_barrier(jnp.sum(derivative_rescaled * standardized_rows, axis=(0, 1)))
    centered_scaled_gradient = derivative_rescaled * rescale_factor
    alignment_rows_gradient = (inverse_deviation * (centered_scaled_gradient - lax.optimization_barrier(jnp.mean(centered_scaled_gradient, axis=-1, keepdims=True)) - standardized_rows * lax.optimization_barrier(jnp.mean(centered_scaled_gradient * standardized_rows, axis=-1, keepdims=True)))).astype(jnp.bfloat16)
    dbias_half = dbias_total.astype(jnp.bfloat16)
    moved = jnp.transpose(dbias_half, (1, 2, 0))

    def project_row(bias_row):
        return jnp.dot(bias_row, pair_bias_matrix.T, preferred_element_type=jnp.float32).astype(jnp.bfloat16)
    pair_input_gradient = lax.map(project_row, moved)
    pair_bias_matrix_gradient = jnp.dot(pair_input_rows.reshape(-1, CZ).T, moved.reshape(-1, H), preferred_element_type=jnp.float32)
    return (alignment_rows_gradient, pair_input_gradient, layer_gain_gradient, query_matrix_gradient, key_matrix_gradient, value_matrix_gradient, gate_matrix_gradient, final_projection_slope, pair_bias_matrix_gradient)
```

```python
import functools
import math

import jax
import jax.numpy as jnp
from jax import lax
from jax.experimental import pallas as pl
from jax.experimental.pallas import tpu as pltpu
from jax.sharding import PartitionSpec as P

MESH = pl.DeviceIdType.MESH
F32 = jnp.float32
BF16 = jnp.bfloat16
VM = pl.BlockSpec(memory_space=pltpu.VMEM)


class Place:
    def __init__(self):
        seq = lax.axis_index("seq")
        res = lax.axis_index("res")
        self.seq, self.res = seq, res
        self.z_lo, self.core = seq // 2, seq % 2
        self.g, self.z_hi = res // 4, res % 2
        self.x_hi = self.g % 2
        x_lo = (res // 2) % 2
        self.h = ((x_lo + self.x_hi) % 2) * 4 + self.z_hi * 2 + self.z_lo

    def spot(self, h):
        return h % 2, ((h // 4 + self.x_hi) % 2) * 2 + (h // 2) % 2

    def member(self, h):
        z_lo, r4 = self.spot(h)
        return (z_lo * 2 + self.core, self.g * 4 + r4)

    def block(self, g):
        return (self.seq, g * 4 + ((self.h // 4 + g % 2) % 2) * 2 + self.z_hi)

    def partner(self):
        return (self.z_lo * 2 + 1 - self.core, self.res)


def enter(devices):
    barrier = pltpu.get_barrier_semaphore()
    for device in devices:
        pl.semaphore_signal(barrier, inc=1, device_id=device, device_id_type=MESH)
    pl.semaphore_wait(barrier, len(devices))


def remote(src, dst, send, recv, device):
    return pltpu.make_async_remote_copy(
        src_ref=src, dst_ref=dst, send_sem=send, recv_sem=recv, device_id=device, device_id_type=MESH
    )


def params(collective_id):
    return pltpu.CompilerParams(
        collective_id=collective_id, has_side_effects=True, vmem_limit_bytes=48 * 1024 * 1024
    )


def aligned(x, n):
    return pl.multiple_of(x * n, n)


def scatter_kernel(t_ref, b_ref, x_ref, bias_ref, ts, tr, bs, br, ps, pr, local):
    p = Place()
    enter([p.member((p.h + k) % 8) for k in range(1, 8)] + [p.partner()])
    z_lo, r4 = p.spot(p.h)
    rows = pl.ds(z_lo * 4, 4)
    toks = pl.ds(aligned(r4, 64), 64)
    cols = pl.ds(aligned(p.seq, 512), 512)
    copies = []
    for k in (4, 3, 5, 2, 6, 1, 7):
        h = (p.h + k) % 8
        dev = p.member(h)
        a = remote(t_ref.at[h], x_ref.at[rows, toks], ts.at[k - 1], tr.at[k - 1], dev)
        b = remote(b_ref.at[h], bias_ref.at[toks, cols], bs.at[k - 1], br.at[k - 1], dev)
        a.start()
        b.start()
        copies += [a, b]
    own = pltpu.make_async_copy(t_ref.at[p.h], x_ref.at[rows, toks], local.at[0])
    own.start()
    own2 = pltpu.make_async_copy(b_ref.at[p.h], bias_ref.at[toks, cols], local.at[1])
    own2.start()
    own.wait()
    own2.wait()
    for c in copies:
        c.wait()
    pair = []
    for b in range(2):
        cols = pl.ds(aligned(b * 2 + p.core, 512), 512)
        c = remote(bias_ref.at[:, cols], bias_ref.at[:, cols], ps.at[b], pr.at[b], p.partner())
        c.start()
        pair.append(c)
    for c in pair:
        c.wait()


def scatter(tokens, bias):
    dma = pltpu.SemaphoreType.DMA
    return pl.pallas_call(
        scatter_kernel,
        out_shape=(
            jax.ShapeDtypeStruct((8, 256, 128), BF16),
            jax.ShapeDtypeStruct((256, 2048), BF16),
        ),
        in_specs=[VM, VM],
        out_specs=(VM, VM),
        scratch_shapes=[dma((7,)), dma((7,)), dma((7,)), dma((7,)), dma((2,)), dma((2,)), dma((2,))],
        compiler_params=params(0),
        name="scatter",
    )(tokens, bias)


def gather_kernel(k_ref, o_ref, ss, rs, local):
    p = Place()
    enter([p.block((p.g + k) % 8) for k in range(1, 8)])
    here = pl.ds(aligned(p.g, 256), 256)
    copies = []
    for k in (4, 3, 5, 2, 6, 1, 7):
        c = remote(k_ref, o_ref.at[:, :, here], ss.at[k - 1], rs.at[k - 1], p.block((p.g + k) % 8))
        c.start()
        copies.append(c)
    own = pltpu.make_async_copy(k_ref, o_ref.at[:, :, here], local)
    own.start()
    own.wait()
    for c in copies:
        c.wait()


def gather(kv):
    dma = pltpu.SemaphoreType.DMA
    return pl.pallas_call(
        gather_kernel,
        out_shape=jax.ShapeDtypeStruct((8, 64, 2048), BF16),
        in_specs=[VM],
        out_specs=VM,
        scratch_shapes=[dma((7,)), dma((7,)), dma],
        compiler_params=params(1),
        name="gather",
    )(kv)


QB = 128


def attention_kernel(x_ref, kv_ref, b_ref, o_ref, dkv_ref, db_ref):
    scale = 1.0 / math.sqrt(32)
    first = pl.program_id(0) == 0
    kt = kv_ref[0, 0:32, :]
    vt = kv_ref[0, 32:64, :]
    tn = (((0,), (0,)), ((), ()))
    nt = (((1,), (1,)), ((), ()))

    dk = jnp.zeros((32, 2048), F32)
    dv = jnp.zeros((32, 2048), F32)
    for n in range(256 // QB):
        q = pl.ds(n * QB, QB)
        qt = x_ref[0, 0:32, q]
        dot = x_ref[0, 96:128, q]
        s = lax.dot_general(qt, kt, tn, preferred_element_type=F32) * scale
        s = s + b_ref[q, :].astype(F32)
        e = jnp.exp(s - jnp.max(s, axis=1, keepdims=True))
        soft = e * (1.0 / jnp.sum(e, axis=1, keepdims=True))
        half = soft.astype(BF16)
        gs = lax.dot_general(dot, vt, tn, preferred_element_type=F32)
        gs = soft * (gs - jnp.sum(soft * gs, axis=1, keepdims=True))
        gh = gs.astype(BF16)

        @pl.when(first)
        def _():
            db_ref[q, :] = gs

        @pl.when(jnp.logical_not(first))
        def _():
            db_ref[q, :] += gs

        o_ref[0, 0:32, q] = lax.dot_general(vt, half, nt, preferred_element_type=F32)
        dq = lax.dot_general(kt, gh, nt, preferred_element_type=F32) * scale
        o_ref[0, 32:64, q] = dq.astype(BF16).astype(F32)
        dk = dk + jnp.dot(qt, gh, preferred_element_type=F32)
        dv = dv + jnp.dot(dot, half, preferred_element_type=F32)
    dkv_ref[0, 0:32, :] = (dk * scale).astype(dkv_ref.dtype)
    dkv_ref[0, 32:64, :] = dv.astype(dkv_ref.dtype)


def attention(x, kv, bias):
    return pl.pallas_call(
        attention_kernel,
        grid=(8,),
        out_shape=(
            jax.ShapeDtypeStruct((8, 64, 256), F32),
            jax.ShapeDtypeStruct((8, 64, 2048), BF16),
            jax.ShapeDtypeStruct((256, 2048), F32),
        ),
        in_specs=[
            pl.BlockSpec((1, 128, 256), lambda s: (s, 0, 0)),
            pl.BlockSpec((1, 64, 2048), lambda s: (s, 0, 0)),
            pl.BlockSpec((256, 2048), lambda s: (0, 0)),
        ],
        out_specs=(
            pl.BlockSpec((1, 64, 256), lambda s: (s, 0, 0)),
            pl.BlockSpec((1, 64, 2048), lambda s: (s, 0, 0)),
            pl.BlockSpec((256, 2048), lambda s: (0, 0)),
        ),
        compiler_params=pltpu.CompilerParams(vmem_limit_bytes=48 * 1024 * 1024),
        name="attention",
    )(x, kv, bias)


def partials_kernel(d_ref, o_ref, buf, ss, rs):
    p = Place()
    enter([p.block((p.g + k) % 8) for k in range(1, 8)])
    copies = []
    for k in (4, 3, 5, 2, 6, 1, 7):
        g = (p.g + k) % 8
        c = remote(
            d_ref.at[:, :, pl.ds(aligned(g, 256), 256)], buf.at[k - 1], ss.at[k - 1], rs.at[k - 1], p.block(g)
        )
        c.start()
        copies.append(c)
    for c in copies:
        c.wait()
    here = pl.ds(aligned(p.g, 256), 256)
    for s in range(8):
        total = d_ref[s, :, here].astype(F32)
        for k in range(7):
            total = total + buf[k, s].astype(F32)
        o_ref[s] = total


def partials(dkv):
    dma = pltpu.SemaphoreType.DMA
    return pl.pallas_call(
        partials_kernel,
        out_shape=jax.ShapeDtypeStruct((8, 64, 256), F32),
        in_specs=[VM],
        out_specs=VM,
        scratch_shapes=[pltpu.VMEM((7, 8, 64, 256), dkv.dtype), dma((7,)), dma((7,))],
        compiler_params=params(2),
        name="partials",
    )(dkv)


def collect_kernel(y_ref, d_ref, t_ref, b_ref, mine, other, ts, tr, bs, br, ps, pr, local):
    p = Place()
    enter([p.member((p.h + k) % 8) for k in range(1, 8)] + [p.partner()])
    copies = []
    for b in range(2):
        cols = pl.ds(aligned(b * 2 + 1 - p.core, 512), 512)
        c = remote(d_ref.at[:, cols], other.at[b], ps.at[b], pr.at[b], p.partner())
        c.start()
        copies.append(c)
    later = []
    for k in (4, 3, 5, 2, 6, 1, 7):
        h = (p.h + k) % 8
        z_lo, r4 = p.spot(h)
        a = remote(
            y_ref.at[pl.ds(z_lo * 4, 4), pl.ds(aligned(r4, 64), 64)],
            t_ref.at[p.h],
            ts.at[k - 1],
            tr.at[k - 1],
            p.member(h),
        )
        a.start()
        later.append(a)
    z_lo, r4 = p.spot(p.h)
    own = pltpu.make_async_copy(
        y_ref.at[pl.ds(z_lo * 4, 4), pl.ds(aligned(r4, 64), 64)], t_ref.at[p.h], local.at[0]
    )
    own.start()
    for b in range(2):
        copies[b].wait()
        cols = pl.ds(aligned(b * 2 + p.core, 512), 512)
        mine[b] = (d_ref[:, cols] + other[b]).astype(BF16)
    for k in (4, 3, 5, 2, 6, 1, 7):
        h = (p.h + k) % 8
        z_lo, r4 = p.spot(h)
        a = remote(
            mine.at[z_lo, pl.ds(aligned(r4, 64), 64)], b_ref.at[p.h], bs.at[k - 1], br.at[k - 1], p.member(h)
        )
        a.start()
        later.append(a)
    z_lo, r4 = p.spot(p.h)
    own2 = pltpu.make_async_copy(mine.at[z_lo, pl.ds(aligned(r4, 64), 64)], b_ref.at[p.h], local.at[1])
    own2.start()
    own.wait()
    own2.wait()
    for a in later:
        a.wait()


def collect(y, d):
    dma = pltpu.SemaphoreType.DMA
    return pl.pallas_call(
        collect_kernel,
        out_shape=(
            jax.ShapeDtypeStruct((8, 4, 64, 128), F32),
            jax.ShapeDtypeStruct((8, 64, 512), BF16),
        ),
        in_specs=[VM, VM],
        out_specs=(VM, VM),
        scratch_shapes=[
            pltpu.VMEM((2, 256, 512), BF16),
            pltpu.VMEM((2, 256, 512), F32),
            dma((7,)), dma((7,)), dma((7,)), dma((7,)), dma((2,)), dma((2,)), dma((2,)),
        ],
        compiler_params=params(3),
        name="collect",
    )(y, d)


def reduce_kernel(w_ref, o_ref, b0, a0, b1, a1, b2, s0, r0, s1, r1, s2, r2, s3, r3, s4, r4, s5, r5):
    p = Place()
    enter(
        [p.member((p.h + k) % 8) for k in range(1, 8)]
        + [p.block((p.g + k) % 8) for k in range(1, 8)]
        + [p.partner()]
    )
    order = (4, 3, 5, 2, 6, 1, 7)
    pair = remote(w_ref.at[1 - p.core], b0, s0, r0, p.partner())
    pair.start()
    pair.wait()
    for m in range(8):
        a0[m] = w_ref[p.core, m] + b0[m]
    copies = []
    for k in order:
        h = (p.h + k) % 8
        c = remote(a0.at[h], b1.at[k - 1], s1.at[k - 1], r1.at[k - 1], p.member(h))
        c.start()
        copies.append(c)
    for c in copies:
        c.wait()
    for m in range(8):
        total = a0[p.h, m]
        for k in range(7):
            total = total + b1[k, m]
        a1[m] = total
    copies = []
    for k in order:
        g = (p.g + k) % 8
        c = remote(a1.at[g], b2.at[k - 1], s2.at[k - 1], r2.at[k - 1], p.block(g))
        c.start()
        copies.append(c)
    for c in copies:
        c.wait()
    total = a1[p.g]
    for k in range(7):
        total = total + b2[k]
    o_ref[p.core, p.h, p.g] = total
    copies = []
    piece = o_ref.at[p.core, p.h, p.g]
    for k in order:
        c = remote(piece, piece, s3.at[k - 1], r3.at[k - 1], p.block((p.g + k) % 8))
        c.start()
        copies.append(c)
    for c in copies:
        c.wait()
    copies = []
    piece = o_ref.at[p.core, p.h]
    for k in order:
        c = remote(piece, piece, s4.at[k - 1], r4.at[k - 1], p.member((p.h + k) % 8))
        c.start()
        copies.append(c)
    for c in copies:
        c.wait()
    piece = o_ref.at[p.core]
    pair = remote(piece, piece, s5, r5, p.partner())
    pair.start()
    pair.wait()


def reduce_all(w):
    dma = pltpu.SemaphoreType.DMA
    n = w.shape[3]
    return pl.pallas_call(
        reduce_kernel,
        out_shape=jax.ShapeDtypeStruct(w.shape, F32),
        in_specs=[VM],
        out_specs=VM,
        scratch_shapes=[
            pltpu.VMEM((8, 8, n, 128), F32),
            pltpu.VMEM((8, 8, n, 128), F32),
            pltpu.VMEM((7, 8, n, 128), F32),
            pltpu.VMEM((8, n, 128), F32),
            pltpu.VMEM((7, n, 128), F32),
            dma, dma, dma((7,)), dma((7,)), dma((7,)), dma((7,)),
            dma((7,)), dma((7,)), dma((7,)), dma((7,)), dma, dma,
        ],
        compiler_params=params(4),
        name="reduce_all",
    )(w)


def body(
    homolog_embedding,
    pair_input_rows,
    incoming_slope,
    rescale_factor,
    probe_weights,
    lookup_weights,
    content_weights,
    sigmoid_weights,
    final_projection,
    pair_bias_matrix,
):
    highest = lax.Precision.HIGHEST
    rows, toks, width = homolog_embedding.shape
    wide = homolog_embedding.astype(F32)
    centered = wide - jnp.mean(wide, axis=-1, keepdims=True)
    inv = lax.rsqrt(jnp.mean(centered * centered, axis=-1, keepdims=True) + 1e-05)
    hat = centered * inv
    plain = (hat * rescale_factor).astype(BF16).reshape(-1, width)
    slope = incoming_slope.reshape(-1, width)

    def dot(a, b):
        return jnp.dot(a, b, preferred_element_type=F32)

    q = dot(plain, probe_weights).astype(BF16)
    k = dot(plain, lookup_weights).astype(BF16)
    v = dot(plain, content_weights).astype(BF16)
    gate = jax.nn.sigmoid(dot(plain, sigmoid_weights))
    grad_gated = dot(slope, final_projection.T)
    grad_att = (grad_gated * gate).astype(BF16)
    tokens = jnp.stack([a.reshape(-1, 8, 32) for a in (q, k, v, grad_att)], axis=2)
    tokens = jnp.transpose(tokens.reshape(-1, 8, 128), (1, 0, 2)).reshape(8, rows, toks, 128)
    bias = jnp.einsum(
        "ijc,ch->hij", pair_input_rows, pair_bias_matrix, preferred_element_type=F32
    ).astype(BF16)

    x, bias_full = scatter(tokens, bias)
    xt = jnp.transpose(x, (0, 2, 1))
    kv = gather(xt[:, 32:96, :])
    out, dkv_part, db = attention(xt, kv, bias_full)
    dkv = partials(dkv_part)
    y = jnp.transpose(jnp.concatenate([out, dkv], axis=1), (0, 2, 1))
    back, db_own = collect(y, db)

    back = jnp.transpose(back.reshape(8, rows * toks, 4, 32), (2, 1, 0, 3)).reshape(4, rows * toks, width)
    attended, dq, dk, dv = back[0], back[1].astype(BF16), back[2], back[3]
    gated = (gate * attended).astype(BF16)
    grad_gate = (grad_gated * attended * gate * (1.0 - gate)).astype(BF16)

    plain_wide = plain.astype(F32)
    part_key = jnp.dot(plain_wide.T, dk, precision=highest)
    part_value = jnp.dot(plain_wide.T, dv, precision=highest)
    part_query = dot(plain.T, dq)
    part_gate = dot(plain.T, grad_gate)
    part_out = dot(gated.T, slope)
    grad_normed = (
        dot(dq, probe_weights.T)
        + dot(grad_gate, sigmoid_weights.T)
        + jnp.dot(dk, lookup_weights.astype(F32).T, precision=highest)
        + jnp.dot(dv, content_weights.astype(F32).T, precision=highest)
    ).reshape(rows, toks, width)
    part_gain = jnp.sum(grad_normed * hat, axis=(0, 1))
    scaled = grad_normed * rescale_factor
    alignment = (
        inv
        * (
            scaled
            - jnp.mean(scaled, axis=-1, keepdims=True)
            - hat * jnp.mean(scaled * hat, axis=-1, keepdims=True)
        )
    ).astype(BF16)
    pair_grad = jnp.einsum(
        "hij,ch->ijc", db_own, pair_bias_matrix, preferred_element_type=F32
    ).astype(BF16)
    part_bias = jnp.einsum("ijc,hij->ch", pair_input_rows, db_own, preferred_element_type=F32)

    packed = jnp.concatenate(
        [
            part_query,
            part_key,
            part_value,
            part_gate,
            part_out,
            part_gain.reshape(1, width),
            part_bias.reshape(4, width),
            jnp.zeros((251, width), F32),
        ],
        axis=0,
    )
    packed = jnp.stack([packed[:, :128], packed[:, 128:]]).reshape(2, 8, 8, 24, 128)
    total = reduce_all(packed).reshape(2, 1536, 128)
    total = jnp.concatenate([total[0], total[1]], axis=1)
    return (
        alignment,
        pair_grad,
        total[1280],
        total[0:256],
        total[256:512],
        total[512:768],
        total[768:1024],
        total[1024:1280],
        total[1281:1285].reshape(128, 8),
    )


def solution(mesh):
    in_specs = (
        P("seq", "res", None),
        P("res", "seq", None),
        P("seq", "res", None),
        P(),
        P(),
        P(),
        P(),
        P(),
        P(),
        P(),
    )
    out_specs = (P("seq", "res", None), P("res", "seq", None), P(), P(), P(), P(), P(), P(), P())
    return jax.shard_map(body, mesh=mesh, in_specs=in_specs, out_specs=out_specs, check_vma=False)
```

```python
import functools
import math

import jax
import jax.numpy as jnp
from jax import lax
from jax.experimental import pallas as pl
from jax.experimental.pallas import tpu as pltpu
from jax.sharding import PartitionSpec as P

MESH = pl.DeviceIdType.MESH
F32 = jnp.float32
BF16 = jnp.bfloat16
VM = pl.BlockSpec(memory_space=pltpu.VMEM)


class Place:
    def __init__(self):
        seq = lax.axis_index("seq")
        res = lax.axis_index("res")
        self.seq, self.res = seq, res
        self.z_lo, self.core = seq // 2, seq % 2
        self.g, self.z_hi = res // 4, res % 2
        self.x_hi = self.g % 2
        x_lo = (res // 2) % 2
        self.h = ((x_lo + self.x_hi) % 2) * 4 + self.z_hi * 2 + self.z_lo

    def spot(self, h):
        return h % 2, ((h // 4 + self.x_hi) % 2) * 2 + (h // 2) % 2

    def member(self, h):
        z_lo, r4 = self.spot(h)
        return (z_lo * 2 + self.core, self.g * 4 + r4)

    def block(self, g):
        return (self.seq, g * 4 + ((self.h // 4 + g % 2) % 2) * 2 + self.z_hi)

    def partner(self):
        return (self.z_lo * 2 + 1 - self.core, self.res)


def enter(devices):
    barrier = pltpu.get_barrier_semaphore()
    for device in devices:
        pl.semaphore_signal(barrier, inc=1, device_id=device, device_id_type=MESH)
    pl.semaphore_wait(barrier, len(devices))


def remote(src, dst, send, recv, device):
    return pltpu.make_async_remote_copy(
        src_ref=src, dst_ref=dst, send_sem=send, recv_sem=recv, device_id=device, device_id_type=MESH
    )


def params(collective_id):
    return pltpu.CompilerParams(
        collective_id=collective_id, has_side_effects=True, vmem_limit_bytes=48 * 1024 * 1024
    )


def aligned(x, n):
    return pl.multiple_of(x * n, n)


ORDER = (4, 3, 5, 2, 6, 1, 7)
CHUNKS = 4
QB = 128


def scatter_kernel(t_ref, x_ref, ts, tr, local):
    p = Place()
    enter([p.member((p.h + k) % 8) for k in range(1, 8)])
    z_lo, r4 = p.spot(p.h)
    here = x_ref.at[pl.ds(z_lo * 4, 4), pl.ds(aligned(r4, 64), 64)]
    copies = []
    for k in ORDER:
        h = (p.h + k) % 8
        a = remote(t_ref.at[h], here, ts.at[k - 1], tr.at[k - 1], p.member(h))
        a.start()
        copies.append(a)
    own = pltpu.make_async_copy(t_ref.at[p.h], here, local)
    own.start()
    own.wait()
    for c in copies:
        c.wait()


def scatter(tokens):
    dma = pltpu.SemaphoreType.DMA
    return pl.pallas_call(
        scatter_kernel,
        out_shape=jax.ShapeDtypeStruct((8, 256, 128), BF16),
        in_specs=[VM],
        out_specs=VM,
        scratch_shapes=[dma((7,)), dma((7,)), dma],
        compiler_params=params(0),
        name="scatter",
    )(tokens)


def row_backward(xt, kv, bias, db, dkv, row):
    scale = 1.0 / math.sqrt(32)
    kt = kv[row, 0:32, :]
    vt = kv[row, 32:64, :]
    tn = (((0,), (0,)), ((), ()))
    nt = (((1,), (1,)), ((), ()))
    dk = jnp.zeros((32, 2048), F32)
    dv = jnp.zeros((32, 2048), F32)
    outs = []
    for n in range(256 // QB):
        q = pl.ds(n * QB, QB)
        qt = xt[row, 0:32, q]
        dot = xt[row, 96:128, q]
        s = lax.dot_general(qt, kt, tn, preferred_element_type=F32) * scale
        s = s + bias[q, :].astype(F32)
        e = jnp.exp(s - jnp.max(s, axis=1, keepdims=True))
        soft = e * (1.0 / jnp.sum(e, axis=1, keepdims=True))
        half = soft.astype(BF16)
        gs = lax.dot_general(dot, vt, tn, preferred_element_type=F32)
        gs = soft * (gs - jnp.sum(soft * gs, axis=1, keepdims=True))
        gh = gs.astype(BF16)
        db[q, :] += gs
        att = lax.dot_general(vt, half, nt, preferred_element_type=F32)
        dq = lax.dot_general(kt, gh, nt, preferred_element_type=F32) * scale
        outs.append(jnp.concatenate([att, dq.astype(BF16).astype(F32)], axis=0))
        dk = dk + jnp.dot(qt, gh, preferred_element_type=F32)
        dv = dv + jnp.dot(dot, half, preferred_element_type=F32)
    dkv[row, 0:32, :] = (dk * scale).astype(dkv.dtype)
    dkv[row, 32:64, :] = dv.astype(dkv.dtype)
    return jnp.concatenate(outs, axis=1)


def main_kernel(
    xt, b_ref, ta, td, bo,
    kv, bias, db, dkv, parts, ya, yd, mine, other,
    ks, kr, bs, br, ps, pr, es, er, as_, ar, ds, dr, fs, fr, hs, hr, local,
):
    p = Place()
    enter(
        [p.member((p.h + k) % 8) for k in range(1, 8)]
        + [p.block((p.g + k) % 8) for k in range(1, 8)]
        + [p.partner()]
    )
    z_lo, r4 = p.spot(p.h)
    toks = pl.ds(aligned(r4, 64), 64)
    here = pl.ds(aligned(p.g, 256), 256)
    per = 8 // CHUNKS

    def keys(c, k):
        rows = pl.ds(c * per, per)
        return remote(
            xt.at[rows, 32:96], kv.at[rows, :, here], ks.at[c, k - 1], kr.at[c, k - 1], p.block((p.g + k) % 8)
        )

    def partial(c, k):
        rows = pl.ds(c * per, per)
        g = (p.g + k) % 8
        return remote(
            dkv.at[rows, :, pl.ds(aligned(g, 256), 256)],
            parts.at[k - 1, rows],
            es.at[c, k - 1],
            er.at[c, k - 1],
            p.block(g),
        )

    first = []
    cols = pl.ds(aligned(p.seq, 512), 512)
    for k in ORDER:
        h = (p.h + k) % 8
        b = remote(b_ref.at[h], bias.at[toks, cols], bs.at[k - 1], br.at[k - 1], p.member(h))
        b.start()
        first.append(b)
        keys(0, k).start()
    own_b = pltpu.make_async_copy(b_ref.at[p.h], bias.at[toks, cols], local.at[0])
    own_b.start()
    own_k = pltpu.make_async_copy(xt.at[:, 32:96], kv.at[:, :, here], local.at[1])
    own_k.start()
    for c in range(1, CHUNKS):
        for k in ORDER:
            keys(c, k).start()
    db[...] = jnp.zeros_like(db)
    own_b.wait()
    own_k.wait()
    for b in first:
        b.wait()
    first = []
    for b in range(2):
        cols = pl.ds(aligned(b * 2 + p.core, 512), 512)
        c = remote(bias.at[:, cols], bias.at[:, cols], ps.at[b], pr.at[b], p.partner())
        c.start()
        first.append(c)
    for c in first:
        c.wait()

    def step(c, carry):
        for k in ORDER:
            keys(c, k).wait_recv()
        outs = []
        for i in range(per):
            outs.append(row_backward(xt, kv, bias, db, dkv, c * per + i))
        for k in ORDER:
            partial(c, k).start()
        ya[c] = jnp.transpose(jnp.concatenate(outs, axis=0))
        return carry

    lax.fori_loop(0, CHUNKS, step, 0)

    pair = []
    for b in range(2):
        cols = pl.ds(aligned(b * 2 + 1 - p.core, 512), 512)
        c = remote(db.at[:, cols], other.at[b], fs.at[b], fr.at[b], p.partner())
        c.start()
        pair.append(c)

    def give(src, dst, send, recv, k):
        h = (p.h + k) % 8
        z, r = p.spot(h)
        return remote(
            src.at[pl.ds(z * 2, 2), pl.ds(aligned(r, 64), 64)], dst.at[p.h], send.at[k - 1], recv.at[k - 1], p.member(h)
        )

    last = []
    for k in ORDER:
        a = give(ya, ta, as_, ar, k)
        a.start()
        last.append(a)
    own_a = pltpu.make_async_copy(ya.at[pl.ds(z_lo * 2, 2), toks], ta.at[p.h], local.at[0])
    own_a.start()
    for b in range(2):
        pair[b].wait()
        cols = pl.ds(aligned(b * 2 + p.core, 512), 512)
        mine[b] = (db[:, cols] + other[b]).astype(BF16)
    for k in ORDER:
        h = (p.h + k) % 8
        z, r = p.spot(h)
        a = remote(
            mine.at[z, pl.ds(aligned(r, 64), 64)], bo.at[p.h], hs.at[k - 1], hr.at[k - 1], p.member(h)
        )
        a.start()
        last.append(a)
    own_m = pltpu.make_async_copy(mine.at[z_lo, toks], bo.at[p.h], local.at[1])
    own_m.start()

    def total(c, carry):
        for k in ORDER:
            partial(c, k).wait_recv()
        outs = []
        for i in range(per):
            row = c * per + i
            t = dkv[row, :, here].astype(F32)
            for k in range(7):
                t = t + parts[k, row].astype(F32)
            outs.append(t)
        yd[c] = jnp.transpose(jnp.concatenate(outs, axis=0))
        return carry

    lax.fori_loop(0, CHUNKS, total, 0)
    for k in ORDER:
        a = give(yd, td, ds, dr, k)
        a.start()
        last.append(a)
    own_d = pltpu.make_async_copy(yd.at[pl.ds(z_lo * 2, 2), toks], td.at[p.h], local.at[2])
    own_d.start()
    own_a.wait()
    own_m.wait()
    own_d.wait()
    for a in last:
        a.wait()

    def drain(c, carry):
        for k in ORDER:
            keys(c, k).wait_send()
            partial(c, k).wait_send()
        return carry

    lax.fori_loop(0, CHUNKS, drain, 0)


def main(xt, bias):
    dma = pltpu.SemaphoreType.DMA
    vmem = pltpu.VMEM
    return pl.pallas_call(
        main_kernel,
        out_shape=(
            jax.ShapeDtypeStruct((8, 2, 64, 128), F32),
            jax.ShapeDtypeStruct((8, 2, 64, 128), F32),
            jax.ShapeDtypeStruct((8, 64, 512), BF16),
        ),
        in_specs=[VM, VM],
        out_specs=(VM, VM, VM),
        scratch_shapes=[
            vmem((8, 64, 2048), BF16),
            vmem((256, 2048), BF16),
            vmem((256, 2048), F32),
            vmem((8, 64, 2048), BF16),
            vmem((7, 8, 64, 256), BF16),
            vmem((4, 256, 128), F32),
            vmem((4, 256, 128), F32),
            vmem((2, 256, 512), BF16),
            vmem((2, 256, 512), F32),
            dma((CHUNKS, 7)), dma((CHUNKS, 7)),
            dma((7,)), dma((7,)),
            dma((2,)), dma((2,)),
            dma((CHUNKS, 7)), dma((CHUNKS, 7)),
            dma((7,)), dma((7,)),
            dma((7,)), dma((7,)),
            dma((2,)), dma((2,)),
            dma((7,)), dma((7,)),
            dma((3,)),
        ],
        compiler_params=params(1),
        name="main",
    )(xt, bias)


def reduce_kernel(w_ref, o_ref, b0, a0, b1, a1, b2, s0, r0, s1, r1, s2, r2, s3, r3, s4, r4, s5, r5):
    p = Place()
    enter(
        [p.member((p.h + k) % 8) for k in range(1, 8)]
        + [p.block((p.g + k) % 8) for k in range(1, 8)]
        + [p.partner()]
    )
    pair = remote(w_ref.at[1 - p.core], b0, s0, r0, p.partner())
    pair.start()
    pair.wait()
    for m in range(8):
        a0[m] = w_ref[p.core, m] + b0[m]
    copies = []
    for k in ORDER:
        h = (p.h + k) % 8
        c = remote(a0.at[h], b1.at[k - 1], s1.at[k - 1], r1.at[k - 1], p.member(h))
        c.start()
        copies.append(c)
    for c in copies:
        c.wait()
    for m in range(8):
        total = a0[p.h, m]
        for k in range(7):
            total = total + b1[k, m]
        a1[m] = total
    copies = []
    for k in ORDER:
        g = (p.g + k) % 8
        c = remote(a1.at[g], b2.at[k - 1], s2.at[k - 1], r2.at[k - 1], p.block(g))
        c.start()
        copies.append(c)
    for c in copies:
        c.wait()
    total = a1[p.g]
    for k in range(7):
        total = total + b2[k]
    o_ref[p.core, p.h, p.g] = total
    copies = []
    piece = o_ref.at[p.core, p.h, p.g]
    for k in ORDER:
        c = remote(piece, piece, s3.at[k - 1], r3.at[k - 1], p.block((p.g + k) % 8))
        c.start()
        copies.append(c)
    for c in copies:
        c.wait()
    copies = []
    piece = o_ref.at[p.core, p.h]
    for k in ORDER:
        c = remote(piece, piece, s4.at[k - 1], r4.at[k - 1], p.member((p.h + k) % 8))
        c.start()
        copies.append(c)
    for c in copies:
        c.wait()
    piece = o_ref.at[p.core]
    pair = remote(piece, piece, s5, r5, p.partner())
    pair.start()
    pair.wait()


def reduce_all(w):
    dma = pltpu.SemaphoreType.DMA
    n = w.shape[3]
    return pl.pallas_call(
        reduce_kernel,
        out_shape=jax.ShapeDtypeStruct(w.shape, F32),
        in_specs=[VM],
        out_specs=VM,
        scratch_shapes=[
            pltpu.VMEM((8, 8, n, 128), F32),
            pltpu.VMEM((8, 8, n, 128), F32),
            pltpu.VMEM((7, 8, n, 128), F32),
            pltpu.VMEM((8, n, 128), F32),
            pltpu.VMEM((7, n, 128), F32),
            dma, dma, dma((7,)), dma((7,)), dma((7,)), dma((7,)),
            dma((7,)), dma((7,)), dma((7,)), dma((7,)), dma, dma,
        ],
        compiler_params=params(2),
        name="reduce_all",
    )(w)


def body(
    homolog_embedding,
    pair_input_rows,
    incoming_slope,
    rescale_factor,
    probe_weights,
    lookup_weights,
    content_weights,
    sigmoid_weights,
    final_projection,
    pair_bias_matrix,
):
    highest = lax.Precision.HIGHEST
    rows, toks, width = homolog_embedding.shape
    wide = homolog_embedding.astype(F32)
    centered = wide - jnp.mean(wide, axis=-1, keepdims=True)
    inv = lax.rsqrt(jnp.mean(centered * centered, axis=-1, keepdims=True) + 1e-05)
    hat = centered * inv
    plain = (hat * rescale_factor).astype(BF16).reshape(-1, width)
    slope = incoming_slope.reshape(-1, width)

    def dot(a, b):
        return jnp.dot(a, b, preferred_element_type=F32)

    q = dot(plain, probe_weights).astype(BF16)
    k = dot(plain, lookup_weights).astype(BF16)
    v = dot(plain, content_weights).astype(BF16)
    gate = jax.nn.sigmoid(dot(plain, sigmoid_weights))
    grad_gated = dot(slope, final_projection.T)
    grad_att = (grad_gated * gate).astype(BF16)
    tokens = jnp.stack([a.reshape(-1, 8, 32) for a in (q, k, v, grad_att)], axis=2)
    tokens = jnp.transpose(tokens.reshape(-1, 8, 128), (1, 0, 2)).reshape(8, rows, toks, 128)
    bias = jnp.einsum(
        "ijc,ch->hij", pair_input_rows, pair_bias_matrix, preferred_element_type=F32
    ).astype(BF16)

    xt = jnp.transpose(scatter(tokens), (0, 2, 1))
    back, back_kv, db_own = main(xt, bias)

    def tokenwise(a):
        a = jnp.transpose(a.reshape(8, 2, toks, 2, 2, 32), (4, 1, 3, 2, 0, 5))
        return a.reshape(2, rows * toks, width)

    attended, dq = tokenwise(back)
    dq = dq.astype(BF16)
    dk, dv = tokenwise(back_kv)
    gated = (gate * attended).astype(BF16)
    grad_gate = (grad_gated * attended * gate * (1.0 - gate)).astype(BF16)

    plain_wide = plain.astype(F32)
    part_key = jnp.dot(plain_wide.T, dk, precision=highest)
    part_value = jnp.dot(plain_wide.T, dv, precision=highest)
    part_query = dot(plain.T, dq)
    part_gate = dot(plain.T, grad_gate)
    part_out = dot(gated.T, slope)
    grad_normed = (
        dot(dq, probe_weights.T)
        + dot(grad_gate, sigmoid_weights.T)
        + jnp.dot(dk, lookup_weights.astype(F32).T, precision=highest)
        + jnp.dot(dv, content_weights.astype(F32).T, precision=highest)
    ).reshape(rows, toks, width)
    part_gain = jnp.sum(grad_normed * hat, axis=(0, 1))
    scaled = grad_normed * rescale_factor
    alignment = (
        inv
        * (
            scaled
            - jnp.mean(scaled, axis=-1, keepdims=True)
            - hat * jnp.mean(scaled * hat, axis=-1, keepdims=True)
        )
    ).astype(BF16)
    pair_grad = jnp.einsum(
        "hij,ch->ijc", db_own, pair_bias_matrix, preferred_element_type=F32
    ).astype(BF16)
    part_bias = jnp.einsum("ijc,hij->ch", pair_input_rows, db_own, preferred_element_type=F32)

    packed = jnp.concatenate(
        [
            part_query,
            part_key,
            part_value,
            part_gate,
            part_out,
            part_gain.reshape(1, width),
            part_bias.reshape(4, width),
            jnp.zeros((251, width), F32),
        ],
        axis=0,
    )
    packed = jnp.stack([packed[:, :128], packed[:, 128:]]).reshape(2, 8, 8, 24, 128)
    total = reduce_all(packed).reshape(2, 1536, 128)
    total = jnp.concatenate([total[0], total[1]], axis=1)
    return (
        alignment,
        pair_grad,
        total[1280],
        total[0:256],
        total[256:512],
        total[512:768],
        total[768:1024],
        total[1024:1280],
        total[1281:1285].reshape(128, 8),
    )


def solution(mesh):
    in_specs = (
        P("seq", "res", None),
        P("res", "seq", None),
        P("seq", "res", None),
        P(),
        P(),
        P(),
        P(),
        P(),
        P(),
        P(),
    )
    out_specs = (P("seq", "res", None), P("res", "seq", None), P(), P(), P(), P(), P(), P(), P())
    return jax.shard_map(body, mesh=mesh, in_specs=in_specs, out_specs=out_specs, check_vma=False)
```

```python
import functools
import math

import jax
import jax.numpy as jnp
from jax import lax
from jax.experimental import pallas as pl
from jax.experimental.pallas import tpu as pltpu
from jax.sharding import PartitionSpec as P

MESH = pl.DeviceIdType.MESH
F32 = jnp.float32
BF16 = jnp.bfloat16
VM = pl.BlockSpec(memory_space=pltpu.VMEM)


class Place:
    def __init__(self):
        seq = lax.axis_index("seq")
        res = lax.axis_index("res")
        self.seq, self.res = seq, res
        self.z_lo, self.core = seq // 2, seq % 2
        self.g, self.z_hi = res // 4, res % 2
        self.x_hi = self.g % 2
        x_lo = (res // 2) % 2
        self.h = ((x_lo + self.x_hi) % 2) * 4 + self.z_hi * 2 + self.z_lo

    def spot(self, h):
        return h % 2, ((h // 4 + self.x_hi) % 2) * 2 + (h // 2) % 2

    def member(self, h):
        z_lo, r4 = self.spot(h)
        return (z_lo * 2 + self.core, self.g * 4 + r4)

    def block(self, g):
        return (self.seq, g * 4 + ((self.h // 4 + g % 2) % 2) * 2 + self.z_hi)

    def partner(self):
        return (self.z_lo * 2 + 1 - self.core, self.res)


def enter(devices):
    barrier = pltpu.get_barrier_semaphore()
    for device in devices:
        pl.semaphore_signal(barrier, inc=1, device_id=device, device_id_type=MESH)
    pl.semaphore_wait(barrier, len(devices))


def remote(src, dst, send, recv, device):
    return pltpu.make_async_remote_copy(
        src_ref=src, dst_ref=dst, send_sem=send, recv_sem=recv, device_id=device, device_id_type=MESH
    )


def params(collective_id):
    return pltpu.CompilerParams(
        collective_id=collective_id, has_side_effects=True, vmem_limit_bytes=48 * 1024 * 1024
    )


def aligned(x, n):
    return pl.multiple_of(x * n, n)


ORDER = (4, 3, 5, 2, 6, 1, 7)
CHUNKS = 4
QB = 128


ORDER = (4, 3, 5, 2, 6, 1, 7)
CHUNKS = 4
QB = 128


def row_backward(xt, kv, bias, db, dkv, row):
    scale = 1.0 / math.sqrt(32)
    kt = kv[row, 0:32, :]
    vt = kv[row, 32:64, :]
    tn = (((0,), (0,)), ((), ()))
    nt = (((1,), (1,)), ((), ()))
    dk = jnp.zeros((32, 2048), F32)
    dv = jnp.zeros((32, 2048), F32)
    outs = []
    for n in range(256 // QB):
        q = pl.ds(n * QB, QB)
        qt = xt[row, 0:32, q]
        dot = xt[row, 96:128, q]
        s = lax.dot_general(qt, kt, tn, preferred_element_type=F32) * scale
        s = s + bias[q, :].astype(F32)
        e = jnp.exp(s - jnp.max(s, axis=1, keepdims=True))
        soft = e * (1.0 / jnp.sum(e, axis=1, keepdims=True))
        half = soft.astype(BF16)
        gs = lax.dot_general(dot, vt, tn, preferred_element_type=F32)
        gs = soft * (gs - jnp.sum(soft * gs, axis=1, keepdims=True))
        gh = gs.astype(BF16)
        db[q, :] += gs
        att = lax.dot_general(vt, half, nt, preferred_element_type=F32)
        dq = lax.dot_general(kt, gh, nt, preferred_element_type=F32) * scale
        outs.append(jnp.concatenate([att, dq.astype(BF16).astype(F32)], axis=0))
        dk = dk + jnp.dot(qt, gh, preferred_element_type=F32)
        dv = dv + jnp.dot(dot, half, preferred_element_type=F32)
    dkv[row, 0:32, :] = (dk * scale).astype(dkv.dtype)
    dkv[row, 32:64, :] = dv.astype(dkv.dtype)
    return jnp.concatenate(outs, axis=1)


TN = (((0,), (0,)), ((), ()))
NT = (((1,), (1,)), ((), ()))


def mm(a, b, dims=(((1,), (0,)), ((), ()))):
    return lax.dot_general(a, b, dims, preferred_element_type=F32)


def halves(a):
    hi = a.astype(BF16)
    return hi, (a - hi.astype(F32)).astype(BF16)


class Fan:
    def __init__(self, p, send, recv):
        self.p, self.send, self.recv = p, send, recv

    def members(self, stage, src, dst):
        return self.all(stage, src, dst, self.p.h, self.p.member)

    def blocks(self, stage, src, dst):
        return self.all(stage, src, dst, self.p.g, self.p.block)

    def all(self, stage, src, dst, me, device):
        copies = []
        for k in ORDER:
            n = (me + k) % 8
            c = remote(src(n), dst(k), self.send.at[stage, k - 1], self.recv.at[stage, k - 1], device(n))
            c.start()
            copies.append(c)
        return copies

    def partner(self, stage, src, dst):
        c = remote(src, dst, self.send.at[stage, 0], self.recv.at[stage, 0], self.p.partner())
        c.start()
        return [c]


def finish(copies):
    for c in copies:
        c.wait()


class Reduce:
    def __init__(self, p, w, o, bufs, sems):
        self.p, self.w, self.o = p, w, o
        self.b0, self.a0, self.b1, self.a1, self.b2 = bufs
        self.fan = Fan(p, *sems)
        rows = w.shape[1]
        self.n1, self.n2 = rows // 8, rows // 64
        self.lanes = pl.ds(aligned(p.core, 128), 128)
        self.copies = []

    def pair(self):
        self.copies = self.fan.partner(0, self.w.at[1 - self.p.core], self.b0)

    def member(self):
        finish(self.copies)
        self.a0[...] = self.w[self.p.core] + self.b0[...]
        n = self.n1
        self.copies = self.fan.members(
            1, lambda h: self.a0.at[pl.ds(aligned(h, n), n)], lambda k: self.b1.at[k - 1]
        )

    def block(self):
        finish(self.copies)
        total = self.a0[pl.ds(aligned(self.p.h, self.n1), self.n1)]
        for k in range(7):
            total = total + self.b1[k]
        self.a1[...] = total
        n = self.n2
        self.copies = self.fan.blocks(
            2, lambda g: self.a1.at[pl.ds(aligned(g, n), n)], lambda k: self.b2.at[k - 1]
        )

    def back_block(self):
        finish(self.copies)
        n = self.n2
        total = self.a1[pl.ds(aligned(self.p.g, n), n)]
        for k in range(7):
            total = total + self.b2[k]
        rows = pl.ds(pl.multiple_of(self.p.h * self.n1 + self.p.g * n, n), n)
        self.o[rows, self.lanes] = total
        piece = self.o.at[rows, self.lanes]
        self.copies = self.fan.blocks(3, lambda g: piece, lambda k: piece)

    def back_member(self):
        finish(self.copies)
        piece = self.o.at[pl.ds(aligned(self.p.h, self.n1), self.n1), self.lanes]
        self.copies = self.fan.members(4, lambda h: piece, lambda k: piece)

    def back_pair(self):
        finish(self.copies)
        piece = self.o.at[:, self.lanes]
        self.copies = self.fan.partner(5, piece, piece)

    def done(self):
        finish(self.copies)
        self.copies = []


def main_kernel(
    hom, slope, gain, wq, wk, wv, wg, wo, pbt, pair_hbm,
    align, bo, oa, ob, ex_out,
    sc, sm,
):
    p = Place()
    z_lo, r4 = p.spot(p.h)
    toks = pl.ds(aligned(r4, 64), 64)
    here = pl.ds(aligned(p.g, 256), 256)
    cols = pl.ds(aligned(p.seq, 512), 512)
    per = 8 // CHUNKS
    xr, xt, kv, bias, db, dkv, parts = (sc[n] for n in ("xr", "xt", "kv", "bias", "db", "dkv", "parts"))
    rows_buf, local = sc["rows"], sm["local"]

    def stream(n):
        return pltpu.make_async_copy(pair_hbm.at[pl.ds(n * 16, 16)], rows_buf.at[n % 2], sm["hbm"].at[n % 2])

    stream(0).start()
    stream(1).start()

    x = jnp.transpose(hom[...].astype(F32))
    centered = x - jnp.mean(x, axis=0, keepdims=True)
    inv = lax.rsqrt(jnp.mean(centered * centered, axis=0, keepdims=True) + 1e-05)
    hat = centered * inv
    scale_t = jnp.transpose(jnp.broadcast_to(gain[...], (256, 256)))
    normed = (hat * scale_t).astype(BF16)
    sc["hat"][...] = hat
    sc["scale"][...] = scale_t
    sc["inv"][...] = jnp.broadcast_to(inv, (8, 256))
    sc["normed"][...] = normed
    t_ref = sc["t"]
    for n, w in enumerate((wq, wk, wv)):
        t_ref[:, n * 32 : n * 32 + 32, :] = mm(w[...], normed, TN).astype(BF16).reshape(8, 32, 256)
    gate = jax.nn.sigmoid(mm(wg[...], normed, TN))
    grad_gated = mm(wo[...], slope[...], NT)
    sc["gate"][...] = gate
    sc["gg"][...] = grad_gated
    t_ref[:, 96:128, :] = (grad_gated * gate).astype(BF16).reshape(8, 32, 256)

    enter(
        [p.member((p.h + k) % 8) for k in range(1, 8)]
        + [p.block((p.g + k) % 8) for k in range(1, 8)]
        + [p.partner()]
    )
    fan = Fan(p, sm["send"], sm["recv"])

    moved = fan.members(0, lambda h: t_ref.at[h], lambda k: xr.at[z_lo, r4])
    own_t = pltpu.make_async_copy(t_ref.at[p.h], xr.at[z_lo, r4], local.at[0])
    own_t.start()

    b_ref = sc["b"]
    for n in range(4):
        stream(n).wait()
        flat = rows_buf[n % 2].reshape(16 * 512, 128)
        out = mm(pbt[...], flat, NT)
        out = jnp.stack([out[:, i * 512 : (i + 1) * 512] for i in range(16)], axis=1)
        b_ref[:, n * 16 : (n + 1) * 16, :] = out.astype(BF16)
        if n + 2 < 4:
            stream(n + 2).start()
    biases = fan.members(1, lambda h: b_ref.at[h], lambda k: bias.at[toks, cols])
    own_b = pltpu.make_async_copy(b_ref.at[p.h], bias.at[toks, cols], local.at[1])
    own_b.start()

    own_t.wait()
    finish(moved)
    for z in range(2):
        for pp in range(2):
            for i in range(2):
                lane = pp * 128 + i * 64
                xt[z * 4 + pp * 2 + i] = jnp.concatenate(
                    [xr[z, r, :, lane : lane + 64] for r in range(4)], axis=1
                )

    def keys(c, k):
        rows = pl.ds(c * per, per)
        return remote(
            xt.at[rows, 32:96], kv.at[rows, :, here], sm["ks"].at[c, k - 1], sm["kr"].at[c, k - 1],
            p.block((p.g + k) % 8),
        )

    def partial(c, k):
        rows = pl.ds(c * per, per)
        g = (p.g + k) % 8
        return remote(
            dkv.at[rows, :, pl.ds(aligned(g, 256), 256)],
            parts.at[k - 1, rows],
            sm["es"].at[c, k - 1],
            sm["er"].at[c, k - 1],
            p.block(g),
        )

    for c in range(CHUNKS):
        for k in ORDER:
            keys(c, k).start()
    own_k = pltpu.make_async_copy(xt.at[:, 32:96], kv.at[:, :, here], local.at[2])
    own_k.start()
    db[...] = jnp.zeros_like(db)
    own_b.wait()
    own_k.wait()
    finish(biases)
    moved = []
    for b in range(2):
        part = bias.at[:, pl.ds(aligned(b * 2 + p.core, 512), 512)]
        moved += fan.partner(2 + b, part, part)
    finish(moved)

    ya, yd = sc["ya"], sc["yd"]

    def by_member(outs, dst, c):
        for r in range(4):
            lane = slice(r * 64, r * 64 + 64)
            dst[c, r] = jnp.concatenate([outs[0][:, lane], outs[1][:, lane]], axis=1)

    def step(c, carry):
        for k in ORDER:
            keys(c, k).wait_recv()
        outs = []
        for i in range(per):
            outs.append(row_backward(xt, kv, bias, db, dkv, c * per + i))
        for k in ORDER:
            partial(c, k).start()
        by_member(outs, ya, c)
        return carry

    lax.fori_loop(0, CHUNKS, step, 0)

    stream(0).start()
    stream(1).start()
    other, mine, ta, td = sc["other"], sc["mine"], sc["ta"], sc["td"]
    pair = []
    for b in range(2):
        pair += fan.partner(4 + b, db.at[:, pl.ds(aligned(b * 2 + 1 - p.core, 512), 512)], other.at[b])

    def give(stage, src, dst):
        def of(h):
            z, r = p.spot(h)
            return src.at[pl.ds(z * 2, 2), r]

        return fan.members(stage, of, lambda k: dst.at[p.h])

    back = give(6, ya, ta)
    own_a = pltpu.make_async_copy(ya.at[pl.ds(z_lo * 2, 2), r4], ta.at[p.h], local.at[0])
    own_a.start()
    for b in range(2):
        pair[b].wait()
        mine[b] = (db[:, pl.ds(aligned(b * 2 + p.core, 512), 512)] + other[b]).astype(BF16)

    def bias_of(h):
        z, r = p.spot(h)
        return mine.at[z, pl.ds(aligned(r, 64), 64)]

    bias_back = fan.members(7, bias_of, lambda k: bo.at[p.h])
    own_m = pltpu.make_async_copy(bias_of(p.h), bo.at[p.h], local.at[1])
    own_m.start()

    def assemble(src, part):
        rows = slice(part * 32, part * 32 + 32)
        return jnp.concatenate([src[:, pp, rows, :].reshape(256, 128) for pp in range(2)], axis=1)

    own_a.wait()
    finish(back)
    attended = assemble(ta, 0)
    dq = assemble(ta, 1).astype(BF16)
    gate = sc["gate"][...]
    gated = (gate * attended).astype(BF16)
    grad_gate = (sc["gg"][...] * attended * gate * (1.0 - gate)).astype(BF16)
    sc["dq"][...] = dq
    sc["dg"][...] = grad_gate
    normed = sc["normed"][...]
    wa, wb = sc["wa"], sc["wb"]

    def put(dst, n, value):
        for i in range(2):
            dst[i, n * 256 : n * 256 + 256, :] = value[:, i * 128 : i * 128 + 128]

    put(wa, 0, mm(normed, dq, NT))
    put(wa, 1, mm(normed, grad_gate, NT))
    put(wa, 2, mm(gated, slope[...]))
    wa[:, 768:1024, :] = jnp.zeros((2, 256, 128), F32)
    first = Reduce(p, wa, oa, [sc[n] for n in ("a_b0", "a_a0", "a_b1", "a_a1", "a_b2")], (sm["as"], sm["ar"]))
    last = Reduce(p, wb, ob, [sc[n] for n in ("b_b0", "b_a0", "b_b1", "b_a1", "b_b2")], (sm["bs"], sm["br"]))
    first.pair()

    own_m.wait()
    finish(bias_back)
    grad_bias = jnp.zeros((8, 128), F32)
    for n in range(4):
        stream(n).wait()
        part = bo[:, n * 16 : (n + 1) * 16, :].astype(F32)
        for i in range(16):
            grad_bias = grad_bias + mm(part[:, i, :].astype(BF16), rows_buf[n % 2, i])
        if n + 2 < 4:
            stream(n + 2).start()
        if n == 0:
            first.member()
    first.block()

    def total(c, carry):
        for k in ORDER:
            partial(c, k).wait_recv()
        outs = []
        for i in range(per):
            row = c * per + i
            t = dkv[row, :, here].astype(F32)
            for k in range(7):
                t = t + parts[k, row].astype(F32)
            outs.append(t)
        by_member(outs, yd, c)
        return carry

    lax.fori_loop(0, CHUNKS, total, 0)
    back = give(8, yd, td)
    own_d = pltpu.make_async_copy(yd.at[pl.ds(z_lo * 2, 2), r4], td.at[p.h], local.at[0])
    own_d.start()
    first.back_block()
    grad_normed = mm(wq[...], sc["dq"][...]) + mm(wg[...], sc["dg"][...])
    own_d.wait()
    finish(back)
    first.back_member()

    dk_hi, dk_lo = halves(assemble(td, 0))
    dv_hi, dv_lo = halves(assemble(td, 1))
    normed = sc["normed"][...]
    put(wb, 0, mm(normed, dk_hi, NT) + mm(normed, dk_lo, NT))
    put(wb, 1, mm(normed, dv_hi, NT) + mm(normed, dv_lo, NT))
    last.pair()
    grad_normed = grad_normed + mm(wk[...], dk_hi) + mm(wk[...], dk_lo) + mm(wv[...], dv_hi) + mm(wv[...], dv_lo)
    hat = sc["hat"][...]
    by_gain = jnp.sum(jnp.transpose(grad_normed * hat), axis=0, keepdims=True)
    ex, ex_own, exm, exb = sc["ex"], sc["ex_own"], sc["exm"], sc["exb"]
    ex[0:8, :] = grad_bias
    ex[8:16, :] = jnp.concatenate([by_gain[:, :128], by_gain[:, 128:], jnp.zeros((6, 128), F32)], axis=0)
    extra = fan.partner(9, ex, ex_own)
    last.member()
    finish(extra)
    exm[p.h] = ex[...] + ex_own[...]
    extra = fan.members(10, lambda h: exm.at[p.h], lambda k: exm.at[p.h])

    scaled = grad_normed * sc["scale"][...]
    m1 = jnp.mean(scaled, axis=0, keepdims=True)
    m2 = jnp.mean(scaled * hat, axis=0, keepdims=True)
    align[...] = jnp.transpose(sc["inv"][0:1, :] * (scaled - m1 - hat * m2)).astype(BF16)

    last.block()
    finish(extra)
    exb[p.g] = sum_of(exm)
    extra = fan.blocks(11, lambda g: exb.at[p.g], lambda k: exb.at[p.g])
    first.back_pair()
    last.back_block()
    finish(extra)
    ex_out[...] = sum_of(exb)
    last.back_member()
    last.back_pair()
    first.done()
    last.done()

    def drain(c, carry):
        for k in ORDER:
            keys(c, k).wait_send()
            partial(c, k).wait_send()
        return carry

    lax.fori_loop(0, CHUNKS, drain, 0)


def sum_of(ref):
    total = ref[0]
    for n in range(1, 8):
        total = total + ref[n]
    return total


def main(hom, slope, gain, wq, wk, wv, wg, wo, pbt, pair_rows):
    dma = pltpu.SemaphoreType.DMA
    vmem = pltpu.VMEM

    def reduce_bufs(name, rows):
        return {
            name + "_b0": vmem((rows, 128), F32),
            name + "_a0": vmem((rows, 128), F32),
            name + "_b1": vmem((7, rows // 8, 128), F32),
            name + "_a1": vmem((rows // 8, 128), F32),
            name + "_b2": vmem((7, rows // 64, 128), F32),
        }

    square = vmem((256, 256), F32)
    square_half = vmem((256, 256), BF16)
    scratch = {
        "rows": vmem((2, 16, 512, 128), BF16),
        "hat": square, "scale": square, "inv": vmem((8, 256), F32), "gate": square, "gg": square,
        "normed": square_half, "dq": square_half, "dg": square_half,
        "t": vmem((8, 128, 256), BF16),
        "b": vmem((8, 64, 512), BF16),
        "xr": vmem((2, 4, 128, 256), BF16),
        "xt": vmem((8, 128, 256), BF16),
        "kv": vmem((8, 64, 2048), BF16),
        "bias": vmem((256, 2048), BF16),
        "db": vmem((256, 2048), F32),
        "dkv": vmem((8, 64, 2048), BF16),
        "parts": vmem((7, 8, 64, 256), BF16),
        "ya": vmem((4, 4, 64, 128), F32),
        "yd": vmem((4, 4, 64, 128), F32),
        "ta": vmem((8, 2, 64, 128), F32),
        "td": vmem((8, 2, 64, 128), F32),
        "mine": vmem((2, 256, 512), BF16),
        "other": vmem((2, 256, 512), F32),
        "wa": vmem((2, 1024, 128), F32),
        "wb": vmem((2, 512, 128), F32),
        "ex": vmem((16, 128), F32), "ex_own": vmem((16, 128), F32),
        "exm": vmem((8, 16, 128), F32), "exb": vmem((8, 16, 128), F32),
        **reduce_bufs("a", 1024),
        **reduce_bufs("b", 512),
    }
    sems = {
        "hbm": dma((2,)), "local": dma((3,)),
        "send": dma((12, 7)), "recv": dma((12, 7)),
        "ks": dma((CHUNKS, 7)), "kr": dma((CHUNKS, 7)),
        "es": dma((CHUNKS, 7)), "er": dma((CHUNKS, 7)),
        "as": dma((6, 7)), "ar": dma((6, 7)),
        "bs": dma((6, 7)), "br": dma((6, 7)),
    }
    return pl.pallas_call(
        main_kernel,
        out_shape=(
            jax.ShapeDtypeStruct((256, 256), BF16),
            jax.ShapeDtypeStruct((8, 64, 512), BF16),
            jax.ShapeDtypeStruct((1024, 256), F32),
            jax.ShapeDtypeStruct((512, 256), F32),
            jax.ShapeDtypeStruct((16, 128), F32),
        ),
        in_specs=[VM] * 9 + [pl.BlockSpec(memory_space=pl.ANY)],
        out_specs=(VM,) * 5,
        scratch_shapes=[scratch, sems],
        compiler_params=params(0),
        name="main",
    )(hom, slope, gain, wq, wk, wv, wg, wo, pbt, pair_rows)


def body(
    homolog_embedding,
    pair_input_rows,
    incoming_slope,
    rescale_factor,
    probe_weights,
    lookup_weights,
    content_weights,
    sigmoid_weights,
    final_projection,
    pair_bias_matrix,
):
    rows, toks, width = homolog_embedding.shape
    align, db_own, oa, ob, extra = main(
        homolog_embedding.reshape(-1, width),
        incoming_slope.reshape(-1, width),
        rescale_factor.reshape(1, width),
        probe_weights,
        lookup_weights,
        content_weights,
        sigmoid_weights,
        final_projection,
        pair_bias_matrix.T,
        pair_input_rows,
    )
    pair_grad = jnp.einsum(
        "hij,ch->ijc", db_own, pair_bias_matrix, preferred_element_type=F32
    ).astype(BF16)
    return (
        align.reshape(rows, toks, width),
        pair_grad,
        extra[8:10].reshape(width),
        oa[0:256],
        ob[0:256],
        ob[256:512],
        oa[256:512],
        oa[512:768],
        extra[0:8].T,
    )


def solution(mesh):
    in_specs = (
        P("seq", "res", None),
        P("res", "seq", None),
        P("seq", "res", None),
        P(),
        P(),
        P(),
        P(),
        P(),
        P(),
        P(),
    )
    out_specs = (P("seq", "res", None), P("res", "seq", None), P(), P(), P(), P(), P(), P(), P())
    return jax.shard_map(body, mesh=mesh, in_specs=in_specs, out_specs=out_specs, check_vma=False)
```

```python
import functools
import math

import jax
import jax.numpy as jnp
from jax import lax
from jax.experimental import pallas as pl
from jax.experimental.pallas import tpu as pltpu
from jax.sharding import PartitionSpec as P

MESH = pl.DeviceIdType.MESH
F32 = jnp.float32
BF16 = jnp.bfloat16
VM = pl.BlockSpec(memory_space=pltpu.VMEM)
HB = pl.BlockSpec(memory_space=pltpu.HBM)


class Place:
    def __init__(self):
        seq = lax.axis_index("seq")
        res = lax.axis_index("res")
        self.seq, self.res = seq, res
        self.z_lo, self.core = seq // 2, seq % 2
        self.g, self.z_hi = res // 4, res % 2
        self.x_hi = self.g % 2
        x_lo = (res // 2) % 2
        self.h = ((x_lo + self.x_hi) % 2) * 4 + self.z_hi * 2 + self.z_lo

    def spot(self, h):
        return h % 2, ((h // 4 + self.x_hi) % 2) * 2 + (h // 2) % 2

    def member(self, h):
        z_lo, r4 = self.spot(h)
        return (z_lo * 2 + self.core, self.g * 4 + r4)

    def block(self, g):
        return (self.seq, g * 4 + ((self.h // 4 + g % 2) % 2) * 2 + self.z_hi)

    def partner(self):
        return (self.z_lo * 2 + 1 - self.core, self.res)


def greet(devices):
    barrier = pltpu.get_barrier_semaphore()
    for device in devices:
        pl.semaphore_signal(barrier, inc=1, device_id=device, device_id_type=MESH)


def remote(src, dst, send, recv, device):
    return pltpu.make_async_remote_copy(
        src_ref=src, dst_ref=dst, send_sem=send, recv_sem=recv, device_id=device, device_id_type=MESH
    )


def params(collective_id):
    return pltpu.CompilerParams(
        collective_id=collective_id, has_side_effects=True, vmem_limit_bytes=48 * 1024 * 1024
    )


def aligned(x, n):
    return pl.multiple_of(x * n, n)


ORDER = (4, 3, 5, 2, 6, 1, 7)
CHUNKS = 4
QB = 128


ORDER = (4, 3, 5, 2, 6, 1, 7)
CHUNKS = 4
QB = 128


def row_backward(xt, kv, bias, db, dkv, row):
    scale = 1.0 / math.sqrt(32)
    kt = kv[row, 0:32, :]
    vt = kv[row, 32:64, :]
    dk = jnp.zeros((32, 2048), F32)
    dv = jnp.zeros((32, 2048), F32)
    outs = []
    for n in range(256 // QB):
        q = pl.ds(n * QB, QB)
        qt = xt[row, 64:96, q]
        dot = xt[row, 96:128, q]
        s = mm(qt, kt, TN) * scale
        s = s + bias[q, :].astype(F32)
        e = jnp.exp(s - jnp.max(s, axis=1, keepdims=True))
        soft = e * (1.0 / jnp.sum(e, axis=1, keepdims=True))
        half = soft.astype(BF16)
        gs = mm(dot, vt, TN)
        gs = soft * (gs - jnp.sum(soft * gs, axis=1, keepdims=True))
        gh = gs.astype(BF16)
        db[q, :] += gs
        att = mm(vt, half, NT)
        dq = mm(kt, gh, NT) * scale
        outs.append(jnp.concatenate([att, dq.astype(BF16).astype(F32)], axis=0))
        dk = dk + mm(qt, gh)
        dv = dv + mm(dot, half)
    dkv[row, 0:32, :] = (dk * scale).astype(dkv.dtype)
    dkv[row, 32:64, :] = dv.astype(dkv.dtype)
    return jnp.concatenate(outs, axis=1)


TN = (((0,), (0,)), ((), ()))
NT = (((1,), (1,)), ((), ()))


def mm(a, b, dims=(((1,), (0,)), ((), ()))):
    return lax.dot_general(a, b, dims, preferred_element_type=F32)


def halves(a):
    hi = a.astype(BF16)
    return hi, (a - hi.astype(F32)).astype(BF16)


class Fan:
    def __init__(self, p, send, recv):
        self.p, self.send, self.recv = p, send, recv

    def members(self, stage, src, dst):
        return self.all(stage, src, dst, self.p.h, self.p.member)

    def blocks(self, stage, src, dst):
        return self.all(stage, src, dst, self.p.g, self.p.block)

    def all(self, stage, src, dst, me, device):
        copies = []
        for k in ORDER:
            n = (me + k) % 8
            c = remote(src(n), dst(k), self.send.at[stage, k - 1], self.recv.at[stage, k - 1], device(n))
            c.start()
            copies.append(c)
        return copies

    def partner(self, stage, src, dst):
        c = remote(src, dst, self.send.at[stage, 0], self.recv.at[stage, 0], self.p.partner())
        c.start()
        return [c]


def finish(copies):
    for c in copies:
        c.wait()


class Reduce:
    def __init__(self, p, w, o, bufs, sems):
        self.p, self.w, self.o = p, w, o
        self.b0, self.a0, self.b1, self.a1 = bufs
        self.fan = Fan(p, *sems)
        self.n = w.shape[1] // 8
        self.lanes = pl.ds(aligned(p.core, 128), 128)
        self.copies = []

    def rows(self, g):
        return pl.ds(aligned(g, self.n), self.n)

    def pair(self):
        self.copies = self.fan.partner(0, self.w.at[1 - self.p.core], self.b0)

    def block(self):
        finish(self.copies)
        self.a0[...] = self.w[self.p.core] + self.b0[...]
        self.copies = self.fan.blocks(1, lambda g: self.a0.at[self.rows(g)], lambda k: self.b1.at[k - 1])

    def member(self):
        finish(self.copies)
        total = self.a0[self.rows(self.p.g)]
        for k in range(7):
            total = total + self.b1[k]
        self.a1[self.p.h] = total
        piece = self.a1.at[self.p.h]
        self.copies = self.fan.members(2, lambda h: piece, lambda k: piece)

    def back_block(self):
        finish(self.copies)
        self.o[self.rows(self.p.g), self.lanes] = sum_of(self.a1)
        piece = self.o.at[self.rows(self.p.g), self.lanes]
        self.copies = self.fan.blocks(3, lambda g: piece, lambda k: piece)

    def back_pair(self):
        finish(self.copies)
        piece = self.o.at[:, self.lanes]
        self.copies = self.fan.partner(4, piece, piece)

    def done(self):
        finish(self.copies)
        self.copies = []


def only(value, n, i):
    row = lax.broadcasted_iota(jnp.int32, value.shape, 0) % n
    return jnp.where(row == i, value, jnp.zeros_like(value))


def spread(pbt):
    return jnp.broadcast_to(pbt.astype(F32)[:, None, :], (8, 16, 128)).reshape(128, 128)


def main_kernel(
    hom_in, slope_in, gain_in, wq_in, wk_in, wv_in, wg_in, wo_in, pbt_in, pair_hbm,
    align, bo, oa, ob, ex_out,
    sc, sm,
):
    p = Place()
    z_lo, r4 = p.spot(p.h)
    toks = pl.ds(aligned(r4, 64), 64)
    here = pl.ds(aligned(p.g, 256), 256)
    cols = pl.ds(aligned(p.seq, 512), 512)
    per = 8 // CHUNKS
    xr, xt, kv, bias, db, dkv, parts = (sc[n] for n in ("xr", "xt", "kv", "bias", "db", "dkv", "parts"))
    rows_buf, local = sc["rows"], sm["local"]

    greet(
        [p.member((p.h + k) % 8) for k in range(1, 8)]
        + [p.block((p.g + k) % 8) for k in range(1, 8)]
        + [p.partner()]
    )
    loads = {}
    names = ("hom", "gain", "wk", "wv", "slope", "wo", "wg", "wq", "pbt")
    for n, (name, src) in enumerate(
        zip(names, (hom_in, gain_in, wk_in, wv_in, slope_in, wo_in, wg_in, wq_in, pbt_in))
    ):
        loads[name] = pltpu.make_async_copy(src, sc[name], sm["in"].at[n])
        loads[name].start()

    def stream(n):
        return pltpu.make_async_copy(pair_hbm.at[pl.ds(n * 16, 16)], rows_buf.at[n % 2], sm["hbm"].at[n % 2])

    stream(0).start()
    stream(1).start()
    hom, gain, wk, wv, slope, wo, wg, wq, pbt = (sc[n] for n in names)

    loads["hom"].wait()
    loads["gain"].wait()
    x = jnp.transpose(hom[...].astype(F32))
    centered = x - jnp.mean(x, axis=0, keepdims=True)
    inv = lax.rsqrt(jnp.mean(centered * centered, axis=0, keepdims=True) + 1e-05)
    hat = centered * inv
    scale_t = jnp.transpose(jnp.broadcast_to(gain[...], (256, 256)))
    normed = (hat * scale_t).astype(BF16)
    t_ref = sc["t"]
    loads["wk"].wait()
    loads["wv"].wait()
    for n, w in enumerate((wk, wv)):
        t_ref[:, n * 32 : n * 32 + 32, :] = mm(w[...], normed, TN).astype(BF16).reshape(8, 32, 256)
    pl.semaphore_wait(pltpu.get_barrier_semaphore(), 15)
    fan = Fan(p, sm["send"], sm["recv"])

    moved = fan.members(0, lambda h: t_ref.at[h, 0:64], lambda k: xr.at[z_lo, r4, 0:64])
    own_t = pltpu.make_async_copy(t_ref.at[p.h, 0:64], xr.at[z_lo, r4, 0:64], local.at[0])
    own_t.start()
    sc["hat"][...] = hat
    sc["scale"][...] = scale_t
    sc["inv"][...] = jnp.broadcast_to(inv, (8, 256))
    sc["normed"][...] = normed
    for name in ("slope", "wo", "wg", "wq", "pbt"):
        loads[name].wait()
    t_ref[:, 64:96, :] = mm(wq[...], normed, TN).astype(BF16).reshape(8, 32, 256)
    gate = jax.nn.sigmoid(mm(wg[...], normed, TN))
    grad_gated = mm(wo[...], slope[...], NT)
    sc["gate"][...] = gate
    sc["gg"][...] = grad_gated
    t_ref[:, 96:128, :] = (grad_gated * gate).astype(BF16).reshape(8, 32, 256)
    moved_q = fan.members(12, lambda h: t_ref.at[h, 64:128], lambda k: xr.at[z_lo, r4, 64:128])
    own_q = pltpu.make_async_copy(t_ref.at[p.h, 64:128], xr.at[z_lo, r4, 64:128], local.at[3])
    own_q.start()

    b_ref, mask = sc["b"], sc["mask"]
    base = spread(pbt[...])
    for i in range(16):
        mask[i] = only(base, 16, i).astype(BF16)
    for n in range(4):
        stream(n).wait()
        out = mm(mask[0], rows_buf[n % 2, 0], NT)
        for i in range(1, 16):
            out = out + mm(mask[i], rows_buf[n % 2, i], NT)
        b_ref[:, n * 16 : (n + 1) * 16, :] = out.astype(BF16).reshape(8, 16, 512)
        if n + 2 < 4:
            stream(n + 2).start()
    biases = fan.members(1, lambda h: b_ref.at[h], lambda k: bias.at[toks, cols])
    own_b = pltpu.make_async_copy(b_ref.at[p.h], bias.at[toks, cols], local.at[1])
    own_b.start()

    def by_row(lo):
        for z in range(2):
            for pp in range(2):
                for i in range(2):
                    lane = pp * 128 + i * 64
                    xt[z * 4 + pp * 2 + i, lo : lo + 64] = jnp.concatenate(
                        [xr[z, r, lo : lo + 64, lane : lane + 64] for r in range(4)], axis=1
                    )

    own_t.wait()
    finish(moved)
    by_row(0)

    def keys(c, k):
        rows = pl.ds(c * per, per)
        return remote(
            xt.at[rows, 0:64], kv.at[rows, :, here], sm["ks"].at[c, k - 1], sm["kr"].at[c, k - 1],
            p.block((p.g + k) % 8),
        )

    def partial(c, k):
        rows = pl.ds(c * per, per)
        g = (p.g + k) % 8
        return remote(
            dkv.at[rows, :, pl.ds(aligned(g, 256), 256)],
            parts.at[k - 1, rows],
            sm["es"].at[c, k - 1],
            sm["er"].at[c, k - 1],
            p.block(g),
        )

    for c in range(CHUNKS):
        for k in ORDER:
            keys(c, k).start()
    own_k = pltpu.make_async_copy(xt.at[:, 0:64], kv.at[:, :, here], local.at[2])
    own_k.start()
    db[...] = jnp.zeros_like(db)
    own_q.wait()
    finish(moved_q)
    by_row(64)
    own_k.wait()
    own_b.wait()
    finish(biases)
    moved = []
    for b in range(2):
        part = bias.at[:, pl.ds(aligned(b * 2 + p.core, 512), 512)]
        moved += fan.partner(2 + b, part, part)
    finish(moved)

    ya, yd = sc["ya"], sc["yd"]

    def by_member(outs, dst, c):
        for r in range(4):
            lane = slice(r * 64, r * 64 + 64)
            dst[c, r] = jnp.concatenate([outs[0][:, lane], outs[1][:, lane]], axis=1)

    ta, td, other, mine = sc["ta"], sc["td"], sc["other"], sc["mine"]

    def give(stage, src, dst, k, z):
        h = (p.h + k) % 8
        return remote(
            src.at[pl.ds(z * 2, 2), p.spot(h)[1]], dst.at[p.h],
            sm["send"].at[stage, k - 1], sm["recv"].at[stage, k - 1], p.member(h),
        )

    def keep(n, src, dst):
        return pltpu.make_async_copy(src.at[pl.ds(z_lo * 2, 2), r4], dst.at[p.h], local.at[n])

    def give_half(stage, n, src, dst, z):
        @pl.when(z_lo == z)
        def _():
            for k in (4, 2, 6):
                give(stage, src, dst, k, z).start()
            keep(n, src, dst).start()

        @pl.when(z_lo != z)
        def _():
            for k in (3, 5, 1, 7):
                give(stage, src, dst, k, z).start()

    def taken(stage, n, src, dst):
        keep(n, src, dst).wait()
        for k in ORDER:
            give(stage, src, dst, k, 0).wait()

    def step(c, carry):
        for k in ORDER:
            keys(c, k).wait_recv()
        outs = []
        for i in range(per):
            outs.append(row_backward(xt, kv, bias, db, dkv, c * per + i))
        for k in ORDER:
            partial(c, k).start()
        by_member(outs, ya, c)
        for z in range(2):

            @pl.when(c == 2 * z + 1)
            def _():
                give_half(6, 0, ya, ta, z)

        return carry

    lax.fori_loop(0, CHUNKS, step, 0)

    stream(0).start()
    stream(1).start()
    pair = []
    for b in range(2):
        pair += fan.partner(4 + b, db.at[:, pl.ds(aligned(b * 2 + 1 - p.core, 512), 512)], other.at[b])

    def total(c, carry):
        for k in ORDER:
            partial(c, k).wait_recv()
        outs = []
        for i in range(per):
            row = c * per + i
            t = dkv[row, :, here].astype(F32)
            for k in range(7):
                t = t + parts[k, row].astype(F32)
            outs.append(t)
        by_member(outs, yd, c)
        return carry

    lax.fori_loop(0, 2, total, 0)
    give_half(8, 2, yd, td, 0)
    for b in range(2):
        pair[b].wait()
        mine[b] = (db[:, pl.ds(aligned(b * 2 + p.core, 512), 512)] + other[b]).astype(BF16)

    def assemble(src, part):
        rows = slice(part * 32, part * 32 + 32)
        return jnp.concatenate([src[:, pp, rows, :].reshape(256, 128) for pp in range(2)], axis=1)

    taken(6, 0, ya, ta)
    attended = assemble(ta, 0)
    dq = assemble(ta, 1).astype(BF16)
    gate = sc["gate"][...]
    gated = (gate * attended).astype(BF16)
    grad_gate = (sc["gg"][...] * attended * gate * (1.0 - gate)).astype(BF16)
    sc["dq"][...] = dq
    sc["dg"][...] = grad_gate
    normed = sc["normed"][...]
    wa, wb = sc["wa"], sc["wb"]

    def put(dst, n, value):
        for i in range(2):
            dst[i, n * 256 : n * 256 + 256, :] = value[:, i * 128 : i * 128 + 128]

    put(wa, 0, mm(normed, dq, NT))
    put(wa, 1, mm(normed, grad_gate, NT))
    put(wa, 2, mm(gated, slope[...]))
    first = Reduce(p, wa, oa, [sc[n] for n in ("a_b0", "a_a0", "a_b1", "a_a1")], (sm["as"], sm["ar"]))
    last = Reduce(p, wb, ob, [sc[n] for n in ("b_b0", "b_a0", "b_b1", "b_a1")], (sm["bs"], sm["br"]))
    first.pair()
    lax.fori_loop(2, 4, total, 0)
    give_half(8, 2, yd, td, 1)

    def bias_of(h):
        z, r = p.spot(h)
        return mine.at[z, pl.ds(aligned(r, 64), 64)]

    bias_back = fan.members(7, bias_of, lambda k: bo.at[p.h])
    own_m = pltpu.make_async_copy(bias_of(p.h), bo.at[p.h], local.at[1])
    own_m.start()
    first.block()
    grad_normed = mm(wq[...], sc["dq"][...]) + mm(wg[...], sc["dg"][...])
    first.member()

    taken(8, 2, yd, td)
    dk_hi, dk_lo = halves(assemble(td, 0))
    dv_hi, dv_lo = halves(assemble(td, 1))
    normed = sc["normed"][...]
    put(wb, 0, mm(normed, dk_hi, NT) + mm(normed, dk_lo, NT))
    put(wb, 1, mm(normed, dv_hi, NT) + mm(normed, dv_lo, NT))
    last.pair()
    grad_normed = grad_normed + mm(wk[...], dk_hi) + mm(wk[...], dk_lo) + mm(wv[...], dv_hi) + mm(wv[...], dv_lo)
    hat = sc["hat"][...]
    by_gain = jnp.sum(jnp.transpose(grad_normed * hat), axis=0, keepdims=True)
    last.block()

    own_m.wait()
    finish(bias_back)
    grad_bias = jnp.zeros((128, 128), F32)
    for n in range(4):
        stream(n).wait()
        part = bo[:, n * 16 : (n + 1) * 16, :].reshape(128, 512)
        for i in range(16):
            grad_bias = grad_bias + mm(only(part, 16, i), rows_buf[n % 2, i])
        if n + 2 < 4:
            stream(n + 2).start()
    ex, ex_own, exm, exb = sc["ex"], sc["ex_own"], sc["exm"], sc["exb"]
    ex[0:8, :] = jnp.sum(grad_bias.reshape(8, 16, 128), axis=1)
    ex[8:16, :] = jnp.concatenate([by_gain[:, :128], by_gain[:, 128:], jnp.zeros((6, 128), F32)], axis=0)
    extra = fan.partner(9, ex, ex_own)
    last.member()
    first.back_block()
    finish(extra)
    exm[p.h] = ex[...] + ex_own[...]
    extra = fan.members(10, lambda h: exm.at[p.h], lambda k: exm.at[p.h])

    scaled = grad_normed * sc["scale"][...]
    m1 = jnp.mean(scaled, axis=0, keepdims=True)
    m2 = jnp.mean(scaled * hat, axis=0, keepdims=True)
    align[...] = jnp.transpose(sc["inv"][0:1, :] * (scaled - m1 - hat * m2)).astype(BF16)

    last.back_block()
    finish(extra)
    exb[p.g] = sum_of(exm)
    extra = fan.blocks(11, lambda g: exb.at[p.g], lambda k: exb.at[p.g])
    first.back_pair()
    last.back_pair()
    finish(extra)
    ex_out[...] = sum_of(exb)
    first.done()
    last.done()

    def drain(c, carry):
        for k in ORDER:
            keys(c, k).wait_send()
            partial(c, k).wait_send()
        return carry

    lax.fori_loop(0, CHUNKS, drain, 0)


def sum_of(ref):
    total = ref[0]
    for n in range(1, 8):
        total = total + ref[n]
    return total


def main(hom, slope, gain, wq, wk, wv, wg, wo, pbt, pair_rows):
    dma = pltpu.SemaphoreType.DMA
    vmem = pltpu.VMEM

    def reduce_bufs(name, rows):
        return {
            name + "_b0": vmem((rows, 128), F32),
            name + "_a0": vmem((rows, 128), F32),
            name + "_b1": vmem((7, rows // 8, 128), F32),
            name + "_a1": vmem((8, rows // 8, 128), F32),
        }

    square = vmem((256, 256), F32)
    square_half = vmem((256, 256), BF16)
    scratch = {
        "rows": vmem((2, 16, 512, 128), BF16),
        "mask": vmem((16, 128, 128), BF16),
        "hom": square_half, "slope": square_half, "gain": vmem((1, 256), F32), "pbt": vmem((8, 128), BF16),
        "wq": square_half, "wk": square_half, "wv": square_half, "wg": square_half, "wo": square_half,
        "hat": square, "scale": square, "inv": vmem((8, 256), F32), "gate": square, "gg": square,
        "normed": square_half, "dq": square_half, "dg": square_half,
        "t": vmem((8, 128, 256), BF16),
        "b": vmem((8, 64, 512), BF16),
        "xr": vmem((2, 4, 128, 256), BF16),
        "xt": vmem((8, 128, 256), BF16),
        "kv": vmem((8, 64, 2048), BF16),
        "bias": vmem((256, 2048), BF16),
        "db": vmem((256, 2048), F32),
        "dkv": vmem((8, 64, 2048), BF16),
        "parts": vmem((7, 8, 64, 256), BF16),
        "ya": vmem((4, 4, 64, 128), F32),
        "yd": vmem((4, 4, 64, 128), F32),
        "ta": vmem((8, 2, 64, 128), F32),
        "td": vmem((8, 2, 64, 128), F32),
        "mine": vmem((2, 256, 512), BF16),
        "other": vmem((2, 256, 512), F32),
        "wa": vmem((2, 768, 128), F32),
        "wb": vmem((2, 512, 128), F32),
        "ex": vmem((16, 128), F32), "ex_own": vmem((16, 128), F32),
        "exm": vmem((8, 16, 128), F32), "exb": vmem((8, 16, 128), F32),
        **reduce_bufs("a", 768),
        **reduce_bufs("b", 512),
    }
    sems = {
        "hbm": dma((2,)), "local": dma((4,)), "in": dma((9,)),
        "send": dma((13, 7)), "recv": dma((13, 7)),
        "ks": dma((CHUNKS, 7)), "kr": dma((CHUNKS, 7)),
        "es": dma((CHUNKS, 7)), "er": dma((CHUNKS, 7)),
        "as": dma((5, 7)), "ar": dma((5, 7)),
        "bs": dma((5, 7)), "br": dma((5, 7)),
    }
    return pl.pallas_call(
        main_kernel,
        out_shape=(
            jax.ShapeDtypeStruct((256, 256), BF16),
            jax.ShapeDtypeStruct((8, 64, 512), BF16),
            jax.ShapeDtypeStruct((768, 256), F32),
            jax.ShapeDtypeStruct((512, 256), F32),
            jax.ShapeDtypeStruct((16, 128), F32),
        ),
        in_specs=[HB] * 10,
        out_specs=(VM,) * 5,
        scratch_shapes=[scratch, sems],
        compiler_params=params(0),
        name="main",
    )(hom, slope, gain, wq, wk, wv, wg, wo, pbt, pair_rows)


def tail_kernel(bo, pbt, align, oa, ob, ex, pair, align_out, q, k, v, g, o, gain, bias, base, sem):
    n = pl.program_id(0)
    moves = [(align, align_out), (ex.at[8:10], gain), (ex.at[0:8], bias)]
    moves += [(oa.at[0:256], q), (oa.at[256:512], g), (oa.at[512:768], o), (ob.at[0:256], k), (ob.at[256:512], v)]
    copies = [pltpu.make_async_copy(a, b, sem.at[i]) for i, (a, b) in enumerate(moves)]

    @pl.when(n == 0)
    def _():
        for c in copies:
            c.start()
        spreaded = spread(pbt[...])
        for i in range(16):
            base[:, i * 128 : i * 128 + 128] = only(spreaded, 16, i).astype(BF16)

    part = jnp.transpose(bo[:, pl.ds(pl.multiple_of(n * 16, 16), 16), :].reshape(128, 512))
    for i in range(8):
        out = mm(part, base[:, i * 256 : i * 256 + 256]).astype(BF16)
        pair[2 * i] = out[:, :128]
        pair[2 * i + 1] = out[:, 128:]

    @pl.when(n == 3)
    def _():
        for c in copies:
            c.wait()


def tail(bo, pbt, align, oa, ob, ex):
    square = jax.ShapeDtypeStruct((256, 256), F32)
    return pl.pallas_call(
        tail_kernel,
        grid=(4,),
        out_shape=(
            jax.ShapeDtypeStruct((64, 512, 128), BF16),
            jax.ShapeDtypeStruct((256, 256), BF16),
            square, square, square, square, square,
            jax.ShapeDtypeStruct((2, 128), F32),
            jax.ShapeDtypeStruct((8, 128), F32),
        ),
        in_specs=[VM] * 6,
        out_specs=(pl.BlockSpec((16, 512, 128), lambda n: (n, 0, 0)),) + (HB,) * 8,
        scratch_shapes=[pltpu.VMEM((128, 2048), BF16), pltpu.SemaphoreType.DMA((8,))],
        compiler_params=pltpu.CompilerParams(vmem_limit_bytes=32 * 1024 * 1024),
        name="tail",
    )(bo, pbt, align, oa, ob, ex)


def body(
    homolog_embedding,
    pair_input_rows,
    incoming_slope,
    rescale_factor,
    probe_weights,
    lookup_weights,
    content_weights,
    sigmoid_weights,
    final_projection,
    pair_bias_matrix,
):
    rows, toks, width = homolog_embedding.shape
    align, db_own, oa, ob, extra = main(
        homolog_embedding.reshape(-1, width),
        incoming_slope.reshape(-1, width),
        rescale_factor.reshape(1, width),
        probe_weights,
        lookup_weights,
        content_weights,
        sigmoid_weights,
        final_projection,
        pair_bias_matrix.T,
        pair_input_rows,
    )
    pair_grad, align, grad_q, grad_k, grad_v, grad_g, grad_o, gain, bias = tail(
        db_own, pair_bias_matrix.T, align, oa, ob, extra
    )
    return (
        align.reshape(rows, toks, width),
        pair_grad,
        gain.reshape(width),
        grad_q,
        grad_k,
        grad_v,
        grad_g,
        grad_o,
        bias.T,
    )


def solution(mesh):
    in_specs = (
        P("seq", "res", None),
        P("res", "seq", None),
        P("seq", "res", None),
        P(),
        P(),
        P(),
        P(),
        P(),
        P(),
        P(),
    )
    out_specs = (P("seq", "res", None), P("res", "seq", None), P(), P(), P(), P(), P(), P(), P())
    return jax.shard_map(body, mesh=mesh, in_specs=in_specs, out_specs=out_specs, check_vma=False)
```

```python
import functools
import math

import jax
import jax.numpy as jnp
from jax import lax
from jax.experimental import pallas as pl
from jax.experimental.pallas import tpu as pltpu
from jax.sharding import PartitionSpec as P

MESH = pl.DeviceIdType.MESH
F32 = jnp.float32
BF16 = jnp.bfloat16
VM = pl.BlockSpec(memory_space=pltpu.VMEM)
HB = pl.BlockSpec(memory_space=pltpu.HBM)


class Place:
    def __init__(self):
        seq = lax.axis_index("seq")
        res = lax.axis_index("res")
        self.seq, self.res = seq, res
        self.z_lo, self.core = seq // 2, seq % 2
        self.g, self.z_hi = res // 4, res % 2
        self.x_hi = self.g % 2
        x_lo = (res // 2) % 2
        self.h = ((x_lo + self.x_hi) % 2) * 4 + self.z_hi * 2 + self.z_lo

    def spot(self, h):
        return h % 2, ((h // 4 + self.x_hi) % 2) * 2 + (h // 2) % 2

    def member(self, h):
        z_lo, r4 = self.spot(h)
        return (z_lo * 2 + self.core, self.g * 4 + r4)

    def block(self, g):
        return (self.seq, g * 4 + ((self.h // 4 + g % 2) % 2) * 2 + self.z_hi)

    def partner(self):
        return (self.z_lo * 2 + 1 - self.core, self.res)


def greet(devices):
    barrier = pltpu.get_barrier_semaphore()
    for device in devices:
        pl.semaphore_signal(barrier, inc=1, device_id=device, device_id_type=MESH)


def remote(src, dst, send, recv, device):
    return pltpu.make_async_remote_copy(
        src_ref=src, dst_ref=dst, send_sem=send, recv_sem=recv, device_id=device, device_id_type=MESH
    )


def params(collective_id):
    return pltpu.CompilerParams(
        collective_id=collective_id, has_side_effects=True, vmem_limit_bytes=48 * 1024 * 1024
    )


def aligned(x, n):
    return pl.multiple_of(x * n, n)


ORDER = (4, 3, 5, 2, 6, 1, 7)
CHUNKS = 4
QB = 128


ORDER = (4, 3, 5, 2, 6, 1, 7)
CHUNKS = 4
QB = 128


def row_backward(xt, kv, bias, db, dkv, row):
    scale = 1.0 / math.sqrt(32)
    kt = kv[row, 0:32, :]
    vt = kv[row, 32:64, :]
    dk = jnp.zeros((32, 2048), F32)
    dv = jnp.zeros((32, 2048), F32)
    outs = []
    for n in range(256 // QB):
        q = pl.ds(n * QB, QB)
        qt = xt[row, 64:96, q]
        dot = xt[row, 96:128, q]
        s = mm(qt, kt, TN) * scale
        s = s + bias[q, :].astype(F32)
        e = jnp.exp(s - jnp.max(s, axis=1, keepdims=True))
        soft = e * (1.0 / jnp.sum(e, axis=1, keepdims=True))
        half = soft.astype(BF16)
        gs = mm(dot, vt, TN)
        gs = soft * (gs - jnp.sum(soft * gs, axis=1, keepdims=True))
        gh = gs.astype(BF16)
        db[q, :] += gs
        att = mm(vt, half, NT)
        dq = mm(kt, gh, NT) * scale
        outs.append(jnp.concatenate([att, dq.astype(BF16).astype(F32)], axis=0))
        dk = dk + mm(qt, gh)
        dv = dv + mm(dot, half)
    dkv[row, 0:32, :] = (dk * scale).astype(dkv.dtype)
    dkv[row, 32:64, :] = dv.astype(dkv.dtype)
    return jnp.concatenate(outs, axis=1)


TN = (((0,), (0,)), ((), ()))
NT = (((1,), (1,)), ((), ()))


def mm(a, b, dims=(((1,), (0,)), ((), ()))):
    return lax.dot_general(a, b, dims, preferred_element_type=F32)


def halves(a):
    hi = a.astype(BF16)
    return hi, (a - hi.astype(F32)).astype(BF16)


class Fan:
    def __init__(self, p, send, recv):
        self.p, self.send, self.recv = p, send, recv

    def members(self, stage, src, dst):
        return self.all(stage, src, dst, self.p.h, self.p.member)

    def blocks(self, stage, src, dst):
        return self.all(stage, src, dst, self.p.g, self.p.block)

    def all(self, stage, src, dst, me, device):
        copies = []
        for k in ORDER:
            n = (me + k) % 8
            c = remote(src(n), dst(k), self.send.at[stage, k - 1], self.recv.at[stage, k - 1], device(n))
            c.start()
            copies.append(c)
        return copies

    def partner(self, stage, src, dst):
        c = remote(src, dst, self.send.at[stage, 0], self.recv.at[stage, 0], self.p.partner())
        c.start()
        return [c]


def finish(copies):
    for c in copies:
        c.wait()


class Reduce:
    def __init__(self, p, w, o, bufs, sems):
        self.p, self.w, self.o = p, w, o
        self.b0, self.a0, self.b1, self.a1 = bufs
        self.fan = Fan(p, *sems)
        self.n = w.shape[1] // 8
        self.lanes = pl.ds(aligned(p.core, 128), 128)
        self.copies = []

    def rows(self, h):
        return pl.ds(aligned(h, self.n), self.n)

    def pair(self):
        self.copies = self.fan.partner(0, self.w.at[1 - self.p.core], self.b0)

    def member(self):
        finish(self.copies)
        self.a0[...] = self.w[self.p.core] + self.b0[...]
        self.copies = self.fan.members(1, lambda h: self.a0.at[self.rows(h)], lambda k: self.b1.at[k - 1])

    def block(self):
        finish(self.copies)
        total = self.a0[self.rows(self.p.h)]
        for k in range(7):
            total = total + self.b1[k]
        self.a1[self.p.g] = total
        piece = self.a1.at[self.p.g]
        self.copies = self.fan.blocks(2, lambda g: piece, lambda k: piece)

    def back_member(self):
        finish(self.copies)
        self.o[self.rows(self.p.h), self.lanes] = sum_of(self.a1)
        piece = self.o.at[self.rows(self.p.h), self.lanes]
        self.copies = self.fan.members(3, lambda h: piece, lambda k: piece)

    def back_pair(self):
        finish(self.copies)
        piece = self.o.at[:, self.lanes]
        self.copies = self.fan.partner(4, piece, piece)

    def done(self):
        finish(self.copies)
        self.copies = []


def only(value, n, i):
    row = lax.broadcasted_iota(jnp.int32, value.shape, 0) % n
    return jnp.where(row == i, value, jnp.zeros_like(value))


def spread(pbt):
    return jnp.broadcast_to(pbt.astype(F32)[:, None, :], (8, 16, 128)).reshape(128, 128)


def main_kernel(
    hom_in, slope_in, gain_in, wq_in, wk_in, wv_in, wg_in, wo_in, pbt_in, pair_hbm,
    align, bo, oa, ob, ex_out,
    sc, sm,
):
    p = Place()
    z_lo, r4 = p.spot(p.h)
    toks = pl.ds(aligned(r4, 64), 64)
    here = pl.ds(aligned(p.g, 256), 256)
    cols = pl.ds(aligned(p.seq, 512), 512)
    per = 8 // CHUNKS
    xr, xt, kv, bias, db, dkv, parts = (sc[n] for n in ("xr", "xt", "kv", "bias", "db", "dkv", "parts"))
    rows_buf, local = sc["rows"], sm["local"]

    greet(
        [p.member((p.h + k) % 8) for k in range(1, 8)]
        + [p.block((p.g + k) % 8) for k in range(1, 8)]
        + [p.partner()]
    )
    loads = {}
    names = ("hom", "gain", "wk", "wv", "slope", "wo", "wg", "wq", "pbt")
    for n, (name, src) in enumerate(
        zip(names, (hom_in, gain_in, wk_in, wv_in, slope_in, wo_in, wg_in, wq_in, pbt_in))
    ):
        loads[name] = pltpu.make_async_copy(src, sc[name], sm["in"].at[n])
        loads[name].start()

    def stream(n):
        return pltpu.make_async_copy(pair_hbm.at[pl.ds(n * 16, 16)], rows_buf.at[n % 2], sm["hbm"].at[n % 2])

    stream(0).start()
    stream(1).start()
    hom, gain, wk, wv, slope, wo, wg, wq, pbt = (sc[n] for n in names)

    loads["hom"].wait()
    loads["gain"].wait()
    x = jnp.transpose(hom[...].astype(F32))
    centered = x - jnp.mean(x, axis=0, keepdims=True)
    inv = lax.rsqrt(jnp.mean(centered * centered, axis=0, keepdims=True) + 1e-05)
    hat = centered * inv
    scale_t = jnp.transpose(jnp.broadcast_to(gain[...], (256, 256)))
    normed = (hat * scale_t).astype(BF16)
    t_ref = sc["t"]
    loads["wk"].wait()
    loads["wv"].wait()
    for n, w in enumerate((wk, wv)):
        t_ref[:, n * 32 : n * 32 + 32, :] = mm(w[...], normed, TN).astype(BF16).reshape(8, 32, 256)
    pl.semaphore_wait(pltpu.get_barrier_semaphore(), 15)
    fan = Fan(p, sm["send"], sm["recv"])

    moved = fan.members(0, lambda h: t_ref.at[h, 0:64], lambda k: xr.at[z_lo, r4, 0:64])
    own_t = pltpu.make_async_copy(t_ref.at[p.h, 0:64], xr.at[z_lo, r4, 0:64], local.at[0])
    own_t.start()
    sc["hat"][...] = hat
    sc["scale"][...] = scale_t
    sc["inv"][...] = jnp.broadcast_to(inv, (8, 256))
    sc["normed"][...] = normed
    for name in ("slope", "wo", "wg", "wq", "pbt"):
        loads[name].wait()
    t_ref[:, 64:96, :] = mm(wq[...], normed, TN).astype(BF16).reshape(8, 32, 256)
    gate = jax.nn.sigmoid(mm(wg[...], normed, TN))
    grad_gated = mm(wo[...], slope[...], NT)
    sc["gate"][...] = gate
    sc["gg"][...] = grad_gated
    t_ref[:, 96:128, :] = (grad_gated * gate).astype(BF16).reshape(8, 32, 256)
    moved_q = fan.members(12, lambda h: t_ref.at[h, 64:128], lambda k: xr.at[z_lo, r4, 64:128])
    own_q = pltpu.make_async_copy(t_ref.at[p.h, 64:128], xr.at[z_lo, r4, 64:128], local.at[3])
    own_q.start()

    b_ref, mask = sc["b"], sc["mask"]
    base = spread(pbt[...])
    for i in range(16):
        mask[i] = only(base, 16, i).astype(BF16)
    for n in range(4):
        stream(n).wait()
        out = mm(mask[0], rows_buf[n % 2, 0], NT)
        for i in range(1, 16):
            out = out + mm(mask[i], rows_buf[n % 2, i], NT)
        b_ref[:, n * 16 : (n + 1) * 16, :] = out.astype(BF16).reshape(8, 16, 512)
        if n + 2 < 4:
            stream(n + 2).start()
    biases = fan.members(1, lambda h: b_ref.at[h], lambda k: bias.at[toks, cols])
    own_b = pltpu.make_async_copy(b_ref.at[p.h], bias.at[toks, cols], local.at[1])
    own_b.start()
    normed_all = sc["xn"]
    moved_n = fan.members(13, lambda h: sc["normed"], lambda k: normed_all.at[z_lo, r4])
    own_n = pltpu.make_async_copy(sc["normed"], normed_all.at[z_lo, r4], local.at[3])

    def by_row(lo):
        for z in range(2):
            for pp in range(2):
                for i in range(2):
                    lane = pp * 128 + i * 64
                    xt[z * 4 + pp * 2 + i, lo : lo + 64] = jnp.concatenate(
                        [xr[z, r, lo : lo + 64, lane : lane + 64] for r in range(4)], axis=1
                    )

    own_t.wait()
    finish(moved)
    by_row(0)

    def keys(c, k):
        rows = pl.ds(c * per, per)
        return remote(
            xt.at[rows, 0:64], kv.at[rows, :, here], sm["ks"].at[c, k - 1], sm["kr"].at[c, k - 1],
            p.block((p.g + k) % 8),
        )

    def partial(c, k):
        rows = pl.ds(c * per, per)
        g = (p.g + k) % 8
        return remote(
            dkv.at[rows, :, pl.ds(aligned(g, 256), 256)],
            parts.at[k - 1, rows],
            sm["es"].at[c, k - 1],
            sm["er"].at[c, k - 1],
            p.block(g),
        )

    for c in range(CHUNKS):
        for k in ORDER:
            keys(c, k).start()
    own_k = pltpu.make_async_copy(xt.at[:, 0:64], kv.at[:, :, here], local.at[2])
    own_k.start()
    db[...] = jnp.zeros_like(db)
    own_q.wait()
    own_n.start()
    finish(moved_q)
    by_row(64)
    own_k.wait()
    own_b.wait()
    finish(biases)
    moved = []
    for b in range(2):
        part = bias.at[:, pl.ds(aligned(b * 2 + p.core, 512), 512)]
        moved += fan.partner(2 + b, part, part)
    finish(moved)

    ya, yd = sc["ya"], sc["yd"]

    def by_member(outs, dst, c):
        pieces = []
        for r in range(4):
            lane = slice(r * 64, r * 64 + 64)
            pieces.append(jnp.concatenate([outs[0][:, lane], outs[1][:, lane]], axis=1))
            dst[c, r] = pieces[r]
        return pieces

    ta, td, other, mine = sc["ta"], sc["td"], sc["other"], sc["mine"]

    def give(stage, src, dst, k, z):
        h = (p.h + k) % 8
        return remote(
            src.at[pl.ds(z * 2, 2), p.spot(h)[1]], dst.at[p.h],
            sm["send"].at[stage, k - 1], sm["recv"].at[stage, k - 1], p.member(h),
        )

    def keep(n, src, dst):
        return pltpu.make_async_copy(src.at[pl.ds(z_lo * 2, 2), r4], dst.at[p.h], local.at[n])

    def give_half(stage, n, src, dst, z):
        @pl.when(z_lo == z)
        def _():
            for k in (4, 2, 6):
                give(stage, src, dst, k, z).start()
            keep(n, src, dst).start()

        @pl.when(z_lo != z)
        def _():
            for k in (3, 5, 1, 7):
                give(stage, src, dst, k, z).start()

    def taken(stage, n, src, dst):
        keep(n, src, dst).wait()
        for k in ORDER:
            give(stage, src, dst, k, 0).wait()

    def step(c, carry):
        for k in ORDER:
            keys(c, k).wait_recv()
        outs = []
        for i in range(per):
            outs.append(row_backward(xt, kv, bias, db, dkv, c * per + i))
        for k in ORDER:
            partial(c, k).start()
        by_member(outs, ya, c)
        for z in range(2):

            @pl.when(c == 2 * z + 1)
            def _():
                give_half(6, 0, ya, ta, z)

        return carry

    lax.fori_loop(0, CHUNKS, step, 0)

    stream(0).start()
    stream(1).start()
    pair = []
    for b in range(2):
        pair += fan.partner(4 + b, db.at[:, pl.ds(aligned(b * 2 + 1 - p.core, 512), 512)], other.at[b])
    own_n.wait()
    finish(moved_n)
    dw = sc["dw"]
    dw[...] = jnp.zeros_like(dw)

    def total(c, carry):
        for k in ORDER:
            partial(c, k).wait_recv()
        outs = []
        for i in range(per):
            row = c * per + i
            t = dkv[row, :, here].astype(F32)
            for k in range(7):
                t = t + parts[k, row].astype(F32)
            outs.append(t)
        grad = dw[...]
        lanes = pl.ds(aligned(c % 2, 128), 128)
        for r, piece in enumerate(by_member(outs, yd, c)):
            hi, lo = halves(piece)
            n = normed_all[c // 2, r, :, lanes]
            grad = grad + mm(hi, n, NT) + mm(lo, n, NT)
        dw[...] = grad
        return carry

    lax.fori_loop(0, 2, total, 0)
    give_half(8, 2, yd, td, 0)
    for b in range(2):
        pair[b].wait()
        mine[b] = (db[:, pl.ds(aligned(b * 2 + p.core, 512), 512)] + other[b]).astype(BF16)

    def bias_of(h):
        z, r = p.spot(h)
        return mine.at[z, pl.ds(aligned(r, 64), 64)]

    bias_back = fan.members(7, bias_of, lambda k: bo.at[p.h])
    own_m = pltpu.make_async_copy(bias_of(p.h), bo.at[p.h], local.at[1])
    own_m.start()

    def assemble(src, part):
        rows = slice(part * 32, part * 32 + 32)
        return jnp.concatenate([src[:, pp, rows, :].reshape(256, 128) for pp in range(2)], axis=1)

    taken(6, 0, ya, ta)
    attended = assemble(ta, 0)
    dq = assemble(ta, 1).astype(BF16)
    gate = sc["gate"][...]
    gated = (gate * attended).astype(BF16)
    grad_gate = (sc["gg"][...] * attended * gate * (1.0 - gate)).astype(BF16)
    sc["dq"][...] = dq
    sc["dg"][...] = grad_gate
    normed = sc["normed"][...]
    wa = sc["wa"]

    def put(dst, n, value):
        for i in range(2):
            dst[i, n * 256 : n * 256 + 256, :] = value[:, i * 128 : i * 128 + 128]

    put(wa, 0, mm(normed, dq, NT))
    put(wa, 1, mm(normed, grad_gate, NT))
    put(wa, 2, mm(gated, slope[...]))
    first = Reduce(p, wa, oa, [sc[n] for n in ("a_b0", "a_a0", "a_b1", "a_a1")], (sm["as"], sm["ar"]))
    first.pair()
    lax.fori_loop(2, 3, total, 0)
    first.member()

    own_m.wait()
    finish(bias_back)
    grad_bias = jnp.zeros((128, 128), F32)
    for n in range(4):
        stream(n).wait()
        part = bo[:, n * 16 : (n + 1) * 16, :].reshape(128, 512)
        for i in range(16):
            grad_bias = grad_bias + mm(only(part, 16, i), rows_buf[n % 2, i])
        if n + 2 < 4:
            stream(n + 2).start()
    ex, ex_own, exm, exb = sc["ex"], sc["ex_own"], sc["exm"], sc["exb"]
    ex[0:8, :] = jnp.sum(grad_bias.reshape(8, 16, 128), axis=1)
    grad_normed = mm(wq[...], sc["dq"][...]) + mm(wg[...], sc["dg"][...])

    lax.fori_loop(3, 4, total, 0)
    dw_r, dw_s, dw_o = sc["dw_r"], sc["dw_s"], sc["dw_o"]
    eight = pl.ds(aligned(p.g, 8), 8)
    weights = fan.blocks(14, lambda g: dw.at[pl.ds(aligned(g, 8), 8)], lambda k: dw_r.at[k - 1])
    give_half(8, 2, yd, td, 1)
    first.block()
    finish(weights)
    grad = dw[eight]
    for k in range(7):
        grad = grad + dw_r[k]
    dw_s[...] = grad
    weights = fan.partner(15, dw_s, dw_o)

    taken(8, 2, yd, td)
    dk_hi, dk_lo = halves(assemble(td, 0))
    dv_hi, dv_lo = halves(assemble(td, 1))
    grad_normed = grad_normed + mm(wk[...], dk_hi) + mm(wk[...], dk_lo) + mm(wv[...], dv_hi) + mm(wv[...], dv_lo)
    hat = sc["hat"][...]
    by_gain = jnp.sum(jnp.transpose(grad_normed * hat), axis=0, keepdims=True)
    ex[8:16, :] = jnp.concatenate([by_gain[:, :128], by_gain[:, 128:], jnp.zeros((6, 128), F32)], axis=0)
    extra = fan.partner(9, ex, ex_own)
    finish(weights)
    ob[p.h, eight] = dw_s[...] + dw_o[...]
    piece = ob.at[p.h, eight]
    weights = fan.blocks(16, lambda g: piece, lambda k: piece)
    finish(extra)
    exm[p.h] = ex[...] + ex_own[...]
    extra = fan.members(10, lambda h: exm.at[p.h], lambda k: exm.at[p.h])
    first.back_member()

    scaled = grad_normed * sc["scale"][...]
    m1 = jnp.mean(scaled, axis=0, keepdims=True)
    m2 = jnp.mean(scaled * hat, axis=0, keepdims=True)
    align[...] = jnp.transpose(sc["inv"][0:1, :] * (scaled - m1 - hat * m2)).astype(BF16)

    finish(weights)
    weights = fan.members(17, lambda h: ob.at[p.h], lambda k: ob.at[p.h])
    finish(extra)
    exb[p.g] = sum_of(exm)
    extra = fan.blocks(11, lambda g: exb.at[p.g], lambda k: exb.at[p.g])
    first.back_pair()
    finish(extra)
    ex_out[0:16, :] = sum_of(exb)
    ex_out[16:24, :] = pbt[...].astype(F32)
    finish(weights)
    first.done()

    def drain(c, carry):
        for k in ORDER:
            keys(c, k).wait_send()
            partial(c, k).wait_send()
        return carry

    lax.fori_loop(0, CHUNKS, drain, 0)


def sum_of(ref):
    total = ref[0]
    for n in range(1, 8):
        total = total + ref[n]
    return total


def main(hom, slope, gain, wq, wk, wv, wg, wo, pbt, pair_rows):
    dma = pltpu.SemaphoreType.DMA
    vmem = pltpu.VMEM

    def reduce_bufs(name, rows):
        return {
            name + "_b0": vmem((rows, 128), F32),
            name + "_a0": vmem((rows, 128), F32),
            name + "_b1": vmem((7, rows // 8, 128), F32),
            name + "_a1": vmem((8, rows // 8, 128), F32),
        }

    square = vmem((256, 256), F32)
    square_half = vmem((256, 256), BF16)
    scratch = {
        "rows": vmem((2, 16, 512, 128), BF16),
        "mask": vmem((16, 128, 128), BF16),
        "hom": square_half, "slope": square_half, "gain": vmem((1, 256), F32), "pbt": vmem((8, 128), BF16),
        "wq": square_half, "wk": square_half, "wv": square_half, "wg": square_half, "wo": square_half,
        "hat": square, "scale": square, "inv": vmem((8, 256), F32), "gate": square, "gg": square,
        "normed": square_half, "dq": square_half, "dg": square_half,
        "t": vmem((8, 128, 256), BF16),
        "b": vmem((8, 64, 512), BF16),
        "xr": vmem((2, 4, 128, 256), BF16),
        "xt": vmem((8, 128, 256), BF16),
        "kv": vmem((8, 64, 2048), BF16),
        "bias": vmem((256, 2048), BF16),
        "db": vmem((256, 2048), F32),
        "dkv": vmem((8, 64, 2048), BF16),
        "parts": vmem((7, 8, 64, 256), BF16),
        "ya": vmem((4, 4, 64, 128), F32),
        "yd": vmem((4, 4, 64, 128), F32),
        "ta": vmem((8, 2, 64, 128), F32),
        "td": vmem((8, 2, 64, 128), F32),
        "mine": vmem((2, 256, 512), BF16),
        "other": vmem((2, 256, 512), F32),
        "wa": vmem((2, 768, 128), F32),
        "xn": vmem((2, 4, 256, 256), BF16),
        "dw": vmem((64, 256), F32), "dw_r": vmem((7, 8, 256), F32),
        "dw_s": vmem((8, 256), F32), "dw_o": vmem((8, 256), F32),
        "ex": vmem((16, 128), F32), "ex_own": vmem((16, 128), F32),
        "exm": vmem((8, 16, 128), F32), "exb": vmem((8, 16, 128), F32),
        **reduce_bufs("a", 768),
    }
    sems = {
        "hbm": dma((2,)), "local": dma((4,)), "in": dma((9,)),
        "send": dma((18, 7)), "recv": dma((18, 7)),
        "ks": dma((CHUNKS, 7)), "kr": dma((CHUNKS, 7)),
        "es": dma((CHUNKS, 7)), "er": dma((CHUNKS, 7)),
        "as": dma((5, 7)), "ar": dma((5, 7)),
    }
    return pl.pallas_call(
        main_kernel,
        out_shape=(
            jax.ShapeDtypeStruct((256, 256), BF16),
            jax.ShapeDtypeStruct((8, 64, 512), BF16),
            jax.ShapeDtypeStruct((768, 256), F32),
            jax.ShapeDtypeStruct((8, 64, 256), F32),
            jax.ShapeDtypeStruct((24, 128), F32),
        ),
        in_specs=[HB] * 10,
        out_specs=(VM,) * 5,
        scratch_shapes=[scratch, sems],
        compiler_params=params(0),
        name="main",
    )(*[pltpu.with_memory_space_constraint(a, pltpu.HBM) for a in (hom, slope, gain, wq, wk, wv, wg, wo, pbt, pair_rows)])


def tail_kernel(bo, align, oa, ob, ex, pair, align_out, q, k, v, g, o, gain, bias, base, kv, sem):
    n = pl.program_id(0)
    moves = [(align, align_out), (ex.at[8:10], gain), (ex.at[0:8], bias)]
    moves += [(oa.at[0:256], q), (oa.at[256:512], g), (oa.at[512:768], o), (kv.at[0], k), (kv.at[1], v)]
    copies = [pltpu.make_async_copy(a, b, sem.at[i]) for i, (a, b) in enumerate(moves)]

    @pl.when(n == 0)
    def _():
        for i in range(2):
            kv[i] = jnp.transpose(ob[:, i * 32 : i * 32 + 32, :].reshape(256, 256))
        for c in copies:
            c.start()
        spreaded = spread(ex[16:24, :])
        for i in range(16):
            base[:, i * 128 : i * 128 + 128] = only(spreaded, 16, i).astype(BF16)

    part = jnp.transpose(bo[:, pl.ds(pl.multiple_of(n * 16, 16), 16), :].reshape(128, 512))
    for i in range(8):
        out = mm(part, base[:, i * 256 : i * 256 + 256]).astype(BF16)
        pair[2 * i] = out[:, :128]
        pair[2 * i + 1] = out[:, 128:]

    @pl.when(n == 3)
    def _():
        for c in copies:
            c.wait()


def tail(bo, align, oa, ob, ex):
    square = jax.ShapeDtypeStruct((256, 256), F32)
    return pl.pallas_call(
        tail_kernel,
        grid=(4,),
        out_shape=(
            jax.ShapeDtypeStruct((64, 512, 128), BF16),
            jax.ShapeDtypeStruct((256, 256), BF16),
            square, square, square, square, square,
            jax.ShapeDtypeStruct((2, 128), F32),
            jax.ShapeDtypeStruct((8, 128), F32),
        ),
        in_specs=[VM] * 5,
        out_specs=(pl.BlockSpec((16, 512, 128), lambda n: (n, 0, 0)),) + (HB,) * 8,
        scratch_shapes=[pltpu.VMEM((128, 2048), BF16), pltpu.VMEM((2, 256, 256), F32), pltpu.SemaphoreType.DMA((8,))],
        compiler_params=pltpu.CompilerParams(vmem_limit_bytes=32 * 1024 * 1024),
        name="tail",
    )(bo, align, oa, ob, ex)


def body(
    homolog_embedding,
    pair_input_rows,
    incoming_slope,
    rescale_factor,
    probe_weights,
    lookup_weights,
    content_weights,
    sigmoid_weights,
    final_projection,
    pair_bias_matrix,
):
    rows, toks, width = homolog_embedding.shape
    align, db_own, oa, ob, extra = main(
        homolog_embedding.reshape(-1, width),
        incoming_slope.reshape(-1, width),
        rescale_factor.reshape(1, width),
        probe_weights,
        lookup_weights,
        content_weights,
        sigmoid_weights,
        final_projection,
        pair_bias_matrix.T,
        pair_input_rows,
    )
    pair_grad, align, grad_q, grad_k, grad_v, grad_g, grad_o, gain, bias = tail(
        db_own, align, oa, ob, extra
    )
    return (
        align.reshape(rows, toks, width),
        pair_grad,
        gain.reshape(width),
        grad_q,
        grad_k,
        grad_v,
        grad_g,
        grad_o,
        bias.T,
    )


def solution(mesh):
    in_specs = (
        P("seq", "res", None),
        P("res", "seq", None),
        P("seq", "res", None),
        P(),
        P(),
        P(),
        P(),
        P(),
        P(),
        P(),
    )
    out_specs = (P("seq", "res", None), P("res", "seq", None), P(), P(), P(), P(), P(), P(), P())
    return jax.shard_map(body, mesh=mesh, in_specs=in_specs, out_specs=out_specs, check_vma=False)
```

```python
import functools
import math

import jax
import jax.numpy as jnp
from jax import lax
from jax.experimental import pallas as pl
from jax.experimental.pallas import tpu as pltpu
from jax.sharding import PartitionSpec as P

MESH = pl.DeviceIdType.MESH
F32 = jnp.float32
BF16 = jnp.bfloat16
VM = pl.BlockSpec(memory_space=pltpu.VMEM)
HB = pl.BlockSpec(memory_space=pltpu.HBM)


class Place:
    def __init__(self):
        seq = lax.axis_index("seq")
        res = lax.axis_index("res")
        self.seq, self.res = seq, res
        self.z_lo, self.core = seq // 2, seq % 2
        self.g, self.z_hi = res // 4, res % 2
        self.x_hi = self.g % 2
        x_lo = (res // 2) % 2
        self.h = ((x_lo + self.x_hi) % 2) * 4 + self.z_hi * 2 + self.z_lo

    def spot(self, h):
        return h % 2, ((h // 4 + self.x_hi) % 2) * 2 + (h // 2) % 2

    def member(self, h):
        z_lo, r4 = self.spot(h)
        return (z_lo * 2 + self.core, self.g * 4 + r4)

    def block(self, g):
        return (self.seq, g * 4 + ((self.h // 4 + g % 2) % 2) * 2 + self.z_hi)

    def partner(self):
        return (self.z_lo * 2 + 1 - self.core, self.res)


def greet(devices):
    barrier = pltpu.get_barrier_semaphore()
    for device in devices:
        pl.semaphore_signal(barrier, inc=1, device_id=device, device_id_type=MESH)


def remote(src, dst, send, recv, device):
    return pltpu.make_async_remote_copy(
        src_ref=src, dst_ref=dst, send_sem=send, recv_sem=recv, device_id=device, device_id_type=MESH
    )


def params(collective_id):
    return pltpu.CompilerParams(
        collective_id=collective_id, has_side_effects=True, vmem_limit_bytes=48 * 1024 * 1024
    )


def aligned(x, n):
    return pl.multiple_of(x * n, n)


ORDER = (4, 3, 5, 2, 6, 1, 7)
CHUNKS = 4
QB = 128


ORDER = (4, 3, 5, 2, 6, 1, 7)
CHUNKS = 4
QB = 128


def row_backward(xt, kv, bias, db, dkv, row):
    scale = 1.0 / math.sqrt(32)
    kt = kv[row, 0:32, :]
    vt = kv[row, 32:64, :]
    dk = jnp.zeros((32, 2048), F32)
    dv = jnp.zeros((32, 2048), F32)
    outs = []
    for n in range(256 // QB):
        q = pl.ds(n * QB, QB)
        qt = xt[row, 64:96, q]
        dot = xt[row, 96:128, q]
        s = mm(qt, kt, TN) * scale
        s = s + bias[q, :].astype(F32)
        e = jnp.exp(s - jnp.max(s, axis=1, keepdims=True))
        soft = e * (1.0 / jnp.sum(e, axis=1, keepdims=True))
        half = soft.astype(BF16)
        gs = mm(dot, vt, TN)
        gs = soft * (gs - jnp.sum(soft * gs, axis=1, keepdims=True))
        gh = gs.astype(BF16)
        db[q, :] += gs
        att = mm(vt, half, NT)
        dq = mm(kt, gh, NT) * scale
        outs.append(jnp.concatenate([att, dq.astype(BF16).astype(F32)], axis=0))
        dk = dk + mm(qt, gh)
        dv = dv + mm(dot, half)
    dkv[row, 0:32, :] = (dk * scale).astype(dkv.dtype)
    dkv[row, 32:64, :] = dv.astype(dkv.dtype)
    return jnp.concatenate(outs, axis=1)


TN = (((0,), (0,)), ((), ()))
NT = (((1,), (1,)), ((), ()))


def mm(a, b, dims=(((1,), (0,)), ((), ()))):
    return lax.dot_general(a, b, dims, preferred_element_type=F32)


def halves(a):
    hi = a.astype(BF16)
    return hi, (a - hi.astype(F32)).astype(BF16)


class Fan:
    def __init__(self, p, send, recv):
        self.p, self.send, self.recv = p, send, recv

    def members(self, stage, src, dst):
        return self.all(stage, src, dst, self.p.h, self.p.member)

    def blocks(self, stage, src, dst):
        return self.all(stage, src, dst, self.p.g, self.p.block)

    def all(self, stage, src, dst, me, device):
        copies = []
        for k in ORDER:
            n = (me + k) % 8
            c = remote(src(n), dst(k), self.send.at[stage, k - 1], self.recv.at[stage, k - 1], device(n))
            c.start()
            copies.append(c)
        return copies

    def partner(self, stage, src, dst):
        c = remote(src, dst, self.send.at[stage, 0], self.recv.at[stage, 0], self.p.partner())
        c.start()
        return [c]


def finish(copies):
    for c in copies:
        c.wait()


class Reduce:
    def __init__(self, p, w, o, bufs, sems):
        self.p, self.w, self.o = p, w, o
        self.b0, self.a0, self.b1, self.a1 = bufs
        self.fan = Fan(p, *sems)
        self.n = w.shape[1] // 8
        self.lanes = pl.ds(aligned(p.core, 128), 128)
        self.copies = []

    def rows(self, h):
        return pl.ds(aligned(h, self.n), self.n)

    def pair(self):
        self.copies = self.fan.partner(0, self.w.at[1 - self.p.core], self.b0)

    def member(self):
        finish(self.copies)
        self.a0[...] = self.w[self.p.core] + self.b0[...]
        self.copies = self.fan.members(1, lambda h: self.a0.at[self.rows(h)], lambda k: self.b1.at[k - 1])

    def block(self):
        finish(self.copies)
        total = self.a0[self.rows(self.p.h)]
        for k in range(7):
            total = total + self.b1[k]
        self.a1[self.p.g] = total
        piece = self.a1.at[self.p.g]
        self.copies = self.fan.blocks(2, lambda g: piece, lambda k: piece)

    def back_member(self):
        finish(self.copies)
        self.o[self.rows(self.p.h), self.lanes] = sum_of(self.a1)
        piece = self.o.at[self.rows(self.p.h), self.lanes]
        self.copies = self.fan.members(3, lambda h: piece, lambda k: piece)

    def back_pair(self):
        finish(self.copies)
        piece = self.o.at[:, self.lanes]
        self.copies = self.fan.partner(4, piece, piece)

    def done(self):
        finish(self.copies)
        self.copies = []


def only(value, n, i):
    row = lax.broadcasted_iota(jnp.int32, value.shape, 0) % n
    return jnp.where(row == i, value, jnp.zeros_like(value))


def spread(pbt):
    return jnp.broadcast_to(pbt.astype(F32)[:, None, :], (8, 16, 128)).reshape(128, 128)


def main_kernel(
    hom_in, slope_in, gain_in, wq_in, wk_in, wv_in, wg_in, wo_in, pbt_in, pair_hbm,
    align, bo, oa, ob, ex_out,
    sc, sm,
):
    p = Place()
    z_lo, r4 = p.spot(p.h)
    toks = pl.ds(aligned(r4, 64), 64)
    here = pl.ds(aligned(p.g, 256), 256)
    cols = pl.ds(aligned(p.seq, 512), 512)
    per = 8 // CHUNKS
    xr, xt, kv, bias, db, dkv, parts = (sc[n] for n in ("xr", "xt", "kv", "bias", "db", "dkv", "parts"))
    rows_buf, local = sc["rows"], sm["local"]

    greet(
        [p.member((p.h + k) % 8) for k in range(1, 8)]
        + [p.block((p.g + k) % 8) for k in range(1, 8)]
        + [p.partner()]
    )
    loads = {}
    names = ("hom", "gain", "wk", "wv", "slope", "wo", "wg", "wq", "pbt")
    for n, (name, src) in enumerate(
        zip(names, (hom_in, gain_in, wk_in, wv_in, slope_in, wo_in, wg_in, wq_in, pbt_in))
    ):
        loads[name] = pltpu.make_async_copy(src, sc[name], sm["in"].at[n])
        loads[name].start()

    def stream(n):
        return pltpu.make_async_copy(pair_hbm.at[pl.ds(n * 16, 16)], rows_buf.at[n % 2], sm["hbm"].at[n % 2])

    stream(0).start()
    stream(1).start()
    hom, gain, wk, wv, slope, wo, wg, wq, pbt = (sc[n] for n in names)

    loads["hom"].wait()
    loads["gain"].wait()
    x = jnp.transpose(hom[...].astype(F32))
    centered = x - jnp.mean(x, axis=0, keepdims=True)
    inv = lax.rsqrt(jnp.mean(centered * centered, axis=0, keepdims=True) + 1e-05)
    hat = centered * inv
    scale_t = jnp.transpose(jnp.broadcast_to(gain[...], (256, 256)))
    normed = (hat * scale_t).astype(BF16)
    t_ref = sc["t"]
    loads["wk"].wait()
    loads["wv"].wait()
    for n, w in enumerate((wk, wv)):
        t_ref[:, n * 32 : n * 32 + 32, :] = mm(w[...], normed, TN).astype(BF16).reshape(8, 32, 256)
    pl.semaphore_wait(pltpu.get_barrier_semaphore(), 15)
    fan = Fan(p, sm["send"], sm["recv"])

    moved = fan.members(0, lambda h: t_ref.at[h, 0:64], lambda k: xr.at[z_lo, r4, 0:64])
    own_t = pltpu.make_async_copy(t_ref.at[p.h, 0:64], xr.at[z_lo, r4, 0:64], local.at[0])
    own_t.start()
    sc["hat"][...] = hat
    sc["scale"][...] = scale_t
    sc["inv"][...] = jnp.broadcast_to(inv, (8, 256))
    sc["normed"][...] = normed
    for name in ("slope", "wo", "wg", "wq", "pbt"):
        loads[name].wait()
    t_ref[:, 64:96, :] = mm(wq[...], normed, TN).astype(BF16).reshape(8, 32, 256)
    gate = jax.nn.sigmoid(mm(wg[...], normed, TN))
    grad_gated = mm(wo[...], slope[...], NT)
    sc["gate"][...] = gate
    sc["gg"][...] = grad_gated
    t_ref[:, 96:128, :] = (grad_gated * gate).astype(BF16).reshape(8, 32, 256)
    moved_q = fan.members(12, lambda h: t_ref.at[h, 64:128], lambda k: xr.at[z_lo, r4, 64:128])
    own_q = pltpu.make_async_copy(t_ref.at[p.h, 64:128], xr.at[z_lo, r4, 64:128], local.at[3])
    own_q.start()

    b_ref, mask = sc["b"], sc["mask"]
    base = spread(pbt[...])
    for i in range(16):
        mask[i] = only(base, 16, i).astype(BF16)
    for n in range(4):
        stream(n).wait()
        out = mm(mask[0], rows_buf[n % 2, 0], NT)
        for i in range(1, 16):
            out = out + mm(mask[i], rows_buf[n % 2, i], NT)
        b_ref[:, n * 16 : (n + 1) * 16, :] = out.astype(BF16).reshape(8, 16, 512)
        if n + 2 < 4:
            stream(n + 2).start()
    biases = fan.members(1, lambda h: b_ref.at[h], lambda k: bias.at[toks, cols])
    own_b = pltpu.make_async_copy(b_ref.at[p.h], bias.at[toks, cols], local.at[1])
    own_b.start()
    normed_all = sc["xn"]
    moved_n = fan.members(13, lambda h: sc["normed"], lambda k: normed_all.at[z_lo, r4])
    own_n = pltpu.make_async_copy(sc["normed"], normed_all.at[z_lo, r4], local.at[3])

    def by_row(lo):
        for z in range(2):
            for pp in range(2):
                for i in range(2):
                    lane = pp * 128 + i * 64
                    xt[z * 4 + pp * 2 + i, lo : lo + 64] = jnp.concatenate(
                        [xr[z, r, lo : lo + 64, lane : lane + 64] for r in range(4)], axis=1
                    )

    own_t.wait()
    finish(moved)
    by_row(0)

    def keys(c, k):
        rows = pl.ds(c * per, per)
        return remote(
            xt.at[rows, 0:64], kv.at[rows, :, here], sm["ks"].at[c, k - 1], sm["kr"].at[c, k - 1],
            p.block((p.g + k) % 8),
        )

    def partial(c, k):
        rows = pl.ds(c * per, per)
        g = (p.g + k) % 8
        return remote(
            dkv.at[rows, :, pl.ds(aligned(g, 256), 256)],
            parts.at[k - 1, rows],
            sm["es"].at[c, k - 1],
            sm["er"].at[c, k - 1],
            p.block(g),
        )

    for c in range(CHUNKS):
        for k in ORDER:
            keys(c, k).start()
    own_k = pltpu.make_async_copy(xt.at[:, 0:64], kv.at[:, :, here], local.at[2])
    own_k.start()
    db[...] = jnp.zeros_like(db)
    own_q.wait()
    own_n.start()
    finish(moved_q)
    by_row(64)
    own_k.wait()
    own_b.wait()
    finish(biases)
    moved = []
    for b in range(2):
        part = bias.at[:, pl.ds(aligned(b * 2 + p.core, 512), 512)]
        moved += fan.partner(2 + b, part, part)
    finish(moved)

    ya, yd = sc["ya"], sc["yd"]

    def by_member(outs, dst, c):
        pieces = []
        for r in range(4):
            lane = slice(r * 64, r * 64 + 64)
            pieces.append(jnp.concatenate([outs[0][:, lane], outs[1][:, lane]], axis=1))
            dst[c, r] = pieces[r]
        return pieces

    ta, td, other, mine = sc["ta"], sc["td"], sc["other"], sc["mine"]

    def give(stage, src, dst, k, z):
        h = (p.h + k) % 8
        return remote(
            src.at[pl.ds(z * 2, 2), p.spot(h)[1]], dst.at[p.h],
            sm["send"].at[stage, k - 1], sm["recv"].at[stage, k - 1], p.member(h),
        )

    def keep(n, src, dst):
        return pltpu.make_async_copy(src.at[pl.ds(z_lo * 2, 2), r4], dst.at[p.h], local.at[n])

    def give_half(stage, n, src, dst, z):
        @pl.when(z_lo == z)
        def _():
            for k in (4, 2, 6):
                give(stage, src, dst, k, z).start()
            keep(n, src, dst).start()

        @pl.when(z_lo != z)
        def _():
            for k in (3, 5, 1, 7):
                give(stage, src, dst, k, z).start()

    def taken(stage, n, src, dst):
        keep(n, src, dst).wait()
        for k in ORDER:
            give(stage, src, dst, k, 0).wait()

    def step(c, carry):
        for k in ORDER:
            keys(c, k).wait_recv()
        outs = []
        for i in range(per):
            outs.append(row_backward(xt, kv, bias, db, dkv, c * per + i))
        for k in ORDER:
            partial(c, k).start()
        by_member(outs, ya, c)
        for z in range(2):

            @pl.when(c == 2 * z + 1)
            def _():
                give_half(6, 0, ya, ta, z)

        return carry

    lax.fori_loop(0, CHUNKS, step, 0)

    stream(0).start()
    stream(1).start()
    pair = []
    for b in range(2):
        pair += fan.partner(4 + b, db.at[:, pl.ds(aligned(b * 2 + 1 - p.core, 512), 512)], other.at[b])
    own_n.wait()
    finish(moved_n)
    dw = sc["dw"]
    dw[...] = jnp.zeros_like(dw)

    def total(c, carry):
        for k in ORDER:
            partial(c, k).wait_recv()
        outs = []
        for i in range(per):
            row = c * per + i
            t = dkv[row, :, here].astype(F32)
            for k in range(7):
                t = t + parts[k, row].astype(F32)
            outs.append(t)
        grad = dw[...]
        lanes = pl.ds(aligned(c % 2, 128), 128)
        for r, piece in enumerate(by_member(outs, yd, c)):
            hi, lo = halves(piece)
            n = normed_all[c // 2, r, :, lanes]
            grad = grad + mm(hi, n, NT) + mm(lo, n, NT)
        dw[...] = grad
        return carry

    lax.fori_loop(0, 2, total, 0)
    give_half(8, 2, yd, td, 0)
    for b in range(2):
        pair[b].wait()
        mine[b] = (db[:, pl.ds(aligned(b * 2 + p.core, 512), 512)] + other[b]).astype(BF16)

    def assemble(src, part):
        rows = slice(part * 32, part * 32 + 32)
        return jnp.concatenate([src[:, pp, rows, :].reshape(256, 128) for pp in range(2)], axis=1)

    taken(6, 0, ya, ta)
    attended = assemble(ta, 0)
    dq = assemble(ta, 1).astype(BF16)
    gate = sc["gate"][...]
    gated = (gate * attended).astype(BF16)
    grad_gate = (sc["gg"][...] * attended * gate * (1.0 - gate)).astype(BF16)
    sc["dq"][...] = dq
    sc["dg"][...] = grad_gate
    normed = sc["normed"][...]
    wa = sc["wa"]

    def put(dst, n, value):
        for i in range(2):
            dst[i, n * 256 : n * 256 + 256, :] = value[:, i * 128 : i * 128 + 128]

    put(wa, 0, mm(normed, dq, NT))
    put(wa, 1, mm(normed, grad_gate, NT))
    put(wa, 2, mm(gated, slope[...]))
    first = Reduce(p, wa, oa, [sc[n] for n in ("a_b0", "a_a0", "a_b1", "a_a1")], (sm["as"], sm["ar"]))
    first.pair()
    lax.fori_loop(2, 3, total, 0)
    first.member()

    def bias_of(h):
        z, r = p.spot(h)
        return mine.at[z, pl.ds(aligned(r, 64), 64)]

    bias_back = fan.members(7, bias_of, lambda k: bo.at[p.h])
    own_m = pltpu.make_async_copy(bias_of(p.h), bo.at[p.h], local.at[1])
    own_m.start()

    lax.fori_loop(3, 4, total, 0)
    dw_r, dw_s, dw_o = sc["dw_r"], sc["dw_s"], sc["dw_o"]
    eight = pl.ds(aligned(p.g, 8), 8)
    weights = fan.blocks(14, lambda g: dw.at[pl.ds(aligned(g, 8), 8)], lambda k: dw_r.at[k - 1])
    give_half(8, 2, yd, td, 1)
    grad_normed = mm(wq[...], sc["dq"][...]) + mm(wg[...], sc["dg"][...])
    first.block()
    finish(weights)
    grad = dw[eight]
    for k in range(7):
        grad = grad + dw_r[k]
    dw_s[...] = grad
    weights = fan.partner(15, dw_s, dw_o)

    own_m.wait()
    finish(bias_back)
    grad_bias = jnp.zeros((128, 128), F32)
    for n in range(4):
        stream(n).wait()
        part = bo[:, n * 16 : (n + 1) * 16, :].reshape(128, 512)
        for i in range(16):
            grad_bias = grad_bias + mm(only(part, 16, i), rows_buf[n % 2, i])
        if n + 2 < 4:
            stream(n + 2).start()
    ex, ex_own, exm, exb = sc["ex"], sc["ex_own"], sc["exm"], sc["exb"]
    ex[0:8, :] = jnp.sum(grad_bias.reshape(8, 16, 128), axis=1)
    finish(weights)
    ob[p.h, eight] = dw_s[...] + dw_o[...]
    piece = ob.at[p.h, eight]
    weights = fan.blocks(16, lambda g: piece, lambda k: piece)
    first.back_member()

    taken(8, 2, yd, td)
    dk_hi, dk_lo = halves(assemble(td, 0))
    dv_hi, dv_lo = halves(assemble(td, 1))
    grad_normed = grad_normed + mm(wk[...], dk_hi) + mm(wk[...], dk_lo) + mm(wv[...], dv_hi) + mm(wv[...], dv_lo)
    hat = sc["hat"][...]
    by_gain = jnp.sum(jnp.transpose(grad_normed * hat), axis=0, keepdims=True)
    ex[8:16, :] = jnp.concatenate([by_gain[:, :128], by_gain[:, 128:], jnp.zeros((6, 128), F32)], axis=0)
    extra = fan.partner(9, ex, ex_own)
    finish(weights)
    weights = fan.members(17, lambda h: ob.at[p.h], lambda k: ob.at[p.h])
    finish(extra)
    exm[p.h] = ex[...] + ex_own[...]
    extra = fan.members(10, lambda h: exm.at[p.h], lambda k: exm.at[p.h])

    scaled = grad_normed * sc["scale"][...]
    m1 = jnp.mean(scaled, axis=0, keepdims=True)
    m2 = jnp.mean(scaled * hat, axis=0, keepdims=True)
    align[...] = jnp.transpose(sc["inv"][0:1, :] * (scaled - m1 - hat * m2)).astype(BF16)

    finish(extra)
    exb[p.g] = sum_of(exm)
    extra = fan.blocks(11, lambda g: exb.at[p.g], lambda k: exb.at[p.g])
    first.back_pair()
    finish(extra)
    ex_out[0:16, :] = sum_of(exb)
    ex_out[16:24, :] = pbt[...].astype(F32)
    finish(weights)
    first.done()

    def drain(c, carry):
        for k in ORDER:
            keys(c, k).wait_send()
            partial(c, k).wait_send()
        return carry

    lax.fori_loop(0, CHUNKS, drain, 0)


def sum_of(ref):
    total = ref[0]
    for n in range(1, 8):
        total = total + ref[n]
    return total


def main(hom, slope, gain, wq, wk, wv, wg, wo, pbt, pair_rows):
    dma = pltpu.SemaphoreType.DMA
    vmem = pltpu.VMEM

    def reduce_bufs(name, rows):
        return {
            name + "_b0": vmem((rows, 128), F32),
            name + "_a0": vmem((rows, 128), F32),
            name + "_b1": vmem((7, rows // 8, 128), F32),
            name + "_a1": vmem((8, rows // 8, 128), F32),
        }

    square = vmem((256, 256), F32)
    square_half = vmem((256, 256), BF16)
    scratch = {
        "rows": vmem((2, 16, 512, 128), BF16),
        "mask": vmem((16, 128, 128), BF16),
        "hom": square_half, "slope": square_half, "gain": vmem((1, 256), F32), "pbt": vmem((8, 128), BF16),
        "wq": square_half, "wk": square_half, "wv": square_half, "wg": square_half, "wo": square_half,
        "hat": square, "scale": square, "inv": vmem((8, 256), F32), "gate": square, "gg": square,
        "normed": square_half, "dq": square_half, "dg": square_half,
        "t": vmem((8, 128, 256), BF16),
        "b": vmem((8, 64, 512), BF16),
        "xr": vmem((2, 4, 128, 256), BF16),
        "xt": vmem((8, 128, 256), BF16),
        "kv": vmem((8, 64, 2048), BF16),
        "bias": vmem((256, 2048), BF16),
        "db": vmem((256, 2048), F32),
        "dkv": vmem((8, 64, 2048), BF16),
        "parts": vmem((7, 8, 64, 256), BF16),
        "ya": vmem((4, 4, 64, 128), F32),
        "yd": vmem((4, 4, 64, 128), F32),
        "ta": vmem((8, 2, 64, 128), F32),
        "td": vmem((8, 2, 64, 128), F32),
        "mine": vmem((2, 256, 512), BF16),
        "other": vmem((2, 256, 512), F32),
        "wa": vmem((2, 768, 128), F32),
        "xn": vmem((2, 4, 256, 256), BF16),
        "dw": vmem((64, 256), F32), "dw_r": vmem((7, 8, 256), F32),
        "dw_s": vmem((8, 256), F32), "dw_o": vmem((8, 256), F32),
        "ex": vmem((16, 128), F32), "ex_own": vmem((16, 128), F32),
        "exm": vmem((8, 16, 128), F32), "exb": vmem((8, 16, 128), F32),
        **reduce_bufs("a", 768),
    }
    sems = {
        "hbm": dma((2,)), "local": dma((4,)), "in": dma((9,)),
        "send": dma((18, 7)), "recv": dma((18, 7)),
        "ks": dma((CHUNKS, 7)), "kr": dma((CHUNKS, 7)),
        "es": dma((CHUNKS, 7)), "er": dma((CHUNKS, 7)),
        "as": dma((5, 7)), "ar": dma((5, 7)),
    }
    return pl.pallas_call(
        main_kernel,
        out_shape=(
            jax.ShapeDtypeStruct((256, 256), BF16),
            jax.ShapeDtypeStruct((8, 64, 512), BF16),
            jax.ShapeDtypeStruct((768, 256), F32),
            jax.ShapeDtypeStruct((8, 64, 256), F32),
            jax.ShapeDtypeStruct((24, 128), F32),
        ),
        in_specs=[HB] * 10,
        out_specs=(VM,) * 5,
        scratch_shapes=[scratch, sems],
        compiler_params=params(0),
        name="main",
    )(*[pltpu.with_memory_space_constraint(a, pltpu.HBM) for a in (hom, slope, gain, wq, wk, wv, wg, wo, pbt, pair_rows)])


def tail_kernel(bo, align, oa, ob, ex, pair, align_out, q, k, v, g, o, gain, bias, base, kv, sem):
    n = pl.program_id(0)
    moves = [(align, align_out), (ex.at[8:10], gain), (ex.at[0:8], bias)]
    moves += [(oa.at[0:256], q), (oa.at[256:512], g), (oa.at[512:768], o), (kv.at[0], k), (kv.at[1], v)]
    copies = [pltpu.make_async_copy(a, b, sem.at[i]) for i, (a, b) in enumerate(moves)]

    @pl.when(n == 0)
    def _():
        for i in range(2):
            kv[i] = jnp.transpose(ob[:, i * 32 : i * 32 + 32, :].reshape(256, 256))
        for c in copies:
            c.start()
        spreaded = spread(ex[16:24, :])
        for i in range(16):
            base[:, i * 128 : i * 128 + 128] = only(spreaded, 16, i).astype(BF16)

    part = jnp.transpose(bo[:, pl.ds(pl.multiple_of(n * 16, 16), 16), :].reshape(128, 512))
    for i in range(8):
        out = mm(part, base[:, i * 256 : i * 256 + 256]).astype(BF16)
        pair[2 * i] = out[:, :128]
        pair[2 * i + 1] = out[:, 128:]

    @pl.when(n == 3)
    def _():
        for c in copies:
            c.wait()


def tail(bo, align, oa, ob, ex):
    square = jax.ShapeDtypeStruct((256, 256), F32)
    return pl.pallas_call(
        tail_kernel,
        grid=(4,),
        out_shape=(
            jax.ShapeDtypeStruct((64, 512, 128), BF16),
            jax.ShapeDtypeStruct((256, 256), BF16),
            square, square, square, square, square,
            jax.ShapeDtypeStruct((2, 128), F32),
            jax.ShapeDtypeStruct((8, 128), F32),
        ),
        in_specs=[VM] * 5,
        out_specs=(pl.BlockSpec((16, 512, 128), lambda n: (n, 0, 0)),) + (HB,) * 8,
        scratch_shapes=[pltpu.VMEM((128, 2048), BF16), pltpu.VMEM((2, 256, 256), F32), pltpu.SemaphoreType.DMA((8,))],
        compiler_params=pltpu.CompilerParams(vmem_limit_bytes=32 * 1024 * 1024),
        name="tail",
    )(bo, align, oa, ob, ex)


def body(
    homolog_embedding,
    pair_input_rows,
    incoming_slope,
    rescale_factor,
    probe_weights,
    lookup_weights,
    content_weights,
    sigmoid_weights,
    final_projection,
    pair_bias_matrix,
):
    rows, toks, width = homolog_embedding.shape
    align, db_own, oa, ob, extra = main(
        homolog_embedding.reshape(-1, width),
        incoming_slope.reshape(-1, width),
        rescale_factor.reshape(1, width),
        probe_weights,
        lookup_weights,
        content_weights,
        sigmoid_weights,
        final_projection,
        pair_bias_matrix.T,
        pair_input_rows,
    )
    pair_grad, align, grad_q, grad_k, grad_v, grad_g, grad_o, gain, bias = tail(
        db_own, align, oa, ob, extra
    )
    return (
        align.reshape(rows, toks, width),
        pair_grad,
        gain.reshape(width),
        grad_q,
        grad_k,
        grad_v,
        grad_g,
        grad_o,
        bias.T,
    )


def solution(mesh):
    in_specs = (
        P("seq", "res", None),
        P("res", "seq", None),
        P("seq", "res", None),
        P(),
        P(),
        P(),
        P(),
        P(),
        P(),
        P(),
    )
    out_specs = (P("seq", "res", None), P("res", "seq", None), P(), P(), P(), P(), P(), P(), P())
    return jax.shard_map(body, mesh=mesh, in_specs=in_specs, out_specs=out_specs, check_vma=False)
```

```python
import functools
import math

import jax
import jax.numpy as jnp
from jax import lax
from jax.experimental import pallas as pl
from jax.experimental.pallas import tpu as pltpu
from jax.sharding import PartitionSpec as P

MESH = pl.DeviceIdType.MESH
F32 = jnp.float32
BF16 = jnp.bfloat16
VM = pl.BlockSpec(memory_space=pltpu.VMEM)
HB = pl.BlockSpec(memory_space=pltpu.HBM)


class Place:
    def __init__(self):
        seq = lax.axis_index("seq")
        res = lax.axis_index("res")
        self.seq, self.res = seq, res
        self.z_lo, self.core = seq // 2, seq % 2
        self.g, self.z_hi = res // 4, res % 2
        self.x_hi = self.g % 2
        x_lo = (res // 2) % 2
        self.h = ((x_lo + self.x_hi) % 2) * 4 + self.z_hi * 2 + self.z_lo

    def spot(self, h):
        return h % 2, ((h // 4 + self.x_hi) % 2) * 2 + (h // 2) % 2

    def member(self, h):
        z_lo, r4 = self.spot(h)
        return (z_lo * 2 + self.core, self.g * 4 + r4)

    def block(self, g):
        return (self.seq, g * 4 + ((self.h // 4 + g % 2) % 2) * 2 + self.z_hi)

    def partner(self):
        return (self.z_lo * 2 + 1 - self.core, self.res)


def greet(devices):
    barrier = pltpu.get_barrier_semaphore()
    for device in devices:
        pl.semaphore_signal(barrier, inc=1, device_id=device, device_id_type=MESH)


def remote(src, dst, send, recv, device):
    return pltpu.make_async_remote_copy(
        src_ref=src, dst_ref=dst, send_sem=send, recv_sem=recv, device_id=device, device_id_type=MESH
    )


def params(collective_id):
    return pltpu.CompilerParams(
        collective_id=collective_id, has_side_effects=True, vmem_limit_bytes=48 * 1024 * 1024
    )


def aligned(x, n):
    return pl.multiple_of(x * n, n)


ORDER = (4, 3, 5, 2, 6, 1, 7)
CHUNKS = 4
QB = 128


ORDER = (4, 3, 5, 2, 6, 1, 7)
CHUNKS = 4
QB = 128


def row_backward(xt, kv, bias, db, dkv, row):
    scale = 1.0 / math.sqrt(32)
    kt = kv[row, 0:32, :]
    vt = kv[row, 32:64, :]
    dk = jnp.zeros((32, 2048), F32)
    dv = jnp.zeros((32, 2048), F32)
    outs = []
    for n in range(256 // QB):
        q = pl.ds(n * QB, QB)
        qt = xt[row, 64:96, q]
        dot = xt[row, 96:128, q]
        s = mm(qt, kt, TN) * scale
        s = s + bias[q, :].astype(F32)
        e = jnp.exp(s - jnp.max(s, axis=1, keepdims=True))
        soft = e * (1.0 / jnp.sum(e, axis=1, keepdims=True))
        half = soft.astype(BF16)
        gs = mm(dot, vt, TN)
        gs = soft * (gs - jnp.sum(soft * gs, axis=1, keepdims=True))
        gh = gs.astype(BF16)
        db[q, :] += gs
        att = mm(vt, half, NT)
        dq = mm(kt, gh, NT) * scale
        outs.append(jnp.concatenate([att, dq.astype(BF16).astype(F32)], axis=0))
        dk = dk + mm(qt, gh)
        dv = dv + mm(dot, half)
    dkv[row, 0:32, :] = (dk * scale).astype(dkv.dtype)
    dkv[row, 32:64, :] = dv.astype(dkv.dtype)
    return jnp.concatenate(outs, axis=1)


TN = (((0,), (0,)), ((), ()))
NT = (((1,), (1,)), ((), ()))


def mm(a, b, dims=(((1,), (0,)), ((), ()))):
    return lax.dot_general(a, b, dims, preferred_element_type=F32)


def halves(a):
    hi = a.astype(BF16)
    return hi, (a - hi.astype(F32)).astype(BF16)


class Fan:
    def __init__(self, p, send, recv):
        self.p, self.send, self.recv = p, send, recv

    def members(self, stage, src, dst):
        return self.all(stage, src, dst, self.p.h, self.p.member)

    def blocks(self, stage, src, dst):
        return self.all(stage, src, dst, self.p.g, self.p.block)

    def all(self, stage, src, dst, me, device):
        copies = []
        for k in ORDER:
            n = (me + k) % 8
            c = remote(src(n), dst(k), self.send.at[stage, k - 1], self.recv.at[stage, k - 1], device(n))
            c.start()
            copies.append(c)
        return copies

    def partner(self, stage, src, dst):
        c = remote(src, dst, self.send.at[stage, 0], self.recv.at[stage, 0], self.p.partner())
        c.start()
        return [c]


def finish(copies):
    for c in copies:
        c.wait()


class Reduce:
    def __init__(self, p, w, o, bufs, sems):
        self.p, self.w, self.o = p, w, o
        self.b0, self.a0, self.b1, self.a1 = bufs
        self.fan = Fan(p, *sems)
        self.n = w.shape[1] // 8
        self.lanes = pl.ds(aligned(p.core, 128), 128)
        self.copies = []

    def rows(self, h):
        return pl.ds(aligned(h, self.n), self.n)

    def pair(self):
        self.copies = self.fan.partner(0, self.w.at[1 - self.p.core], self.b0)

    def member(self):
        finish(self.copies)
        self.a0[...] = self.w[self.p.core] + self.b0[...]
        self.copies = self.fan.members(1, lambda h: self.a0.at[self.rows(h)], lambda k: self.b1.at[k - 1])

    def block(self):
        finish(self.copies)
        total = self.a0[self.rows(self.p.h)]
        for k in range(7):
            total = total + self.b1[k]
        self.a1[self.p.g] = total
        piece = self.a1.at[self.p.g]
        self.copies = self.fan.blocks(2, lambda g: piece, lambda k: piece)

    def back_member(self):
        finish(self.copies)
        self.o[self.rows(self.p.h), self.lanes] = sum_of(self.a1)
        piece = self.o.at[self.rows(self.p.h), self.lanes]
        self.copies = self.fan.members(3, lambda h: piece, lambda k: piece)

    def back_pair(self):
        finish(self.copies)
        piece = self.o.at[:, self.lanes]
        self.copies = self.fan.partner(4, piece, piece)

    def done(self):
        finish(self.copies)
        self.copies = []


def only(value, n, i):
    row = lax.broadcasted_iota(jnp.int32, value.shape, 0) % n
    return jnp.where(row == i, value, jnp.zeros_like(value))


def spread(pbt):
    return jnp.broadcast_to(pbt.astype(F32)[:, None, :], (8, 16, 128)).reshape(128, 128)


def main_kernel(
    hom_in, slope_in, gain_in, wq_in, wk_in, wv_in, wg_in, wo_in, pbt_in, pair_hbm,
    align, bo, oa, ob, ex_out,
    sc, sm,
):
    p = Place()
    z_lo, r4 = p.spot(p.h)
    toks = pl.ds(aligned(r4, 64), 64)
    here = pl.ds(aligned(p.g, 256), 256)
    cols = pl.ds(aligned(p.seq, 512), 512)
    per = 8 // CHUNKS
    xr, xt, kv, bias, db, dkv, parts = (sc[n] for n in ("xr", "xt", "kv", "bias", "db", "dkv", "parts"))
    rows_buf, local = sc["rows"], sm["local"]

    greet(
        [p.member((p.h + k) % 8) for k in range(1, 8)]
        + [p.block((p.g + k) % 8) for k in range(1, 8)]
        + [p.partner()]
    )
    loads = {}
    names = ("hom", "gain", "wk", "wv", "slope", "wo", "wg", "wq", "pbt")
    for n, (name, src) in enumerate(
        zip(names, (hom_in, gain_in, wk_in, wv_in, slope_in, wo_in, wg_in, wq_in, pbt_in))
    ):
        loads[name] = pltpu.make_async_copy(src, sc[name], sm["in"].at[n])
        loads[name].start()

    def stream(n):
        return pltpu.make_async_copy(pair_hbm.at[pl.ds(n * 16, 16)], rows_buf.at[n % 2], sm["hbm"].at[n % 2])

    stream(0).start()
    stream(1).start()
    hom, gain, wk, wv, slope, wo, wg, wq, pbt = (sc[n] for n in names)

    loads["hom"].wait()
    loads["gain"].wait()
    x = jnp.transpose(hom[...].astype(F32))
    centered = x - jnp.mean(x, axis=0, keepdims=True)
    inv = lax.rsqrt(jnp.mean(centered * centered, axis=0, keepdims=True) + 1e-05)
    hat = centered * inv
    scale_t = jnp.transpose(jnp.broadcast_to(gain[...], (256, 256)))
    normed = (hat * scale_t).astype(BF16)
    t_ref = sc["t"]
    loads["wk"].wait()
    loads["wv"].wait()
    for n, w in enumerate((wk, wv)):
        t_ref[:, n * 32 : n * 32 + 32, :] = mm(w[...], normed, TN).astype(BF16).reshape(8, 32, 256)
    pl.semaphore_wait(pltpu.get_barrier_semaphore(), 15)
    fan = Fan(p, sm["send"], sm["recv"])

    moved = fan.members(0, lambda h: t_ref.at[h, 0:64], lambda k: xr.at[z_lo, r4, 0:64])
    own_t = pltpu.make_async_copy(t_ref.at[p.h, 0:64], xr.at[z_lo, r4, 0:64], local.at[0])
    own_t.start()
    sc["hat"][...] = hat
    sc["scale"][...] = scale_t
    sc["inv"][...] = jnp.broadcast_to(inv, (8, 256))
    sc["normed"][...] = normed
    for name in ("slope", "wo", "wg", "wq", "pbt"):
        loads[name].wait()
    t_ref[:, 64:96, :] = mm(wq[...], normed, TN).astype(BF16).reshape(8, 32, 256)
    gate = jax.nn.sigmoid(mm(wg[...], normed, TN))
    grad_gated = mm(wo[...], slope[...], NT)
    sc["gate"][...] = gate
    sc["gg"][...] = grad_gated
    t_ref[:, 96:128, :] = (grad_gated * gate).astype(BF16).reshape(8, 32, 256)
    moved_q = fan.members(12, lambda h: t_ref.at[h, 64:128], lambda k: xr.at[z_lo, r4, 64:128])
    own_q = pltpu.make_async_copy(t_ref.at[p.h, 64:128], xr.at[z_lo, r4, 64:128], local.at[3])
    own_q.start()

    b_ref, mask = sc["b"], sc["mask"]
    base = spread(pbt[...])
    for i in range(16):
        mask[i] = only(base, 16, i).astype(BF16)
    for n in range(4):
        stream(n).wait()
        out = mm(mask[0], rows_buf[n % 2, 0], NT)
        for i in range(1, 16):
            out = out + mm(mask[i], rows_buf[n % 2, i], NT)
        b_ref[:, n * 16 : (n + 1) * 16, :] = out.astype(BF16).reshape(8, 16, 512)
        if n + 2 < 4:
            stream(n + 2).start()
    biases = fan.members(1, lambda h: b_ref.at[h], lambda k: bias.at[toks, cols])
    own_b = pltpu.make_async_copy(b_ref.at[p.h], bias.at[toks, cols], local.at[1])
    own_b.start()
    normed_all = sc["xn"]
    moved_n = fan.members(13, lambda h: sc["normed"], lambda k: normed_all.at[z_lo, r4])
    own_n = pltpu.make_async_copy(sc["normed"], normed_all.at[z_lo, r4], local.at[3])

    def by_row(lo):
        for z in range(2):
            for pp in range(2):
                for i in range(2):
                    lane = pp * 128 + i * 64
                    xt[z * 4 + pp * 2 + i, lo : lo + 64] = jnp.concatenate(
                        [xr[z, r, lo : lo + 64, lane : lane + 64] for r in range(4)], axis=1
                    )

    own_t.wait()
    finish(moved)
    by_row(0)

    def keys(c, k):
        rows = pl.ds(c * per, per)
        return remote(
            xt.at[rows, 0:64], kv.at[rows, :, here], sm["ks"].at[c, k - 1], sm["kr"].at[c, k - 1],
            p.block((p.g + k) % 8),
        )

    def partial(c, k):
        rows = pl.ds(c * per, per)
        g = (p.g + k) % 8
        return remote(
            dkv.at[rows, :, pl.ds(aligned(g, 256), 256)],
            parts.at[k - 1, rows],
            sm["es"].at[c, k - 1],
            sm["er"].at[c, k - 1],
            p.block(g),
        )

    for c in range(CHUNKS):
        for k in ORDER:
            keys(c, k).start()
    own_k = pltpu.make_async_copy(xt.at[:, 0:64], kv.at[:, :, here], local.at[2])
    own_k.start()
    db[...] = jnp.zeros_like(db)
    own_q.wait()
    own_n.start()
    finish(moved_q)
    by_row(64)
    own_k.wait()
    own_b.wait()
    finish(biases)
    moved = []
    for b in range(2):
        part = bias.at[:, pl.ds(aligned(b * 2 + p.core, 512), 512)]
        moved += fan.partner(2 + b, part, part)
    finish(moved)

    ya, yd = sc["ya"], sc["yd"]

    def by_member(outs, dst, c):
        pieces = []
        for r in range(4):
            lane = slice(r * 64, r * 64 + 64)
            pieces.append(jnp.concatenate([outs[0][:, lane], outs[1][:, lane]], axis=1))
            dst[c, r] = pieces[r]
        return pieces

    ta, td, other, mine = sc["ta"], sc["td"], sc["other"], sc["mine"]

    def give(stage, src, dst, k, z):
        h = (p.h + k) % 8
        return remote(
            src.at[pl.ds(z * 2, 2), p.spot(h)[1]], dst.at[p.h],
            sm["send"].at[stage, k - 1], sm["recv"].at[stage, k - 1], p.member(h),
        )

    def keep(n, src, dst):
        return pltpu.make_async_copy(src.at[pl.ds(z_lo * 2, 2), r4], dst.at[p.h], local.at[n])

    def give_half(stage, n, src, dst, z):
        @pl.when(z_lo == z)
        def _():
            for k in (4, 2, 6):
                give(stage, src, dst, k, z).start()
            keep(n, src, dst).start()

        @pl.when(z_lo != z)
        def _():
            for k in (3, 5, 1, 7):
                give(stage, src, dst, k, z).start()

    def taken(stage, n, src, dst):
        keep(n, src, dst).wait()
        for k in ORDER:
            give(stage, src, dst, k, 0).wait()

    def step(c, carry):
        for k in ORDER:
            keys(c, k).wait_recv()
        outs = []
        for i in range(per):
            outs.append(row_backward(xt, kv, bias, db, dkv, c * per + i))
        for k in ORDER:
            partial(c, k).start()
        by_member(outs, ya, c)
        for z in range(2):

            @pl.when(c == 2 * z + 1)
            def _():
                give_half(6, 0, ya, ta, z)

        return carry

    lax.fori_loop(0, CHUNKS, step, 0)

    stream(0).start()
    stream(1).start()
    pair = []
    for b in range(2):
        pair += fan.partner(4 + b, db.at[:, pl.ds(aligned(b * 2 + 1 - p.core, 512), 512)], other.at[b])
    own_n.wait()
    finish(moved_n)
    dw = sc["dw"]
    dw[...] = jnp.zeros_like(dw)

    def total(c, carry):
        for k in ORDER:
            partial(c, k).wait_recv()
        outs = []
        for i in range(per):
            row = c * per + i
            t = dkv[row, :, here].astype(F32)
            for k in range(7):
                t = t + parts[k, row].astype(F32)
            outs.append(t)
        grad = jnp.concatenate([dw[0], dw[1]], axis=1)
        lanes = pl.ds(aligned(c % 2, 128), 128)
        for r, piece in enumerate(by_member(outs, yd, c)):
            hi, lo = halves(piece)
            n = normed_all[c // 2, r, :, lanes]
            grad = grad + mm(hi, n, NT) + mm(lo, n, NT)
        dw[0] = grad[:, :128]
        dw[1] = grad[:, 128:]
        return carry

    lax.fori_loop(0, 2, total, 0)
    give_half(8, 2, yd, td, 0)
    for b in range(2):
        pair[b].wait()
        mine[b] = (db[:, pl.ds(aligned(b * 2 + p.core, 512), 512)] + other[b]).astype(BF16)

    def assemble(src, part):
        rows = slice(part * 32, part * 32 + 32)
        return jnp.concatenate([src[:, pp, rows, :].reshape(256, 128) for pp in range(2)], axis=1)

    taken(6, 0, ya, ta)
    attended = assemble(ta, 0)
    dq = assemble(ta, 1).astype(BF16)
    gate = sc["gate"][...]
    gated = (gate * attended).astype(BF16)
    grad_gate = (sc["gg"][...] * attended * gate * (1.0 - gate)).astype(BF16)
    sc["dq"][...] = dq
    sc["dg"][...] = grad_gate
    normed = sc["normed"][...]
    wa = sc["wa"]

    def put(dst, n, value):
        for i in range(2):
            dst[i, n * 256 : n * 256 + 256, :] = value[:, i * 128 : i * 128 + 128]

    put(wa, 0, mm(normed, dq, NT))
    put(wa, 1, mm(normed, grad_gate, NT))
    put(wa, 2, mm(gated, slope[...]))
    first = Reduce(p, wa, oa, [sc[n] for n in ("a_b0", "a_a0", "a_b1", "a_a1")], (sm["as"], sm["ar"]))
    first.pair()
    lax.fori_loop(2, 3, total, 0)
    first.member()

    def bias_of(h):
        z, r = p.spot(h)
        return mine.at[z, pl.ds(aligned(r, 64), 64)]

    bias_back = fan.members(7, bias_of, lambda k: bo.at[p.h])
    own_m = pltpu.make_async_copy(bias_of(p.h), bo.at[p.h], local.at[1])
    own_m.start()

    lax.fori_loop(3, 4, total, 0)
    dw_o, dws = sc["dw_o"], sc["dws"]
    weights = fan.partner(14, dw.at[1 - p.core], dw_o)
    give_half(8, 2, yd, td, 1)
    grad_normed = mm(wq[...], sc["dq"][...]) + mm(wg[...], sc["dg"][...])
    finish(weights)
    dws[p.g] = dw[p.core] + dw_o[...]
    weights = fan.blocks(15, lambda g: dws.at[p.g], lambda k: dws.at[p.g])
    first.block()

    own_m.wait()
    finish(bias_back)
    grad_bias = jnp.zeros((128, 128), F32)
    for n in range(4):
        stream(n).wait()
        part = bo[:, n * 16 : (n + 1) * 16, :].reshape(128, 512)
        for i in range(16):
            grad_bias = grad_bias + mm(only(part, 16, i), rows_buf[n % 2, i])
        if n + 2 < 4:
            stream(n + 2).start()
    ex, ex_own, exm, exb = sc["ex"], sc["ex_own"], sc["exm"], sc["exb"]
    ex[0:8, :] = jnp.sum(grad_bias.reshape(8, 16, 128), axis=1)
    finish(weights)
    ob[p.core, p.h] = sum_of(dws)
    piece = ob.at[p.core, p.h]
    weights = fan.members(16, lambda h: piece, lambda k: piece)

    taken(8, 2, yd, td)
    dk_hi, dk_lo = halves(assemble(td, 0))
    dv_hi, dv_lo = halves(assemble(td, 1))
    grad_normed = grad_normed + mm(wk[...], dk_hi) + mm(wk[...], dk_lo) + mm(wv[...], dv_hi) + mm(wv[...], dv_lo)
    hat = sc["hat"][...]
    by_gain = jnp.sum(jnp.transpose(grad_normed * hat), axis=0, keepdims=True)
    ex[8:16, :] = jnp.concatenate([by_gain[:, :128], by_gain[:, 128:], jnp.zeros((6, 128), F32)], axis=0)
    extra = fan.partner(9, ex, ex_own)
    first.back_member()
    finish(extra)
    exm[p.h] = ex[...] + ex_own[...]
    extra = fan.members(10, lambda h: exm.at[p.h], lambda k: exm.at[p.h])

    scaled = grad_normed * sc["scale"][...]
    m1 = jnp.mean(scaled, axis=0, keepdims=True)
    m2 = jnp.mean(scaled * hat, axis=0, keepdims=True)
    align[...] = jnp.transpose(sc["inv"][0:1, :] * (scaled - m1 - hat * m2)).astype(BF16)

    finish(extra)
    exb[p.g] = sum_of(exm)
    extra = fan.blocks(11, lambda g: exb.at[p.g], lambda k: exb.at[p.g])
    finish(weights)
    weights = fan.partner(17, ob.at[p.core], ob.at[p.core])
    first.back_pair()
    finish(extra)
    ex_out[0:16, :] = sum_of(exb)
    ex_out[16:24, :] = pbt[...].astype(F32)
    finish(weights)
    first.done()

    def drain(c, carry):
        for k in ORDER:
            keys(c, k).wait_send()
            partial(c, k).wait_send()
        return carry

    lax.fori_loop(0, CHUNKS, drain, 0)


def sum_of(ref):
    total = ref[0]
    for n in range(1, 8):
        total = total + ref[n]
    return total


def main(hom, slope, gain, wq, wk, wv, wg, wo, pbt, pair_rows):
    dma = pltpu.SemaphoreType.DMA
    vmem = pltpu.VMEM

    def reduce_bufs(name, rows):
        return {
            name + "_b0": vmem((rows, 128), F32),
            name + "_a0": vmem((rows, 128), F32),
            name + "_b1": vmem((7, rows // 8, 128), F32),
            name + "_a1": vmem((8, rows // 8, 128), F32),
        }

    square = vmem((256, 256), F32)
    square_half = vmem((256, 256), BF16)
    scratch = {
        "rows": vmem((2, 16, 512, 128), BF16),
        "mask": vmem((16, 128, 128), BF16),
        "hom": square_half, "slope": square_half, "gain": vmem((1, 256), F32), "pbt": vmem((8, 128), BF16),
        "wq": square_half, "wk": square_half, "wv": square_half, "wg": square_half, "wo": square_half,
        "hat": square, "scale": square, "inv": vmem((8, 256), F32), "gate": square, "gg": square,
        "normed": square_half, "dq": square_half, "dg": square_half,
        "t": vmem((8, 128, 256), BF16),
        "b": vmem((8, 64, 512), BF16),
        "xr": vmem((2, 4, 128, 256), BF16),
        "xt": vmem((8, 128, 256), BF16),
        "kv": vmem((8, 64, 2048), BF16),
        "bias": vmem((256, 2048), BF16),
        "db": vmem((256, 2048), F32),
        "dkv": vmem((8, 64, 2048), BF16),
        "parts": vmem((7, 8, 64, 256), BF16),
        "ya": vmem((4, 4, 64, 128), F32),
        "yd": vmem((4, 4, 64, 128), F32),
        "ta": vmem((8, 2, 64, 128), F32),
        "td": vmem((8, 2, 64, 128), F32),
        "mine": vmem((2, 256, 512), BF16),
        "other": vmem((2, 256, 512), F32),
        "wa": vmem((2, 768, 128), F32),
        "xn": vmem((2, 4, 256, 256), BF16),
        "dw": vmem((2, 64, 128), F32), "dw_o": vmem((64, 128), F32), "dws": vmem((8, 64, 128), F32),
        "ex": vmem((16, 128), F32), "ex_own": vmem((16, 128), F32),
        "exm": vmem((8, 16, 128), F32), "exb": vmem((8, 16, 128), F32),
        **reduce_bufs("a", 768),
    }
    sems = {
        "hbm": dma((2,)), "local": dma((4,)), "in": dma((9,)),
        "send": dma((18, 7)), "recv": dma((18, 7)),
        "ks": dma((CHUNKS, 7)), "kr": dma((CHUNKS, 7)),
        "es": dma((CHUNKS, 7)), "er": dma((CHUNKS, 7)),
        "as": dma((5, 7)), "ar": dma((5, 7)),
    }
    return pl.pallas_call(
        main_kernel,
        out_shape=(
            jax.ShapeDtypeStruct((256, 256), BF16),
            jax.ShapeDtypeStruct((8, 64, 512), BF16),
            jax.ShapeDtypeStruct((768, 256), F32),
            jax.ShapeDtypeStruct((2, 8, 64, 128), F32),
            jax.ShapeDtypeStruct((24, 128), F32),
        ),
        in_specs=[HB] * 10,
        out_specs=(VM,) * 5,
        scratch_shapes=[scratch, sems],
        compiler_params=params(0),
        name="main",
    )(*[pltpu.with_memory_space_constraint(a, pltpu.HBM) for a in (hom, slope, gain, wq, wk, wv, wg, wo, pbt, pair_rows)])


def tail_kernel(bo, align, oa, ob, ex, pair, align_out, q, k, v, g, o, gain, bias, base, kv, sem):
    n = pl.program_id(0)
    moves = [(align, align_out), (ex.at[8:10], gain), (ex.at[0:8], bias)]
    moves += [(oa.at[0:256], q), (oa.at[256:512], g), (oa.at[512:768], o), (kv.at[0], k), (kv.at[1], v)]
    copies = [pltpu.make_async_copy(a, b, sem.at[i]) for i, (a, b) in enumerate(moves)]

    @pl.when(n == 0)
    def _():
        for i in range(2):
            for half in range(2):
                part = ob[half, :, i * 32 : i * 32 + 32, :].reshape(256, 128)
                kv[i, half * 128 : half * 128 + 128, :] = jnp.transpose(part)
        for c in copies:
            c.start()
        spreaded = spread(ex[16:24, :])
        for i in range(16):
            base[:, i * 128 : i * 128 + 128] = only(spreaded, 16, i).astype(BF16)

    part = jnp.transpose(bo[:, pl.ds(pl.multiple_of(n * 16, 16), 16), :].reshape(128, 512))
    for i in range(8):
        out = mm(part, base[:, i * 256 : i * 256 + 256]).astype(BF16)
        pair[2 * i] = out[:, :128]
        pair[2 * i + 1] = out[:, 128:]

    @pl.when(n == 3)
    def _():
        for c in copies:
            c.wait()


def tail(bo, align, oa, ob, ex):
    square = jax.ShapeDtypeStruct((256, 256), F32)
    return pl.pallas_call(
        tail_kernel,
        grid=(4,),
        out_shape=(
            jax.ShapeDtypeStruct((64, 512, 128), BF16),
            jax.ShapeDtypeStruct((256, 256), BF16),
            square, square, square, square, square,
            jax.ShapeDtypeStruct((2, 128), F32),
            jax.ShapeDtypeStruct((8, 128), F32),
        ),
        in_specs=[VM] * 5,
        out_specs=(pl.BlockSpec((16, 512, 128), lambda n: (n, 0, 0)),) + (HB,) * 8,
        scratch_shapes=[pltpu.VMEM((128, 2048), BF16), pltpu.VMEM((2, 256, 256), F32), pltpu.SemaphoreType.DMA((8,))],
        compiler_params=pltpu.CompilerParams(vmem_limit_bytes=32 * 1024 * 1024),
        name="tail",
    )(bo, align, oa, ob, ex)


def body(
    homolog_embedding,
    pair_input_rows,
    incoming_slope,
    rescale_factor,
    probe_weights,
    lookup_weights,
    content_weights,
    sigmoid_weights,
    final_projection,
    pair_bias_matrix,
):
    rows, toks, width = homolog_embedding.shape
    align, db_own, oa, ob, extra = main(
        homolog_embedding.reshape(-1, width),
        incoming_slope.reshape(-1, width),
        rescale_factor.reshape(1, width),
        probe_weights,
        lookup_weights,
        content_weights,
        sigmoid_weights,
        final_projection,
        pair_bias_matrix.T,
        pair_input_rows,
    )
    pair_grad, align, grad_q, grad_k, grad_v, grad_g, grad_o, gain, bias = tail(
        db_own, align, oa, ob, extra
    )
    return (
        align.reshape(rows, toks, width),
        pair_grad,
        gain.reshape(width),
        grad_q,
        grad_k,
        grad_v,
        grad_g,
        grad_o,
        bias.T,
    )


def solution(mesh):
    in_specs = (
        P("seq", "res", None),
        P("res", "seq", None),
        P("seq", "res", None),
        P(),
        P(),
        P(),
        P(),
        P(),
        P(),
        P(),
    )
    out_specs = (P("seq", "res", None), P("res", "seq", None), P(), P(), P(), P(), P(), P(), P())
    return jax.shard_map(body, mesh=mesh, in_specs=in_specs, out_specs=out_specs, check_vma=False)
```

```python
import functools
import math

import jax
import jax.numpy as jnp
from jax import lax
from jax.experimental import pallas as pl
from jax.experimental.pallas import tpu as pltpu
from jax.sharding import PartitionSpec as P

MESH = pl.DeviceIdType.MESH
F32 = jnp.float32
BF16 = jnp.bfloat16
VM = pl.BlockSpec(memory_space=pltpu.VMEM)
HB = pl.BlockSpec(memory_space=pltpu.HBM)


class Place:
    def __init__(self):
        seq = lax.axis_index("seq")
        res = lax.axis_index("res")
        self.seq, self.res = seq, res
        self.z_lo, self.core = seq // 2, seq % 2
        self.g, self.z_hi = res // 4, res % 2
        self.x_hi = self.g % 2
        x_lo = (res // 2) % 2
        self.h = ((x_lo + self.x_hi) % 2) * 4 + self.z_hi * 2 + self.z_lo

    def spot(self, h):
        return h % 2, ((h // 4 + self.x_hi) % 2) * 2 + (h // 2) % 2

    def member(self, h):
        z_lo, r4 = self.spot(h)
        return (z_lo * 2 + self.core, self.g * 4 + r4)

    def block(self, g):
        return (self.seq, g * 4 + ((self.h // 4 + g % 2) % 2) * 2 + self.z_hi)

    def partner(self):
        return (self.z_lo * 2 + 1 - self.core, self.res)


def greet(devices):
    barrier = pltpu.get_barrier_semaphore()
    for device in devices:
        pl.semaphore_signal(barrier, inc=1, device_id=device, device_id_type=MESH)


def remote(src, dst, send, recv, device):
    return pltpu.make_async_remote_copy(
        src_ref=src, dst_ref=dst, send_sem=send, recv_sem=recv, device_id=device, device_id_type=MESH
    )


def params(collective_id):
    return pltpu.CompilerParams(
        collective_id=collective_id, has_side_effects=True, vmem_limit_bytes=48 * 1024 * 1024
    )


def aligned(x, n):
    return pl.multiple_of(x * n, n)


ORDER = (4, 3, 5, 2, 6, 1, 7)
CHUNKS = 4
QB = 128


ORDER = (4, 3, 5, 2, 6, 1, 7)
CHUNKS = 4
QB = 128


def row_backward(xt, kv, bias, db, dkv, row):
    scale = 1.0 / math.sqrt(32)
    kt = kv[row, 0:32, :]
    vt = kv[row, 32:64, :]
    dk = jnp.zeros((32, 2048), F32)
    dv = jnp.zeros((32, 2048), F32)
    outs = []
    for n in range(256 // QB):
        q = pl.ds(n * QB, QB)
        qt = xt[row, 64:96, q]
        dot = xt[row, 96:128, q]
        s = mm(qt, kt, TN) * scale
        s = s + bias[q, :].astype(F32)
        e = jnp.exp(s - jnp.max(s, axis=1, keepdims=True))
        soft = e * (1.0 / jnp.sum(e, axis=1, keepdims=True))
        half = soft.astype(BF16)
        gs = mm(dot, vt, TN)
        gs = soft * (gs - jnp.sum(soft * gs, axis=1, keepdims=True))
        gh = gs.astype(BF16)
        db[q, :] += gs
        att = mm(vt, half, NT)
        dq = mm(kt, gh, NT) * scale
        outs.append(jnp.concatenate([att, dq.astype(BF16).astype(F32)], axis=0))
        dk = dk + mm(qt, gh)
        dv = dv + mm(dot, half)
    dkv[row, 0:32, :] = (dk * scale).astype(dkv.dtype)
    dkv[row, 32:64, :] = dv.astype(dkv.dtype)
    return jnp.concatenate(outs, axis=1)


TN = (((0,), (0,)), ((), ()))
NT = (((1,), (1,)), ((), ()))


def mm(a, b, dims=(((1,), (0,)), ((), ()))):
    return lax.dot_general(a, b, dims, preferred_element_type=F32)


def halves(a):
    hi = a.astype(BF16)
    return hi, (a - hi.astype(F32)).astype(BF16)


class Fan:
    def __init__(self, p, send, recv):
        self.p, self.send, self.recv = p, send, recv

    def members(self, stage, src, dst):
        return self.all(stage, src, dst, self.p.h, self.p.member)

    def blocks(self, stage, src, dst):
        return self.all(stage, src, dst, self.p.g, self.p.block)

    def all(self, stage, src, dst, me, device):
        copies = []
        for k in ORDER:
            n = (me + k) % 8
            c = remote(src(n), dst(k), self.send.at[stage, k - 1], self.recv.at[stage, k - 1], device(n))
            c.start()
            copies.append(c)
        return copies

    def partner(self, stage, src, dst):
        c = remote(src, dst, self.send.at[stage, 0], self.recv.at[stage, 0], self.p.partner())
        c.start()
        return [c]


def finish(copies):
    for c in copies:
        c.wait()


class Gather:
    def __init__(self, p, fan, stage, w, other, slots, o):
        self.p, self.fan, self.stage = p, fan, stage
        self.w, self.other, self.slots, self.o = w, other, slots, o
        self.copies = []

    def pair(self):
        self.copies = self.fan.partner(self.stage, self.w.at[1 - self.p.core], self.other)

    def block(self):
        finish(self.copies)
        self.slots[self.p.g] = self.w[self.p.core] + self.other[...]
        piece = self.slots.at[self.p.g]
        self.copies = self.fan.blocks(self.stage + 1, lambda g: piece, lambda k: piece)

    def member(self):
        finish(self.copies)
        self.o[self.p.core, self.p.h] = sum_of(self.slots)
        piece = self.o.at[self.p.core, self.p.h]
        self.copies = self.fan.members(self.stage + 2, lambda h: piece, lambda k: piece)

    def back_pair(self):
        finish(self.copies)
        piece = self.o.at[self.p.core]
        self.copies = self.fan.partner(self.stage + 3, piece, piece)

    def done(self):
        finish(self.copies)


def only(value, n, i):
    row = lax.broadcasted_iota(jnp.int32, value.shape, 0) % n
    return jnp.where(row == i, value, jnp.zeros_like(value))


def spread(pbt):
    return jnp.broadcast_to(pbt.astype(F32)[:, None, :], (8, 16, 128)).reshape(128, 128)


def main_kernel(
    hom_in, slope_in, gain_in, wq_in, wk_in, wv_in, wg_in, wo_in, pbt_in, pair_hbm,
    align, bo, oa, ob, ex_out,
    sc, sm,
):
    p = Place()
    z_lo, r4 = p.spot(p.h)
    toks = pl.ds(aligned(r4, 64), 64)
    here = pl.ds(aligned(p.g, 256), 256)
    cols = pl.ds(aligned(p.seq, 512), 512)
    per = 8 // CHUNKS
    xr, xt, kv, bias, db, dkv, parts = (sc[n] for n in ("xr", "xt", "kv", "bias", "db", "dkv", "parts"))
    rows_buf, local = sc["rows"], sm["local"]

    greet(
        [p.member((p.h + k) % 8) for k in range(1, 8)]
        + [p.block((p.g + k) % 8) for k in range(1, 8)]
        + [p.partner()]
    )
    loads = {}
    names = ("hom", "gain", "wk", "wv", "slope", "wo", "wg", "wq", "pbt")
    for n, (name, src) in enumerate(
        zip(names, (hom_in, gain_in, wk_in, wv_in, slope_in, wo_in, wg_in, wq_in, pbt_in))
    ):
        loads[name] = pltpu.make_async_copy(src, sc[name], sm["in"].at[n])
        loads[name].start()

    def stream(n):
        return pltpu.make_async_copy(pair_hbm.at[pl.ds(n * 16, 16)], rows_buf.at[n % 2], sm["hbm"].at[n % 2])

    stream(0).start()
    stream(1).start()
    hom, gain, wk, wv, slope, wo, wg, wq, pbt = (sc[n] for n in names)

    loads["hom"].wait()
    loads["gain"].wait()
    x = jnp.transpose(hom[...].astype(F32))
    centered = x - jnp.mean(x, axis=0, keepdims=True)
    inv = lax.rsqrt(jnp.mean(centered * centered, axis=0, keepdims=True) + 1e-05)
    hat = centered * inv
    scale_t = jnp.transpose(jnp.broadcast_to(gain[...], (256, 256)))
    normed = (hat * scale_t).astype(BF16)
    t_ref = sc["t"]
    loads["wk"].wait()
    loads["wv"].wait()
    for n, w in enumerate((wk, wv)):
        t_ref[:, n * 32 : n * 32 + 32, :] = mm(w[...], normed, TN).astype(BF16).reshape(8, 32, 256)
    pl.semaphore_wait(pltpu.get_barrier_semaphore(), 15)
    fan = Fan(p, sm["send"], sm["recv"])

    moved = fan.members(0, lambda h: t_ref.at[h, 0:64], lambda k: xr.at[z_lo, r4, 0:64])
    own_t = pltpu.make_async_copy(t_ref.at[p.h, 0:64], xr.at[z_lo, r4, 0:64], local.at[0])
    own_t.start()
    sc["hat"][...] = hat
    sc["scale"][...] = scale_t
    sc["inv"][...] = jnp.broadcast_to(inv, (8, 256))
    sc["normed"][...] = normed
    for name in ("slope", "wo", "wg", "wq", "pbt"):
        loads[name].wait()
    t_ref[:, 64:96, :] = mm(wq[...], normed, TN).astype(BF16).reshape(8, 32, 256)
    gate = jax.nn.sigmoid(mm(wg[...], normed, TN))
    grad_gated = mm(wo[...], slope[...], NT)
    gates = sc["gates"]
    gates[:, 0:32, :] = gate.reshape(8, 32, 256)
    gates[:, 32:64, :] = grad_gated.reshape(8, 32, 256)
    t_ref[:, 96:128, :] = (grad_gated * gate).astype(BF16).reshape(8, 32, 256)
    moved_q = fan.members(12, lambda h: t_ref.at[h, 64:128], lambda k: xr.at[z_lo, r4, 64:128])
    own_q = pltpu.make_async_copy(t_ref.at[p.h, 64:128], xr.at[z_lo, r4, 64:128], local.at[3])
    own_q.start()

    b_ref, mask = sc["b"], sc["mask"]
    base = spread(pbt[...])
    for i in range(16):
        mask[i] = only(base, 16, i).astype(BF16)
    for n in range(4):
        stream(n).wait()
        out = mm(mask[0], rows_buf[n % 2, 0], NT)
        for i in range(1, 16):
            out = out + mm(mask[i], rows_buf[n % 2, i], NT)
        b_ref[:, n * 16 : (n + 1) * 16, :] = out.astype(BF16).reshape(8, 16, 512)
        if n + 2 < 4:
            stream(n + 2).start()
    biases = fan.members(1, lambda h: b_ref.at[h], lambda k: bias.at[toks, cols])
    own_b = pltpu.make_async_copy(b_ref.at[p.h], bias.at[toks, cols], local.at[1])
    own_b.start()
    gates_all, normed_all, slope_all = sc["xg"], sc["xn"], sc["xs"]
    moved_g = fan.members(10, lambda h: gates.at[h], lambda k: gates_all.at[z_lo, r4])
    own_g = pltpu.make_async_copy(gates.at[p.h], gates_all.at[z_lo, r4], local.at[4])
    own_g.start()
    moved_n = fan.members(13, lambda h: sc["normed"], lambda k: normed_all.at[z_lo, r4])
    moved_n += fan.members(11, lambda h: slope, lambda k: slope_all.at[z_lo, r4])
    own_n = pltpu.make_async_copy(sc["normed"], normed_all.at[z_lo, r4], local.at[3])
    own_s = pltpu.make_async_copy(slope, slope_all.at[z_lo, r4], local.at[5])
    own_s.start()

    def by_row(lo):
        for z in range(2):
            for pp in range(2):
                for i in range(2):
                    lane = pp * 128 + i * 64
                    xt[z * 4 + pp * 2 + i, lo : lo + 64] = jnp.concatenate(
                        [xr[z, r, lo : lo + 64, lane : lane + 64] for r in range(4)], axis=1
                    )

    own_t.wait()
    finish(moved)
    by_row(0)

    def keys(c, k):
        rows = pl.ds(c * per, per)
        return remote(
            xt.at[rows, 0:64], kv.at[rows, :, here], sm["ks"].at[c, k - 1], sm["kr"].at[c, k - 1],
            p.block((p.g + k) % 8),
        )

    def partial(c, k):
        rows = pl.ds(c * per, per)
        g = (p.g + k) % 8
        return remote(
            dkv.at[rows, :, pl.ds(aligned(g, 256), 256)],
            parts.at[k - 1, rows],
            sm["es"].at[c, k - 1],
            sm["er"].at[c, k - 1],
            p.block(g),
        )

    for c in range(CHUNKS):
        for k in ORDER:
            keys(c, k).start()
    own_k = pltpu.make_async_copy(xt.at[:, 0:64], kv.at[:, :, here], local.at[2])
    own_k.start()
    db[...] = jnp.zeros_like(db)
    own_q.wait()
    own_n.start()
    finish(moved_q)
    by_row(64)
    own_k.wait()
    own_b.wait()
    finish(biases)
    moved = []
    for b in range(2):
        part = bias.at[:, pl.ds(aligned(b * 2 + p.core, 512), 512)]
        moved += fan.partner(2 + b, part, part)
    finish(moved)

    ya, yd = sc["ya"], sc["yd"]

    def by_member(outs, dst, c):
        pieces = []
        for r in range(4):
            lane = slice(r * 64, r * 64 + 64)
            pieces.append(jnp.concatenate([outs[0][:, lane], outs[1][:, lane]], axis=1))
            if dst is not None:
                dst[c, r] = pieces[r]
        return pieces

    ta, td, other, mine, gated = sc["ta"], sc["td"], sc["other"], sc["mine"], sc["gated"]

    def give(stage, src, dst, k, z):
        h = (p.h + k) % 8
        return remote(
            src.at[pl.ds(z * 2, 2), p.spot(h)[1]], dst.at[p.h],
            sm["send"].at[stage, k - 1], sm["recv"].at[stage, k - 1], p.member(h),
        )

    def keep(n, src, dst):
        return pltpu.make_async_copy(src.at[pl.ds(z_lo * 2, 2), r4], dst.at[p.h], local.at[n])

    def give_half(stage, n, src, dst, z):
        @pl.when(z_lo == z)
        def _():
            for k in (4, 2, 6):
                give(stage, src, dst, k, z).start()
            keep(n, src, dst).start()

        @pl.when(z_lo != z)
        def _():
            for k in (3, 5, 1, 7):
                give(stage, src, dst, k, z).start()

    def taken(stage, n, src, dst):
        keep(n, src, dst).wait()
        for k in ORDER:
            give(stage, src, dst, k, 0).wait()

    def step(c, carry):
        for k in ORDER:
            keys(c, k).wait_recv()
        outs = []
        for i in range(per):
            outs.append(row_backward(xt, kv, bias, db, dkv, c * per + i))
        for k in ORDER:
            partial(c, k).start()
        @pl.when(c == 0)
        def _():
            own_g.wait()
            finish(moved_g)

        lanes = pl.ds(aligned(c % 2, 128), 128)
        for r, piece in enumerate(by_member(outs, None, c)):
            attended = piece[0:32]
            gate = gates_all[c // 2, r, 0:32, lanes]
            grad_gated = gates_all[c // 2, r, 32:64, lanes]
            ya[c, r, 0:32] = piece[32:64].astype(BF16)
            ya[c, r, 32:64] = (grad_gated * attended * gate * (1.0 - gate)).astype(BF16)
            gated[c, r] = (gate * attended).astype(BF16)
        for z in range(2):

            @pl.when(c == 2 * z + 1)
            def _():
                give_half(6, 0, ya, ta, z)

        return carry

    lax.fori_loop(0, CHUNKS, step, 0)

    stream(0).start()
    stream(1).start()
    pair = []
    for b in range(2):
        pair += fan.partner(4 + b, db.at[:, pl.ds(aligned(b * 2 + 1 - p.core, 512), 512)], other.at[b])
    own_n.wait()
    own_s.wait()
    finish(moved_n)
    dw, de = sc["dw"], sc["de"]
    dw[...] = jnp.zeros_like(dw)

    grad_qg = jnp.zeros((64, 256), F32)
    grad_o = jnp.zeros((32, 256), F32)
    for c in range(CHUNKS):
        lane = slice(c % 2 * 128, c % 2 * 128 + 128)
        for r in range(4):
            grad_qg = grad_qg + mm(ya[c, r], normed_all[c // 2, r, :, lane], NT)
            grad_o = grad_o + mm(gated[c, r], slope_all[c // 2, r, lane, :])
    for half in range(2):
        lane = slice(half * 128, half * 128 + 128)
        de[half, 0:64] = grad_qg[:, lane]
        de[half, 64:96] = grad_o[:, lane]
    first = Gather(p, fan, 18, de, sc["de_o"], sc["des"], oa)
    last = Gather(p, fan, 14, dw, sc["dw_o"], sc["dws"], ob)
    first.pair()

    def total(c, carry):
        for k in ORDER:
            partial(c, k).wait_recv()
        outs = []
        for i in range(per):
            row = c * per + i
            t = dkv[row, :, here].astype(F32)
            for k in range(7):
                t = t + parts[k, row].astype(F32)
            outs.append(t)
        grad = jnp.concatenate([dw[0], dw[1]], axis=1)
        lanes = pl.ds(aligned(c % 2, 128), 128)
        for r, piece in enumerate(by_member(outs, yd, c)):
            hi, lo = halves(piece)
            n = normed_all[c // 2, r, :, lanes]
            grad = grad + mm(hi, n, NT) + mm(lo, n, NT)
        dw[0] = grad[:, :128]
        dw[1] = grad[:, 128:]
        return carry

    lax.fori_loop(0, 2, total, 0)
    give_half(8, 2, yd, td, 0)
    for b in range(2):
        pair[b].wait()
        mine[b] = (db[:, pl.ds(aligned(b * 2 + p.core, 512), 512)] + other[b]).astype(BF16)

    def assemble(src, part):
        rows = slice(part * 32, part * 32 + 32)
        return jnp.concatenate([src[:, pp, rows, :].reshape(256, 128) for pp in range(2)], axis=1)

    first.block()
    lax.fori_loop(2, 3, total, 0)

    def bias_of(h):
        z, r = p.spot(h)
        return mine.at[z, pl.ds(aligned(r, 64), 64)]

    bias_back = fan.members(7, bias_of, lambda k: bo.at[p.h])
    own_m = pltpu.make_async_copy(bias_of(p.h), bo.at[p.h], local.at[1])
    own_m.start()

    lax.fori_loop(3, 4, total, 0)
    last.pair()
    give_half(8, 2, yd, td, 1)
    taken(6, 0, ya, ta)
    grad_normed = mm(wq[...], assemble(ta, 0)) + mm(wg[...], assemble(ta, 1))
    last.block()

    own_m.wait()
    finish(bias_back)
    grad_bias = jnp.zeros((128, 128), F32)
    for n in range(4):
        stream(n).wait()
        part = bo[:, n * 16 : (n + 1) * 16, :].reshape(128, 512)
        for i in range(16):
            grad_bias = grad_bias + mm(only(part, 16, i), rows_buf[n % 2, i])
        if n + 2 < 4:
            stream(n + 2).start()
    ex, ex_own, exm, exb = sc["ex"], sc["ex_own"], sc["exm"], sc["exb"]
    ex[0:8, :] = jnp.sum(grad_bias.reshape(8, 16, 128), axis=1)
    first.member()
    last.member()

    taken(8, 2, yd, td)
    dk_hi, dk_lo = halves(assemble(td, 0))
    dv_hi, dv_lo = halves(assemble(td, 1))
    grad_normed = grad_normed + mm(wk[...], dk_hi) + mm(wk[...], dk_lo) + mm(wv[...], dv_hi) + mm(wv[...], dv_lo)
    hat = sc["hat"][...]
    by_gain = jnp.sum(jnp.transpose(grad_normed * hat), axis=0, keepdims=True)
    ex[8:16, :] = jnp.concatenate([by_gain[:, :128], by_gain[:, 128:], jnp.zeros((6, 128), F32)], axis=0)
    extra = fan.partner(9, ex, ex_own)
    finish(extra)
    exm[p.h] = ex[...] + ex_own[...]
    extra = fan.members(22, lambda h: exm.at[p.h], lambda k: exm.at[p.h])

    scaled = grad_normed * sc["scale"][...]
    m1 = jnp.mean(scaled, axis=0, keepdims=True)
    m2 = jnp.mean(scaled * hat, axis=0, keepdims=True)
    align[...] = jnp.transpose(sc["inv"][0:1, :] * (scaled - m1 - hat * m2)).astype(BF16)

    finish(extra)
    exb[p.g] = sum_of(exm)
    extra = fan.blocks(23, lambda g: exb.at[p.g], lambda k: exb.at[p.g])
    first.back_pair()
    last.back_pair()
    finish(extra)
    ex_out[0:16, :] = sum_of(exb)
    ex_out[16:24, :] = pbt[...].astype(F32)
    first.done()
    last.done()

    def drain(c, carry):
        for k in ORDER:
            keys(c, k).wait_send()
            partial(c, k).wait_send()
        return carry

    lax.fori_loop(0, CHUNKS, drain, 0)


def sum_of(ref):
    total = ref[0]
    for n in range(1, 8):
        total = total + ref[n]
    return total


def main(hom, slope, gain, wq, wk, wv, wg, wo, pbt, pair_rows):
    dma = pltpu.SemaphoreType.DMA
    vmem = pltpu.VMEM

    square = vmem((256, 256), F32)
    square_half = vmem((256, 256), BF16)
    scratch = {
        "rows": vmem((2, 16, 512, 128), BF16),
        "mask": vmem((16, 128, 128), BF16),
        "hom": square_half, "slope": square_half, "gain": vmem((1, 256), F32), "pbt": vmem((8, 128), BF16),
        "wq": square_half, "wk": square_half, "wv": square_half, "wg": square_half, "wo": square_half,
        "hat": square, "scale": square, "inv": vmem((8, 256), F32), "gates": vmem((8, 64, 256), F32),
        "normed": square_half,
        "t": vmem((8, 128, 256), BF16),
        "b": vmem((8, 64, 512), BF16),
        "xr": vmem((2, 4, 128, 256), BF16),
        "xt": vmem((8, 128, 256), BF16),
        "kv": vmem((8, 64, 2048), BF16),
        "bias": vmem((256, 2048), BF16),
        "db": vmem((256, 2048), F32),
        "dkv": vmem((8, 64, 2048), BF16),
        "parts": vmem((7, 8, 64, 256), BF16),
        "ya": vmem((4, 4, 64, 128), BF16),
        "gated": vmem((4, 4, 32, 128), BF16),
        "yd": vmem((4, 4, 64, 128), F32),
        "ta": vmem((8, 2, 64, 128), BF16),
        "td": vmem((8, 2, 64, 128), F32),
        "mine": vmem((2, 256, 512), BF16),
        "other": vmem((2, 256, 512), F32),
        "xn": vmem((2, 4, 256, 256), BF16), "xs": vmem((2, 4, 256, 256), BF16), "xg": vmem((2, 4, 64, 256), F32),
        "de": vmem((2, 96, 128), F32), "de_o": vmem((96, 128), F32), "des": vmem((8, 96, 128), F32),
        "dw": vmem((2, 64, 128), F32), "dw_o": vmem((64, 128), F32), "dws": vmem((8, 64, 128), F32),
        "ex": vmem((16, 128), F32), "ex_own": vmem((16, 128), F32),
        "exm": vmem((8, 16, 128), F32), "exb": vmem((8, 16, 128), F32),
    }
    sems = {
        "hbm": dma((2,)), "local": dma((6,)), "in": dma((9,)),
        "send": dma((24, 7)), "recv": dma((24, 7)),
        "ks": dma((CHUNKS, 7)), "kr": dma((CHUNKS, 7)),
        "es": dma((CHUNKS, 7)), "er": dma((CHUNKS, 7)),
    }
    return pl.pallas_call(
        main_kernel,
        out_shape=(
            jax.ShapeDtypeStruct((256, 256), BF16),
            jax.ShapeDtypeStruct((8, 64, 512), BF16),
            jax.ShapeDtypeStruct((2, 8, 96, 128), F32),
            jax.ShapeDtypeStruct((2, 8, 64, 128), F32),
            jax.ShapeDtypeStruct((24, 128), F32),
        ),
        in_specs=[HB] * 10,
        out_specs=(VM,) * 5,
        scratch_shapes=[scratch, sems],
        compiler_params=params(0),
        name="main",
    )(*[pltpu.with_memory_space_constraint(a, pltpu.HBM) for a in (hom, slope, gain, wq, wk, wv, wg, wo, pbt, pair_rows)])


def tail_kernel(bo, align, oa, ob, ex, pair, align_out, q, k, v, g, o, gain, bias, base, kv, sem):
    n = pl.program_id(0)
    moves = [(align, align_out), (ex.at[8:10], gain), (ex.at[0:8], bias)]
    moves += [(kv.at[i], w) for i, w in enumerate((k, v, q, g, o))]
    copies = [pltpu.make_async_copy(a, b, sem.at[i]) for i, (a, b) in enumerate(moves)]

    @pl.when(n == 0)
    def _():
        for half in range(2):
            lane = slice(half * 128, half * 128 + 128)
            for i, (ref, row) in enumerate(((ob, 0), (ob, 32), (oa, 0), (oa, 32))):
                kv[i, lane, :] = jnp.transpose(ref[half, :, row : row + 32, :].reshape(256, 128))
            kv[4, :, lane] = oa[half, :, 64:96, :].reshape(256, 128)
        for c in copies:
            c.start()
        spreaded = spread(ex[16:24, :])
        for i in range(16):
            base[:, i * 128 : i * 128 + 128] = only(spreaded, 16, i).astype(BF16)

    part = jnp.transpose(bo[:, pl.ds(pl.multiple_of(n * 16, 16), 16), :].reshape(128, 512))
    for i in range(8):
        out = mm(part, base[:, i * 256 : i * 256 + 256]).astype(BF16)
        pair[2 * i] = out[:, :128]
        pair[2 * i + 1] = out[:, 128:]

    @pl.when(n == 3)
    def _():
        for c in copies:
            c.wait()


def tail(bo, align, oa, ob, ex):
    square = jax.ShapeDtypeStruct((256, 256), F32)
    return pl.pallas_call(
        tail_kernel,
        grid=(4,),
        out_shape=(
            jax.ShapeDtypeStruct((64, 512, 128), BF16),
            jax.ShapeDtypeStruct((256, 256), BF16),
            square, square, square, square, square,
            jax.ShapeDtypeStruct((2, 128), F32),
            jax.ShapeDtypeStruct((8, 128), F32),
        ),
        in_specs=[VM] * 5,
        out_specs=(pl.BlockSpec((16, 512, 128), lambda n: (n, 0, 0)),) + (HB,) * 8,
        scratch_shapes=[pltpu.VMEM((128, 2048), BF16), pltpu.VMEM((5, 256, 256), F32), pltpu.SemaphoreType.DMA((8,))],
        compiler_params=pltpu.CompilerParams(vmem_limit_bytes=32 * 1024 * 1024),
        name="tail",
    )(bo, align, oa, ob, ex)


def body(
    homolog_embedding,
    pair_input_rows,
    incoming_slope,
    rescale_factor,
    probe_weights,
    lookup_weights,
    content_weights,
    sigmoid_weights,
    final_projection,
    pair_bias_matrix,
):
    rows, toks, width = homolog_embedding.shape
    align, db_own, oa, ob, extra = main(
        homolog_embedding.reshape(-1, width),
        incoming_slope.reshape(-1, width),
        rescale_factor.reshape(1, width),
        probe_weights,
        lookup_weights,
        content_weights,
        sigmoid_weights,
        final_projection,
        pair_bias_matrix.T,
        pair_input_rows,
    )
    pair_grad, align, grad_q, grad_k, grad_v, grad_g, grad_o, gain, bias = tail(
        db_own, align, oa, ob, extra
    )
    return (
        align.reshape(rows, toks, width),
        pair_grad,
        gain.reshape(width),
        grad_q,
        grad_k,
        grad_v,
        grad_g,
        grad_o,
        bias.T,
    )


def solution(mesh):
    in_specs = (
        P("seq", "res", None),
        P("res", "seq", None),
        P("seq", "res", None),
        P(),
        P(),
        P(),
        P(),
        P(),
        P(),
        P(),
    )
    out_specs = (P("seq", "res", None), P("res", "seq", None), P(), P(), P(), P(), P(), P(), P())
    return jax.shard_map(body, mesh=mesh, in_specs=in_specs, out_specs=out_specs, check_vma=False)
```

```python
import functools
import math

import jax
import jax.numpy as jnp
from jax import lax
from jax.experimental import pallas as pl
from jax.experimental.pallas import tpu as pltpu
from jax.sharding import PartitionSpec as P

MESH = pl.DeviceIdType.MESH
F32 = jnp.float32
BF16 = jnp.bfloat16
VM = pl.BlockSpec(memory_space=pltpu.VMEM)
HB = pl.BlockSpec(memory_space=pltpu.HBM)


class Place:
    def __init__(self):
        seq = lax.axis_index("seq")
        res = lax.axis_index("res")
        self.seq, self.res = seq, res
        self.z_lo, self.core = seq // 2, seq % 2
        self.g, self.z_hi = res // 4, res % 2
        self.x_hi = self.g % 2
        x_lo = (res // 2) % 2
        self.h = ((x_lo + self.x_hi) % 2) * 4 + self.z_hi * 2 + self.z_lo

    def spot(self, h):
        return h % 2, ((h // 4 + self.x_hi) % 2) * 2 + (h // 2) % 2

    def member(self, h):
        z_lo, r4 = self.spot(h)
        return (z_lo * 2 + self.core, self.g * 4 + r4)

    def block(self, g):
        return (self.seq, g * 4 + ((self.h // 4 + g % 2) % 2) * 2 + self.z_hi)

    def partner(self):
        return (self.z_lo * 2 + 1 - self.core, self.res)


def greet(devices):
    barrier = pltpu.get_barrier_semaphore()
    for device in devices:
        pl.semaphore_signal(barrier, inc=1, device_id=device, device_id_type=MESH)


def remote(src, dst, send, recv, device):
    return pltpu.make_async_remote_copy(
        src_ref=src, dst_ref=dst, send_sem=send, recv_sem=recv, device_id=device, device_id_type=MESH
    )


def params(collective_id):
    return pltpu.CompilerParams(
        collective_id=collective_id, has_side_effects=True, vmem_limit_bytes=48 * 1024 * 1024
    )


def aligned(x, n):
    return pl.multiple_of(x * n, n)


ORDER = (4, 3, 5, 2, 6, 1, 7)
CHUNKS = 4
QB = 128


ORDER = (4, 3, 5, 2, 6, 1, 7)
CHUNKS = 4
QB = 128


def row_backward(xt, kv, bias, db, dkv, row):
    scale = 1.0 / math.sqrt(32)
    kt = kv[row, 0:32, :]
    vt = kv[row, 32:64, :]
    dk = jnp.zeros((32, 2048), F32)
    dv = jnp.zeros((32, 2048), F32)
    outs = []
    for n in range(256 // QB):
        q = pl.ds(n * QB, QB)
        qt = xt[row, 64:96, q]
        dot = xt[row, 96:128, q]
        s = mm(qt, kt, TN) * scale
        s = s + bias[q, :].astype(F32)
        e = jnp.exp(s - jnp.max(s, axis=1, keepdims=True))
        soft = e * (1.0 / jnp.sum(e, axis=1, keepdims=True))
        half = soft.astype(BF16)
        gs = mm(dot, vt, TN)
        gs = soft * (gs - jnp.sum(soft * gs, axis=1, keepdims=True))
        gh = gs.astype(BF16)
        db[q, :] += gs
        att = mm(vt, half, NT)
        dq = mm(kt, gh, NT) * scale
        outs.append(jnp.concatenate([att, dq.astype(BF16).astype(F32)], axis=0))
        dk = dk + mm(qt, gh)
        dv = dv + mm(dot, half)
    dkv[row, 0:32, :] = (dk * scale).astype(dkv.dtype)
    dkv[row, 32:64, :] = dv.astype(dkv.dtype)
    return jnp.concatenate(outs, axis=1)


TN = (((0,), (0,)), ((), ()))
NT = (((1,), (1,)), ((), ()))


def mm(a, b, dims=(((1,), (0,)), ((), ()))):
    return lax.dot_general(a, b, dims, preferred_element_type=F32)


def halves(a):
    hi = a.astype(BF16)
    return hi, (a - hi.astype(F32)).astype(BF16)


class Fan:
    def __init__(self, p, send, recv):
        self.p, self.send, self.recv = p, send, recv

    def members(self, stage, src, dst):
        return self.all(stage, src, dst, self.p.h, self.p.member)

    def blocks(self, stage, src, dst):
        return self.all(stage, src, dst, self.p.g, self.p.block)

    def all(self, stage, src, dst, me, device):
        copies = []
        for k in ORDER:
            n = (me + k) % 8
            c = remote(src(n), dst(k), self.send.at[stage, k - 1], self.recv.at[stage, k - 1], device(n))
            c.start()
            copies.append(c)
        return copies

    def partner(self, stage, src, dst):
        c = remote(src, dst, self.send.at[stage, 0], self.recv.at[stage, 0], self.p.partner())
        c.start()
        return [c]


def finish(copies):
    for c in copies:
        c.wait()


class Gather:
    def __init__(self, p, fan, stage, w, other, slots, o):
        self.p, self.fan, self.stage = p, fan, stage
        self.w, self.other, self.slots, self.o = w, other, slots, o
        self.copies = []

    def pair(self):
        self.copies = self.fan.partner(self.stage, self.w.at[1 - self.p.core], self.other)

    def block(self):
        finish(self.copies)
        self.slots[self.p.g] = self.w[self.p.core] + self.other[...]
        piece = self.slots.at[self.p.g]
        self.copies = self.fan.blocks(self.stage + 1, lambda g: piece, lambda k: piece)

    def member(self):
        finish(self.copies)
        self.o[self.p.core, self.p.h] = sum_of(self.slots)
        piece = self.o.at[self.p.core, self.p.h]
        self.copies = self.fan.members(self.stage + 2, lambda h: piece, lambda k: piece)

    def back_pair(self):
        finish(self.copies)
        piece = self.o.at[self.p.core]
        self.copies = self.fan.partner(self.stage + 3, piece, piece)

    def done(self):
        finish(self.copies)


def only(value, n, i):
    row = lax.broadcasted_iota(jnp.int32, value.shape, 0) % n
    return jnp.where(row == i, value, jnp.zeros_like(value))


def spread(pbt):
    return jnp.broadcast_to(pbt.astype(F32)[:, None, :], (8, 16, 128)).reshape(128, 128)


def main_kernel(
    hom_in, slope_in, gain_in, wq_in, wk_in, wv_in, wg_in, wo_in, pbt_in, pair_hbm,
    align, bo, oa, ob, ex_out,
    sc, sm,
):
    p = Place()
    z_lo, r4 = p.spot(p.h)
    toks = pl.ds(aligned(r4, 64), 64)
    here = pl.ds(aligned(p.g, 256), 256)
    cols = pl.ds(aligned(p.seq, 512), 512)
    per = 8 // CHUNKS
    xr, xt, kv, bias, db, dkv, parts = (sc[n] for n in ("xr", "xt", "kv", "bias", "db", "dkv", "parts"))
    rows_buf, local = sc["rows"], sm["local"]

    greet(
        [p.member((p.h + k) % 8) for k in range(1, 8)]
        + [p.block((p.g + k) % 8) for k in range(1, 8)]
        + [p.partner()]
    )
    loads = {}
    names = ("hom", "gain", "wk", "wv", "slope", "wo", "wg", "wq", "pbt")
    for n, (name, src) in enumerate(
        zip(names, (hom_in, gain_in, wk_in, wv_in, slope_in, wo_in, wg_in, wq_in, pbt_in))
    ):
        loads[name] = pltpu.make_async_copy(src, sc[name], sm["in"].at[n])
        loads[name].start()

    def stream(n):
        return pltpu.make_async_copy(pair_hbm.at[pl.ds(n * 16, 16)], rows_buf.at[n % 2], sm["hbm"].at[n % 2])

    stream(0).start()
    stream(1).start()
    hom, gain, wk, wv, slope, wo, wg, wq, pbt = (sc[n] for n in names)

    loads["hom"].wait()
    loads["gain"].wait()
    x = jnp.transpose(hom[...].astype(F32))
    centered = x - jnp.mean(x, axis=0, keepdims=True)
    inv = lax.rsqrt(jnp.mean(centered * centered, axis=0, keepdims=True) + 1e-05)
    hat = centered * inv
    scale_t = jnp.transpose(jnp.broadcast_to(gain[...], (256, 256)))
    normed = (hat * scale_t).astype(BF16)
    t_ref = sc["t"]
    loads["wk"].wait()
    loads["wv"].wait()
    for n, w in enumerate((wk, wv)):
        t_ref[:, n * 32 : n * 32 + 32, :] = mm(w[...], normed, TN).astype(BF16).reshape(8, 32, 256)
    pl.semaphore_wait(pltpu.get_barrier_semaphore(), 15)
    fan = Fan(p, sm["send"], sm["recv"])

    moved = fan.members(0, lambda h: t_ref.at[h, 0:64], lambda k: xr.at[z_lo, r4, 0:64])
    own_t = pltpu.make_async_copy(t_ref.at[p.h, 0:64], xr.at[z_lo, r4, 0:64], local.at[0])
    own_t.start()
    sc["hat"][...] = hat
    sc["scale"][...] = scale_t
    sc["inv"][...] = jnp.broadcast_to(inv, (8, 256))
    sc["normed"][...] = normed
    for name in ("slope", "wo", "wg", "wq", "pbt"):
        loads[name].wait()
    t_ref[:, 64:96, :] = mm(wq[...], normed, TN).astype(BF16).reshape(8, 32, 256)
    gate = jax.nn.sigmoid(mm(wg[...], normed, TN))
    grad_gated = mm(wo[...], slope[...], NT)
    gates = sc["gates"]
    gates[:, 0:32, :] = gate.reshape(8, 32, 256)
    gates[:, 32:64, :] = grad_gated.reshape(8, 32, 256)
    t_ref[:, 96:128, :] = (grad_gated * gate).astype(BF16).reshape(8, 32, 256)
    moved_q = fan.members(12, lambda h: t_ref.at[h, 64:128], lambda k: xr.at[z_lo, r4, 64:128])
    own_q = pltpu.make_async_copy(t_ref.at[p.h, 64:128], xr.at[z_lo, r4, 64:128], local.at[3])
    own_q.start()

    b_ref, mask = sc["b"], sc["mask"]
    base = spread(pbt[...])
    for i in range(16):
        mask[i] = only(base, 16, i).astype(BF16)
    for n in range(4):
        stream(n).wait()
        out = mm(mask[0], rows_buf[n % 2, 0], NT)
        for i in range(1, 16):
            out = out + mm(mask[i], rows_buf[n % 2, i], NT)
        b_ref[:, n * 16 : (n + 1) * 16, :] = out.astype(BF16).reshape(8, 16, 512)
        if n + 2 < 4:
            stream(n + 2).start()
    biases = fan.members(1, lambda h: b_ref.at[h], lambda k: bias.at[toks, cols])
    own_b = pltpu.make_async_copy(b_ref.at[p.h], bias.at[toks, cols], local.at[1])
    own_b.start()
    gates_all, normed_all, slope_all = sc["xg"], sc["xn"], sc["xs"]
    moved_g = fan.members(10, lambda h: gates.at[h], lambda k: gates_all.at[z_lo, r4])
    own_g = pltpu.make_async_copy(gates.at[p.h], gates_all.at[z_lo, r4], local.at[4])
    own_g.start()
    moved_n = fan.members(13, lambda h: sc["normed"], lambda k: normed_all.at[z_lo, r4])
    moved_s = fan.members(11, lambda h: slope, lambda k: slope_all.at[z_lo, r4])
    own_n = pltpu.make_async_copy(sc["normed"], normed_all.at[z_lo, r4], local.at[3])
    own_s = pltpu.make_async_copy(slope, slope_all.at[z_lo, r4], local.at[5])
    own_s.start()

    def by_row(lo):
        for z in range(2):
            for pp in range(2):
                for i in range(2):
                    lane = pp * 128 + i * 64
                    xt[z * 4 + pp * 2 + i, lo : lo + 64] = jnp.concatenate(
                        [xr[z, r, lo : lo + 64, lane : lane + 64] for r in range(4)], axis=1
                    )

    own_t.wait()
    finish(moved)
    by_row(0)

    def keys(c, k):
        rows = pl.ds(c * per, per)
        return remote(
            xt.at[rows, 0:64], kv.at[rows, :, here], sm["ks"].at[c, k - 1], sm["kr"].at[c, k - 1],
            p.block((p.g + k) % 8),
        )

    def partial(c, k):
        rows = pl.ds(c * per, per)
        g = (p.g + k) % 8
        return remote(
            dkv.at[rows, :, pl.ds(aligned(g, 256), 256)],
            parts.at[k - 1, rows],
            sm["es"].at[c, k - 1],
            sm["er"].at[c, k - 1],
            p.block(g),
        )

    for c in range(CHUNKS):
        for k in ORDER:
            keys(c, k).start()
    own_k = pltpu.make_async_copy(xt.at[:, 0:64], kv.at[:, :, here], local.at[2])
    own_k.start()
    db[...] = jnp.zeros_like(db)
    own_q.wait()
    own_n.start()
    finish(moved_q)
    by_row(64)
    own_k.wait()
    own_b.wait()
    finish(biases)
    moved = []
    for b in range(2):
        part = bias.at[:, pl.ds(aligned(b * 2 + p.core, 512), 512)]
        moved += fan.partner(2 + b, part, part)
    finish(moved)

    ya, yd = sc["ya"], sc["yd"]

    def by_member(outs, dst, c):
        pieces = []
        for r in range(4):
            lane = slice(r * 64, r * 64 + 64)
            pieces.append(jnp.concatenate([outs[0][:, lane], outs[1][:, lane]], axis=1))
            if dst is not None:
                dst[c, r] = pieces[r]
        return pieces

    ta, td, other, mine, gated = sc["ta"], sc["td"], sc["other"], sc["mine"], sc["gated"]

    def give(stage, src, dst, k, z):
        h = (p.h + k) % 8
        return remote(
            src.at[pl.ds(z * 2, 2), p.spot(h)[1]], dst.at[p.h],
            sm["send"].at[stage, k - 1], sm["recv"].at[stage, k - 1], p.member(h),
        )

    def keep(n, src, dst):
        return pltpu.make_async_copy(src.at[pl.ds(z_lo * 2, 2), r4], dst.at[p.h], local.at[n])

    def give_half(stage, n, src, dst, z):
        @pl.when(z_lo == z)
        def _():
            for k in (4, 2, 6):
                give(stage, src, dst, k, z).start()
            keep(n, src, dst).start()

        @pl.when(z_lo != z)
        def _():
            for k in (3, 5, 1, 7):
                give(stage, src, dst, k, z).start()

    def taken(stage, n, src, dst):
        keep(n, src, dst).wait()
        for k in ORDER:
            give(stage, src, dst, k, 0).wait()

    def step(c, carry):
        for k in ORDER:
            keys(c, k).wait_recv()
        outs = []
        for i in range(per):
            outs.append(row_backward(xt, kv, bias, db, dkv, c * per + i))
        for k in ORDER:
            partial(c, k).start()
        @pl.when(c == 0)
        def _():
            own_g.wait()
            finish(moved_g)

        lanes = pl.ds(aligned(c % 2, 128), 128)
        for r, piece in enumerate(by_member(outs, None, c)):
            attended = piece[0:32]
            gate = gates_all[c // 2, r, 0:32, lanes]
            grad_gated = gates_all[c // 2, r, 32:64, lanes]
            ya[c, r, 0:32] = piece[32:64].astype(BF16)
            ya[c, r, 32:64] = (grad_gated * attended * gate * (1.0 - gate)).astype(BF16)
            gated[c, r] = (gate * attended).astype(BF16)
        for z in range(2):

            @pl.when(c == 2 * z + 1)
            def _():
                give_half(6, 0, ya, ta, z)

        return carry

    lax.fori_loop(0, CHUNKS, step, 0)

    stream(0).start()
    stream(1).start()
    pair = []
    for b in range(2):
        pair += fan.partner(4 + b, db.at[:, pl.ds(aligned(b * 2 + 1 - p.core, 512), 512)], other.at[b])
    own_n.wait()
    finish(moved_n)
    dw, de = sc["dw"], sc["de"]
    dw[...] = jnp.zeros_like(dw)

    def total(c, carry):
        for k in ORDER:
            partial(c, k).wait_recv()
        outs = []
        for i in range(per):
            row = c * per + i
            t = dkv[row, :, here].astype(F32)
            for k in range(7):
                t = t + parts[k, row].astype(F32)
            outs.append(t)
        grad = jnp.concatenate([dw[0], dw[1]], axis=1)
        lanes = pl.ds(aligned(c % 2, 128), 128)
        for r, piece in enumerate(by_member(outs, yd, c)):
            hi, lo = halves(piece)
            n = normed_all[c // 2, r, :, lanes]
            grad = grad + mm(hi, n, NT) + mm(lo, n, NT)
        dw[0] = grad[:, :128]
        dw[1] = grad[:, 128:]
        return carry

    lax.fori_loop(0, 2, total, 0)
    give_half(8, 2, yd, td, 0)
    for b in range(2):
        pair[b].wait()
        mine[b] = (db[:, pl.ds(aligned(b * 2 + p.core, 512), 512)] + other[b]).astype(BF16)

    def bias_of(h):
        z, r = p.spot(h)
        return mine.at[z, pl.ds(aligned(r, 64), 64)]

    bias_back = fan.members(7, bias_of, lambda k: bo.at[p.h])
    own_m = pltpu.make_async_copy(bias_of(p.h), bo.at[p.h], local.at[1])
    own_m.start()

    def assemble(src, part):
        rows = slice(part * 32, part * 32 + 32)
        return jnp.concatenate([src[:, pp, rows, :].reshape(256, 128) for pp in range(2)], axis=1)

    own_s.wait()
    finish(moved_s)
    grad_qg = jnp.zeros((64, 256), F32)
    grad_o = jnp.zeros((32, 256), F32)
    for c in range(CHUNKS):
        lane = slice(c % 2 * 128, c % 2 * 128 + 128)
        for r in range(4):
            grad_qg = grad_qg + mm(ya[c, r], normed_all[c // 2, r, :, lane], NT)
            grad_o = grad_o + mm(gated[c, r], slope_all[c // 2, r, lane, :])
    for half in range(2):
        lane = slice(half * 128, half * 128 + 128)
        de[half, 0:64] = grad_qg[:, lane]
        de[half, 64:96] = grad_o[:, lane]
    first = Gather(p, fan, 18, de, sc["de_o"], sc["des"], oa)
    last = Gather(p, fan, 14, dw, sc["dw_o"], sc["dws"], ob)
    first.pair()
    first.block()
    lax.fori_loop(2, 3, total, 0)

    lax.fori_loop(3, 4, total, 0)
    last.pair()
    give_half(8, 2, yd, td, 1)
    taken(6, 0, ya, ta)
    grad_normed = mm(wq[...], assemble(ta, 0)) + mm(wg[...], assemble(ta, 1))
    last.block()

    own_m.wait()
    finish(bias_back)
    grad_bias = jnp.zeros((128, 128), F32)
    for n in range(4):
        stream(n).wait()
        part = bo[:, n * 16 : (n + 1) * 16, :].reshape(128, 512)
        for i in range(16):
            grad_bias = grad_bias + mm(only(part, 16, i), rows_buf[n % 2, i])
        if n + 2 < 4:
            stream(n + 2).start()
    ex, ex_own, exm, exb = sc["ex"], sc["ex_own"], sc["exm"], sc["exb"]
    ex[0:8, :] = jnp.sum(grad_bias.reshape(8, 16, 128), axis=1)
    first.member()
    last.member()

    taken(8, 2, yd, td)
    dk_hi, dk_lo = halves(assemble(td, 0))
    dv_hi, dv_lo = halves(assemble(td, 1))
    grad_normed = grad_normed + mm(wk[...], dk_hi) + mm(wk[...], dk_lo) + mm(wv[...], dv_hi) + mm(wv[...], dv_lo)
    hat = sc["hat"][...]
    by_gain = jnp.sum(jnp.transpose(grad_normed * hat), axis=0, keepdims=True)
    ex[8:16, :] = jnp.concatenate([by_gain[:, :128], by_gain[:, 128:], jnp.zeros((6, 128), F32)], axis=0)
    extra = fan.partner(9, ex, ex_own)
    finish(extra)
    exm[p.h] = ex[...] + ex_own[...]
    extra = fan.members(22, lambda h: exm.at[p.h], lambda k: exm.at[p.h])

    scaled = grad_normed * sc["scale"][...]
    m1 = jnp.mean(scaled, axis=0, keepdims=True)
    m2 = jnp.mean(scaled * hat, axis=0, keepdims=True)
    align[...] = jnp.transpose(sc["inv"][0:1, :] * (scaled - m1 - hat * m2)).astype(BF16)

    finish(extra)
    exb[p.g] = sum_of(exm)
    extra = fan.blocks(23, lambda g: exb.at[p.g], lambda k: exb.at[p.g])
    first.back_pair()
    last.back_pair()
    finish(extra)
    ex_out[0:16, :] = sum_of(exb)
    ex_out[16:24, :] = pbt[...].astype(F32)
    first.done()
    last.done()

    def drain(c, carry):
        for k in ORDER:
            keys(c, k).wait_send()
            partial(c, k).wait_send()
        return carry

    lax.fori_loop(0, CHUNKS, drain, 0)


def sum_of(ref):
    total = ref[0]
    for n in range(1, 8):
        total = total + ref[n]
    return total


def main(hom, slope, gain, wq, wk, wv, wg, wo, pbt, pair_rows):
    dma = pltpu.SemaphoreType.DMA
    vmem = pltpu.VMEM

    square = vmem((256, 256), F32)
    square_half = vmem((256, 256), BF16)
    scratch = {
        "rows": vmem((2, 16, 512, 128), BF16),
        "mask": vmem((16, 128, 128), BF16),
        "hom": square_half, "slope": square_half, "gain": vmem((1, 256), F32), "pbt": vmem((8, 128), BF16),
        "wq": square_half, "wk": square_half, "wv": square_half, "wg": square_half, "wo": square_half,
        "hat": square, "scale": square, "inv": vmem((8, 256), F32), "gates": vmem((8, 64, 256), F32),
        "normed": square_half,
        "t": vmem((8, 128, 256), BF16),
        "b": vmem((8, 64, 512), BF16),
        "xr": vmem((2, 4, 128, 256), BF16),
        "xt": vmem((8, 128, 256), BF16),
        "kv": vmem((8, 64, 2048), BF16),
        "bias": vmem((256, 2048), BF16),
        "db": vmem((256, 2048), F32),
        "dkv": vmem((8, 64, 2048), BF16),
        "parts": vmem((7, 8, 64, 256), BF16),
        "ya": vmem((4, 4, 64, 128), BF16),
        "gated": vmem((4, 4, 32, 128), BF16),
        "yd": vmem((4, 4, 64, 128), F32),
        "ta": vmem((8, 2, 64, 128), BF16),
        "td": vmem((8, 2, 64, 128), F32),
        "mine": vmem((2, 256, 512), BF16),
        "other": vmem((2, 256, 512), F32),
        "xn": vmem((2, 4, 256, 256), BF16), "xs": vmem((2, 4, 256, 256), BF16), "xg": vmem((2, 4, 64, 256), F32),
        "de": vmem((2, 96, 128), F32), "de_o": vmem((96, 128), F32), "des": vmem((8, 96, 128), F32),
        "dw": vmem((2, 64, 128), F32), "dw_o": vmem((64, 128), F32), "dws": vmem((8, 64, 128), F32),
        "ex": vmem((16, 128), F32), "ex_own": vmem((16, 128), F32),
        "exm": vmem((8, 16, 128), F32), "exb": vmem((8, 16, 128), F32),
    }
    sems = {
        "hbm": dma((2,)), "local": dma((6,)), "in": dma((9,)),
        "send": dma((24, 7)), "recv": dma((24, 7)),
        "ks": dma((CHUNKS, 7)), "kr": dma((CHUNKS, 7)),
        "es": dma((CHUNKS, 7)), "er": dma((CHUNKS, 7)),
    }
    return pl.pallas_call(
        main_kernel,
        out_shape=(
            jax.ShapeDtypeStruct((256, 256), BF16),
            jax.ShapeDtypeStruct((8, 64, 512), BF16),
            jax.ShapeDtypeStruct((2, 8, 96, 128), F32),
            jax.ShapeDtypeStruct((2, 8, 64, 128), F32),
            jax.ShapeDtypeStruct((24, 128), F32),
        ),
        in_specs=[HB] * 10,
        out_specs=(VM,) * 5,
        scratch_shapes=[scratch, sems],
        compiler_params=params(0),
        name="main",
    )(*[pltpu.with_memory_space_constraint(a, pltpu.HBM) for a in (hom, slope, gain, wq, wk, wv, wg, wo, pbt, pair_rows)])


def tail_kernel(bo, align, oa, ob, ex, pair, align_out, q, k, v, g, o, gain, bias, base, kv, sem):
    n = pl.program_id(0)
    moves = [(align, align_out), (ex.at[8:10], gain), (ex.at[0:8], bias)]
    moves += [(kv.at[i], w) for i, w in enumerate((k, v, q, g, o))]
    copies = [pltpu.make_async_copy(a, b, sem.at[i]) for i, (a, b) in enumerate(moves)]

    @pl.when(n == 0)
    def _():
        for half in range(2):
            lane = slice(half * 128, half * 128 + 128)
            for i, (ref, row) in enumerate(((ob, 0), (ob, 32), (oa, 0), (oa, 32))):
                kv[i, lane, :] = jnp.transpose(ref[half, :, row : row + 32, :].reshape(256, 128))
            kv[4, :, lane] = oa[half, :, 64:96, :].reshape(256, 128)
        for c in copies:
            c.start()
        spreaded = spread(ex[16:24, :])
        for i in range(16):
            base[i // 8, :, i % 8 * 128 : i % 8 * 128 + 128] = only(spreaded, 16, i).astype(BF16)

    part = jnp.transpose(bo[:, pl.ds(pl.multiple_of(n // 2 * 16, 16), 16), :].reshape(128, 512))
    for i in range(4):
        out = mm(part, base[n % 2, :, i * 256 : i * 256 + 256]).astype(BF16)
        pair[2 * i] = out[:, :128]
        pair[2 * i + 1] = out[:, 128:]

    @pl.when(n == 7)
    def _():
        for c in copies:
            c.wait()


def tail(bo, align, oa, ob, ex):
    square = jax.ShapeDtypeStruct((256, 256), F32)
    return pl.pallas_call(
        tail_kernel,
        grid=(8,),
        out_shape=(
            jax.ShapeDtypeStruct((64, 512, 128), BF16),
            jax.ShapeDtypeStruct((256, 256), BF16),
            square, square, square, square, square,
            jax.ShapeDtypeStruct((2, 128), F32),
            jax.ShapeDtypeStruct((8, 128), F32),
        ),
        in_specs=[VM] * 5,
        out_specs=(pl.BlockSpec((8, 512, 128), lambda n: (n, 0, 0)),) + (HB,) * 8,
        scratch_shapes=[pltpu.VMEM((2, 128, 1024), BF16), pltpu.VMEM((5, 256, 256), F32), pltpu.SemaphoreType.DMA((8,))],
        compiler_params=pltpu.CompilerParams(vmem_limit_bytes=32 * 1024 * 1024),
        name="tail",
    )(bo, align, oa, ob, ex)


def body(
    homolog_embedding,
    pair_input_rows,
    incoming_slope,
    rescale_factor,
    probe_weights,
    lookup_weights,
    content_weights,
    sigmoid_weights,
    final_projection,
    pair_bias_matrix,
):
    rows, toks, width = homolog_embedding.shape
    align, db_own, oa, ob, extra = main(
        homolog_embedding.reshape(-1, width),
        incoming_slope.reshape(-1, width),
        rescale_factor.reshape(1, width),
        probe_weights,
        lookup_weights,
        content_weights,
        sigmoid_weights,
        final_projection,
        pair_bias_matrix.T,
        pair_input_rows,
    )
    pair_grad, align, grad_q, grad_k, grad_v, grad_g, grad_o, gain, bias = tail(
        db_own, align, oa, ob, extra
    )
    return (
        align.reshape(rows, toks, width),
        pair_grad,
        gain.reshape(width),
        grad_q,
        grad_k,
        grad_v,
        grad_g,
        grad_o,
        bias.T,
    )


def solution(mesh):
    in_specs = (
        P("seq", "res", None),
        P("res", "seq", None),
        P("seq", "res", None),
        P(),
        P(),
        P(),
        P(),
        P(),
        P(),
        P(),
    )
    out_specs = (P("seq", "res", None), P("res", "seq", None), P(), P(), P(), P(), P(), P(), P())
    return jax.shard_map(body, mesh=mesh, in_specs=in_specs, out_specs=out_specs, check_vma=False)
```

```python
import functools
import math

import jax
import jax.numpy as jnp
from jax import lax
from jax.experimental import pallas as pl
from jax.experimental.pallas import tpu as pltpu
from jax.sharding import PartitionSpec as P

MESH = pl.DeviceIdType.MESH
F32 = jnp.float32
BF16 = jnp.bfloat16
VM = pl.BlockSpec(memory_space=pltpu.VMEM)
HB = pl.BlockSpec(memory_space=pltpu.HBM)


class Place:
    def __init__(self):
        seq = lax.axis_index("seq")
        res = lax.axis_index("res")
        self.seq, self.res = seq, res
        self.z_lo, self.core = seq // 2, seq % 2
        self.g, self.z_hi = res // 4, res % 2
        self.x_hi = self.g % 2
        x_lo = (res // 2) % 2
        self.h = ((x_lo + self.x_hi) % 2) * 4 + self.z_hi * 2 + self.z_lo

    def spot(self, h):
        return h % 2, ((h // 4 + self.x_hi) % 2) * 2 + (h // 2) % 2

    def member(self, h):
        z_lo, r4 = self.spot(h)
        return (z_lo * 2 + self.core, self.g * 4 + r4)

    def block(self, g):
        return (self.seq, g * 4 + ((self.h // 4 + g % 2) % 2) * 2 + self.z_hi)

    def across(self, g):
        return (self.z_lo * 2 + 1 - self.core, self.block(g)[1])

    def partner(self):
        return (self.z_lo * 2 + 1 - self.core, self.res)


def greet(devices):
    barrier = pltpu.get_barrier_semaphore()
    for device in devices:
        pl.semaphore_signal(barrier, inc=1, device_id=device, device_id_type=MESH)


def remote(src, dst, send, recv, device):
    return pltpu.make_async_remote_copy(
        src_ref=src, dst_ref=dst, send_sem=send, recv_sem=recv, device_id=device, device_id_type=MESH
    )


def params(collective_id):
    return pltpu.CompilerParams(
        collective_id=collective_id, has_side_effects=True, vmem_limit_bytes=48 * 1024 * 1024
    )


def aligned(x, n):
    return pl.multiple_of(x * n, n)


ORDER = (4, 3, 5, 2, 6, 1, 7)
CHUNKS = 4
QB = 128


ORDER = (4, 3, 5, 2, 6, 1, 7)
CHUNKS = 4
QB = 128


def row_backward(xt, kv, bias, db, dkv, row):
    scale = 1.0 / math.sqrt(32)
    kt = kv[row, 0:32, :]
    vt = kv[row, 32:64, :]
    dk = jnp.zeros((32, 2048), F32)
    dv = jnp.zeros((32, 2048), F32)
    outs = []
    for n in range(256 // QB):
        q = pl.ds(n * QB, QB)
        qt = xt[row, 64:96, q]
        dot = xt[row, 96:128, q]
        s = mm(qt, kt, TN) * scale
        s = s + bias[q, :].astype(F32)
        e = jnp.exp(s - jnp.max(s, axis=1, keepdims=True))
        soft = e * (1.0 / jnp.sum(e, axis=1, keepdims=True))
        half = soft.astype(BF16)
        gs = mm(dot, vt, TN)
        gs = soft * (gs - jnp.sum(soft * gs, axis=1, keepdims=True))
        gh = gs.astype(BF16)
        db[q, :] += gs
        att = mm(vt, half, NT)
        dq = mm(kt, gh, NT) * scale
        outs.append(jnp.concatenate([att, dq.astype(BF16).astype(F32)], axis=0))
        dk = dk + mm(qt, gh)
        dv = dv + mm(dot, half)
    dkv[row, 0:32, :] = (dk * scale).astype(dkv.dtype)
    dkv[row, 32:64, :] = dv.astype(dkv.dtype)
    return jnp.concatenate(outs, axis=1)


TN = (((0,), (0,)), ((), ()))
NT = (((1,), (1,)), ((), ()))


def mm(a, b, dims=(((1,), (0,)), ((), ()))):
    return lax.dot_general(a, b, dims, preferred_element_type=F32)


def halves(a):
    hi = a.astype(BF16)
    return hi, (a - hi.astype(F32)).astype(BF16)


class Fan:
    def __init__(self, p, send, recv):
        self.p, self.send, self.recv = p, send, recv

    def members(self, stage, src, dst):
        return self.all(stage, src, dst, self.p.h, self.p.member)

    def blocks(self, stage, src, dst):
        return self.all(stage, src, dst, self.p.g, self.p.block)

    def all(self, stage, src, dst, me, device):
        copies = []
        for k in ORDER:
            n = (me + k) % 8
            c = remote(src(n), dst(k), self.send.at[stage, k - 1], self.recv.at[stage, k - 1], device(n))
            c.start()
            copies.append(c)
        return copies

    def partner(self, stage, src, dst):
        c = remote(src, dst, self.send.at[stage, 0], self.recv.at[stage, 0], self.p.partner())
        c.start()
        return [c]


def finish(copies):
    for c in copies:
        c.wait()


class Gather:
    def __init__(self, p, fan, stage, w, other, slots, o):
        self.p, self.fan, self.stage = p, fan, stage
        self.w, self.other, self.slots, self.o = w, other, slots, o
        self.copies = []

    def pair(self):
        self.copies = self.fan.partner(self.stage, self.w.at[1 - self.p.core], self.other)

    def block(self):
        finish(self.copies)
        self.slots[self.p.g] = self.w[self.p.core] + self.other[...]
        piece = self.slots.at[self.p.g]
        self.copies = self.fan.blocks(self.stage + 1, lambda g: piece, lambda k: piece)

    def member(self):
        finish(self.copies)
        self.o[self.p.core, self.p.h] = sum_of(self.slots)
        piece = self.o.at[self.p.core, self.p.h]
        self.copies = self.fan.members(self.stage + 2, lambda h: piece, lambda k: piece)

    def back_pair(self):
        finish(self.copies)
        piece = self.o.at[self.p.core]
        self.copies = self.fan.partner(self.stage + 3, piece, piece)

    def done(self):
        finish(self.copies)


def only(value, n, i):
    row = lax.broadcasted_iota(jnp.int32, value.shape, 0) % n
    return jnp.where(row == i, value, jnp.zeros_like(value))


def spread(pbt):
    return jnp.broadcast_to(pbt.astype(F32)[:, None, :], (8, 16, 128)).reshape(128, 128)


def main_kernel(
    hom_in, slope_in, gain_in, wq_in, wk_in, wv_in, wg_in, wo_in, pbt_in, pair_hbm,
    align, bo, oa, ob, ex_out,
    sc, sm,
):
    p = Place()
    z_lo, r4 = p.spot(p.h)
    toks = pl.ds(aligned(r4, 64), 64)
    here = pl.ds(aligned(p.g, 256), 256)
    cols = pl.ds(aligned(p.seq, 512), 512)
    per = 8 // CHUNKS
    xr, xt, kv, bias, db, dkv, parts = (sc[n] for n in ("xr", "xt", "kv", "bias", "db", "dkv", "parts"))
    rows_buf, local = sc["rows"], sm["local"]

    greet(
        [p.member((p.h + k) % 8) for k in range(1, 8)]
        + [p.block((p.g + k) % 8) for k in range(1, 8)]
        + [p.across((p.g + k) % 8) for k in range(1, 8)]
        + [p.partner()]
    )
    loads = {}
    names = ("hom", "gain", "wk", "wv", "slope", "wo", "wg", "wq", "pbt")
    for n, (name, src) in enumerate(
        zip(names, (hom_in, gain_in, wk_in, wv_in, slope_in, wo_in, wg_in, wq_in, pbt_in))
    ):
        loads[name] = pltpu.make_async_copy(src, sc[name], sm["in"].at[n])
        loads[name].start()

    def stream(n):
        return pltpu.make_async_copy(pair_hbm.at[pl.ds(n * 16, 16)], rows_buf.at[n % 2], sm["hbm"].at[n % 2])

    stream(0).start()
    stream(1).start()
    hom, gain, wk, wv, slope, wo, wg, wq, pbt = (sc[n] for n in names)

    loads["hom"].wait()
    loads["gain"].wait()
    x = jnp.transpose(hom[...].astype(F32))
    centered = x - jnp.mean(x, axis=0, keepdims=True)
    inv = lax.rsqrt(jnp.mean(centered * centered, axis=0, keepdims=True) + 1e-05)
    hat = centered * inv
    scale_t = jnp.transpose(jnp.broadcast_to(gain[...], (256, 256)))
    normed = (hat * scale_t).astype(BF16)
    t_ref = sc["t"]
    loads["wk"].wait()
    loads["wv"].wait()
    for n, w in enumerate((wk, wv)):
        t_ref[:, n * 32 : n * 32 + 32, :] = mm(w[...], normed, TN).astype(BF16).reshape(8, 32, 256)
    pl.semaphore_wait(pltpu.get_barrier_semaphore(), 22)
    fan = Fan(p, sm["send"], sm["recv"])

    moved = fan.members(0, lambda h: t_ref.at[h, 0:64], lambda k: xr.at[z_lo, r4, 0:64])
    own_t = pltpu.make_async_copy(t_ref.at[p.h, 0:64], xr.at[z_lo, r4, 0:64], local.at[0])
    own_t.start()
    sc["hat"][...] = hat
    sc["scale"][...] = scale_t
    sc["inv"][...] = jnp.broadcast_to(inv, (8, 256))
    sc["normed"][...] = normed
    for name in ("slope", "wo", "wg", "wq", "pbt"):
        loads[name].wait()
    t_ref[:, 64:96, :] = mm(wq[...], normed, TN).astype(BF16).reshape(8, 32, 256)
    gate = jax.nn.sigmoid(mm(wg[...], normed, TN))
    grad_gated = mm(wo[...], slope[...], NT)
    gates = sc["gates"]
    gates[:, 0:32, :] = gate.reshape(8, 32, 256)
    gates[:, 32:64, :] = grad_gated.reshape(8, 32, 256)
    t_ref[:, 96:128, :] = (grad_gated * gate).astype(BF16).reshape(8, 32, 256)
    moved_q = fan.members(12, lambda h: t_ref.at[h, 64:128], lambda k: xr.at[z_lo, r4, 64:128])
    own_q = pltpu.make_async_copy(t_ref.at[p.h, 64:128], xr.at[z_lo, r4, 64:128], local.at[3])
    own_q.start()

    b_ref, mask = sc["b"], sc["mask"]
    base = spread(pbt[...])
    for i in range(16):
        mask[i] = only(base, 16, i).astype(BF16)
    for n in range(4):
        stream(n).wait()
        out = mm(mask[0], rows_buf[n % 2, 0], NT)
        for i in range(1, 16):
            out = out + mm(mask[i], rows_buf[n % 2, i], NT)
        b_ref[:, n * 16 : (n + 1) * 16, :] = out.astype(BF16).reshape(8, 16, 512)
        if n + 2 < 4:
            stream(n + 2).start()
    biases = fan.members(1, lambda h: b_ref.at[h], lambda k: bias.at[toks, cols])
    own_b = pltpu.make_async_copy(b_ref.at[p.h], bias.at[toks, cols], local.at[1])
    own_b.start()
    gates_all, normed_all, slope_all = sc["xg"], sc["xn"], sc["xs"]
    moved_g = fan.members(10, lambda h: gates.at[h], lambda k: gates_all.at[z_lo, r4])
    own_g = pltpu.make_async_copy(gates.at[p.h], gates_all.at[z_lo, r4], local.at[4])
    own_g.start()
    moved_n = fan.members(13, lambda h: sc["normed"], lambda k: normed_all.at[z_lo, r4])
    moved_s = fan.members(11, lambda h: slope, lambda k: slope_all.at[z_lo, r4])
    own_n = pltpu.make_async_copy(sc["normed"], normed_all.at[z_lo, r4], local.at[3])
    own_s = pltpu.make_async_copy(slope, slope_all.at[z_lo, r4], local.at[5])
    own_s.start()

    def by_row(lo):
        for z in range(2):
            for pp in range(2):
                for i in range(2):
                    lane = pp * 128 + i * 64
                    xt[z * 4 + pp * 2 + i, lo : lo + 64] = jnp.concatenate(
                        [xr[z, r, lo : lo + 64, lane : lane + 64] for r in range(4)], axis=1
                    )

    own_t.wait()
    finish(moved)
    by_row(0)

    def keys(row, k):
        return remote(
            xt.at[row, 0:64], kv.at[row, :, here], sm["ks"].at[row, k - 1], sm["kr"].at[row, k - 1],
            p.block((p.g + k) % 8),
        )

    def partial(row, k):
        g = (p.g + k) % 8
        return remote(
            dkv.at[row, :, pl.ds(aligned(g, 256), 256)],
            parts.at[k - 1, row],
            sm["es"].at[row, k - 1],
            sm["er"].at[row, k - 1],
            p.block(g),
        )

    for row in range(8):
        for k in ORDER:
            keys(row, k).start()
    own_k = pltpu.make_async_copy(xt.at[:, 0:64], kv.at[:, :, here], local.at[2])
    own_k.start()
    db[...] = jnp.zeros_like(db)
    own_q.wait()
    own_n.start()
    finish(moved_q)
    by_row(64)
    own_k.wait()
    own_b.wait()
    finish(biases)
    moved = []
    for b in range(2):
        part = bias.at[:, pl.ds(aligned(b * 2 + p.core, 512), 512)]
        moved += fan.partner(2 + b, part, part)
    finish(moved)

    ya, yd = sc["ya"], sc["yd"]

    def by_member(outs, dst, c):
        pieces = []
        for r in range(4):
            lane = slice(r * 64, r * 64 + 64)
            pieces.append(jnp.concatenate([outs[0][:, lane], outs[1][:, lane]], axis=1))
            if dst is not None:
                dst[c, r] = pieces[r]
        return pieces

    ta, td, other, mine, gated = sc["ta"], sc["td"], sc["other"], sc["mine"], sc["gated"]

    def give(stage, src, dst, k, z):
        h = (p.h + k) % 8
        return remote(
            src.at[pl.ds(z * 2, 2), p.spot(h)[1]], dst.at[p.h],
            sm["send"].at[stage, k - 1], sm["recv"].at[stage, k - 1], p.member(h),
        )

    def keep(n, src, dst):
        return pltpu.make_async_copy(src.at[pl.ds(z_lo * 2, 2), r4], dst.at[p.h], local.at[n])

    def give_half(stage, n, src, dst, z):
        @pl.when(z_lo == z)
        def _():
            for k in (4, 2, 6):
                give(stage, src, dst, k, z).start()
            keep(n, src, dst).start()

        @pl.when(z_lo != z)
        def _():
            for k in (3, 5, 1, 7):
                give(stage, src, dst, k, z).start()

    def taken(stage, n, src, dst):
        keep(n, src, dst).wait()
        for k in ORDER:
            give(stage, src, dst, k, 0).wait()

    def step(c, carry):
        outs = []
        for i in range(per):
            row = c * per + i
            for k in ORDER:
                keys(row, k).wait_recv()
            outs.append(row_backward(xt, kv, bias, db, dkv, row))
            for k in ORDER:
                partial(row, k).start()
        @pl.when(c == 0)
        def _():
            own_g.wait()
            finish(moved_g)

        lanes = pl.ds(aligned(c % 2, 128), 128)
        for r, piece in enumerate(by_member(outs, None, c)):
            attended = piece[0:32]
            gate = gates_all[c // 2, r, 0:32, lanes]
            grad_gated = gates_all[c // 2, r, 32:64, lanes]
            ya[c, r, 0:32] = piece[32:64].astype(BF16)
            ya[c, r, 32:64] = (grad_gated * attended * gate * (1.0 - gate)).astype(BF16)
            gated[c, r] = (gate * attended).astype(BF16)
        for z in range(2):

            @pl.when(c == 2 * z + 1)
            def _():
                give_half(6, 0, ya, ta, z)

        return carry

    lax.fori_loop(0, CHUNKS, step, 0)

    stream(0).start()
    stream(1).start()
    pair = []
    for b in range(2):
        pair += fan.partner(4 + b, db.at[:, pl.ds(aligned(b * 2 + 1 - p.core, 512), 512)], other.at[b])
    own_n.wait()
    finish(moved_n)
    dw, de = sc["dw"], sc["de"]
    dw[...] = jnp.zeros_like(dw)

    def total(c, carry):
        outs = []
        for i in range(per):
            row = c * per + i
            for k in ORDER:
                partial(row, k).wait_recv()
            t = dkv[row, :, here].astype(F32)
            for k in range(7):
                t = t + parts[k, row].astype(F32)
            outs.append(t)
        grad = jnp.concatenate([dw[0], dw[1]], axis=1)
        lanes = pl.ds(aligned(c % 2, 128), 128)
        for r, piece in enumerate(by_member(outs, yd, c)):
            hi, lo = halves(piece)
            n = normed_all[c // 2, r, :, lanes]
            grad = grad + mm(hi, n, NT) + mm(lo, n, NT)
        dw[0] = grad[:, :128]
        dw[1] = grad[:, 128:]
        return carry

    lax.fori_loop(0, 2, total, 0)
    give_half(8, 2, yd, td, 0)
    for b in range(2):
        pair[b].wait()
        mine[b] = (db[:, pl.ds(aligned(b * 2 + p.core, 512), 512)] + other[b]).astype(BF16)

    def bias_of(h):
        z, r = p.spot(h)
        return mine.at[z, pl.ds(aligned(r, 64), 64)]

    bias_back = fan.members(7, bias_of, lambda k: bo.at[p.h])
    own_m = pltpu.make_async_copy(bias_of(p.h), bo.at[p.h], local.at[1])
    own_m.start()

    def assemble(src, part):
        rows = slice(part * 32, part * 32 + 32)
        return jnp.concatenate([src[:, pp, rows, :].reshape(256, 128) for pp in range(2)], axis=1)

    own_s.wait()
    finish(moved_s)
    grad_qg = jnp.zeros((64, 256), F32)
    grad_o = jnp.zeros((32, 256), F32)
    for c in range(CHUNKS):
        lane = slice(c % 2 * 128, c % 2 * 128 + 128)
        for r in range(4):
            grad_qg = grad_qg + mm(ya[c, r], normed_all[c // 2, r, :, lane], NT)
            grad_o = grad_o + mm(gated[c, r], slope_all[c // 2, r, lane, :])
    for half in range(2):
        lane = slice(half * 128, half * 128 + 128)
        de[half, 0:64] = grad_qg[:, lane]
        de[half, 64:96] = grad_o[:, lane]
    first = Gather(p, fan, 18, de, sc["de_o"], sc["des"], oa)
    last = Gather(p, fan, 14, dw, sc["dw_o"], sc["dws"], ob)
    first.pair()
    first.block()
    lax.fori_loop(2, 3, total, 0)

    lax.fori_loop(3, 4, total, 0)
    last.pair()
    give_half(8, 2, yd, td, 1)
    taken(6, 0, ya, ta)
    grad_normed = mm(wq[...], assemble(ta, 0)) + mm(wg[...], assemble(ta, 1))
    last.block()

    own_m.wait()
    finish(bias_back)
    grad_bias = jnp.zeros((128, 128), F32)
    for n in range(4):
        stream(n).wait()
        part = bo[:, n * 16 : (n + 1) * 16, :].reshape(128, 512)
        for i in range(16):
            grad_bias = grad_bias + mm(only(part, 16, i), rows_buf[n % 2, i])
        if n + 2 < 4:
            stream(n + 2).start()
    ex, exm, exb = sc["ex"], sc["exm"], sc["exb"]
    ex[0:8, :] = jnp.sum(grad_bias.reshape(8, 16, 128), axis=1)
    first.member()
    last.member()

    taken(8, 2, yd, td)
    dk_hi, dk_lo = halves(assemble(td, 0))
    dv_hi, dv_lo = halves(assemble(td, 1))
    grad_normed = grad_normed + mm(wk[...], dk_hi) + mm(wk[...], dk_lo) + mm(wv[...], dv_hi) + mm(wv[...], dv_lo)
    hat = sc["hat"][...]
    by_gain = jnp.sum(jnp.transpose(grad_normed * hat), axis=0, keepdims=True)
    ex[8:16, :] = jnp.concatenate([by_gain[:, :128], by_gain[:, 128:], jnp.zeros((6, 128), F32)], axis=0)
    exm[p.h] = ex[...]
    extra = fan.members(22, lambda h: exm.at[p.h], lambda k: exm.at[p.h])

    scaled = grad_normed * sc["scale"][...]
    m1 = jnp.mean(scaled, axis=0, keepdims=True)
    m2 = jnp.mean(scaled * hat, axis=0, keepdims=True)
    align[...] = jnp.transpose(sc["inv"][0:1, :] * (scaled - m1 - hat * m2)).astype(BF16)

    finish(extra)
    exb[p.core * 8 + p.g] = sum_of(exm)
    piece = exb.at[p.core * 8 + p.g]
    extra = fan.partner(9, piece, piece)
    extra += fan.blocks(23, lambda g: piece, lambda k: piece)
    extra += fan.all(24, lambda g: piece, lambda k: piece, p.g, p.across)
    first.back_pair()
    last.back_pair()
    finish(extra)
    ex_out[0:16, :] = sum_of(exb)
    ex_out[16:24, :] = pbt[...].astype(F32)
    first.done()
    last.done()

    def drain(c, carry):
        for k in ORDER:
            keys(c, k).wait_send()
            partial(c, k).wait_send()
        return carry

    lax.fori_loop(0, 8, drain, 0)


def sum_of(ref):
    total = ref[0]
    for n in range(1, ref.shape[0]):
        total = total + ref[n]
    return total


def main(hom, slope, gain, wq, wk, wv, wg, wo, pbt, pair_rows):
    dma = pltpu.SemaphoreType.DMA
    vmem = pltpu.VMEM

    square = vmem((256, 256), F32)
    square_half = vmem((256, 256), BF16)
    scratch = {
        "rows": vmem((2, 16, 512, 128), BF16),
        "mask": vmem((16, 128, 128), BF16),
        "hom": square_half, "slope": square_half, "gain": vmem((1, 256), F32), "pbt": vmem((8, 128), BF16),
        "wq": square_half, "wk": square_half, "wv": square_half, "wg": square_half, "wo": square_half,
        "hat": square, "scale": square, "inv": vmem((8, 256), F32), "gates": vmem((8, 64, 256), F32),
        "normed": square_half,
        "t": vmem((8, 128, 256), BF16),
        "b": vmem((8, 64, 512), BF16),
        "xr": vmem((2, 4, 128, 256), BF16),
        "xt": vmem((8, 128, 256), BF16),
        "kv": vmem((8, 64, 2048), BF16),
        "bias": vmem((256, 2048), BF16),
        "db": vmem((256, 2048), F32),
        "dkv": vmem((8, 64, 2048), BF16),
        "parts": vmem((7, 8, 64, 256), BF16),
        "ya": vmem((4, 4, 64, 128), BF16),
        "gated": vmem((4, 4, 32, 128), BF16),
        "yd": vmem((4, 4, 64, 128), F32),
        "ta": vmem((8, 2, 64, 128), BF16),
        "td": vmem((8, 2, 64, 128), F32),
        "mine": vmem((2, 256, 512), BF16),
        "other": vmem((2, 256, 512), F32),
        "xn": vmem((2, 4, 256, 256), BF16), "xs": vmem((2, 4, 256, 256), BF16), "xg": vmem((2, 4, 64, 256), F32),
        "de": vmem((2, 96, 128), F32), "de_o": vmem((96, 128), F32), "des": vmem((8, 96, 128), F32),
        "dw": vmem((2, 64, 128), F32), "dw_o": vmem((64, 128), F32), "dws": vmem((8, 64, 128), F32),
        "ex": vmem((16, 128), F32),
        "exm": vmem((8, 16, 128), F32), "exb": vmem((16, 16, 128), F32),
    }
    sems = {
        "hbm": dma((2,)), "local": dma((6,)), "in": dma((9,)),
        "send": dma((25, 7)), "recv": dma((25, 7)),
        "ks": dma((8, 7)), "kr": dma((8, 7)),
        "es": dma((8, 7)), "er": dma((8, 7)),
    }
    return pl.pallas_call(
        main_kernel,
        out_shape=(
            jax.ShapeDtypeStruct((256, 256), BF16),
            jax.ShapeDtypeStruct((8, 64, 512), BF16),
            jax.ShapeDtypeStruct((2, 8, 96, 128), F32),
            jax.ShapeDtypeStruct((2, 8, 64, 128), F32),
            jax.ShapeDtypeStruct((24, 128), F32),
        ),
        in_specs=[HB] * 10,
        out_specs=(VM,) * 5,
        scratch_shapes=[scratch, sems],
        compiler_params=params(0),
        name="main",
    )(*[pltpu.with_memory_space_constraint(a, pltpu.HBM) for a in (hom, slope, gain, wq, wk, wv, wg, wo, pbt, pair_rows)])


def tail_kernel(bo, align, oa, ob, ex, pair, align_out, q, k, v, g, o, gain, bias, base, kv, sem):
    n = pl.program_id(0)
    moves = [(align, align_out), (ex.at[8:10], gain), (ex.at[0:8], bias)]
    moves += [(kv.at[i], w) for i, w in enumerate((k, v, q, g, o))]
    copies = [pltpu.make_async_copy(a, b, sem.at[i]) for i, (a, b) in enumerate(moves)]

    @pl.when(n == 0)
    def _():
        for half in range(2):
            lane = slice(half * 128, half * 128 + 128)
            for i, (ref, row) in enumerate(((ob, 0), (ob, 32), (oa, 0), (oa, 32))):
                kv[i, lane, :] = jnp.transpose(ref[half, :, row : row + 32, :].reshape(256, 128))
            kv[4, :, lane] = oa[half, :, 64:96, :].reshape(256, 128)
        for c in copies:
            c.start()
        spreaded = spread(ex[16:24, :])
        for i in range(16):
            base[i // 8, :, i % 8 * 128 : i % 8 * 128 + 128] = only(spreaded, 16, i).astype(BF16)

    part = jnp.transpose(bo[:, pl.ds(pl.multiple_of(n // 2 * 16, 16), 16), :].reshape(128, 512))
    for i in range(4):
        out = mm(part, base[n % 2, :, i * 256 : i * 256 + 256]).astype(BF16)
        pair[2 * i] = out[:, :128]
        pair[2 * i + 1] = out[:, 128:]

    @pl.when(n == 7)
    def _():
        for c in copies:
            c.wait()


def tail(bo, align, oa, ob, ex):
    square = jax.ShapeDtypeStruct((256, 256), F32)
    return pl.pallas_call(
        tail_kernel,
        grid=(8,),
        out_shape=(
            jax.ShapeDtypeStruct((64, 512, 128), BF16),
            jax.ShapeDtypeStruct((256, 256), BF16),
            square, square, square, square, square,
            jax.ShapeDtypeStruct((2, 128), F32),
            jax.ShapeDtypeStruct((8, 128), F32),
        ),
        in_specs=[VM] * 5,
        out_specs=(pl.BlockSpec((8, 512, 128), lambda n: (n, 0, 0)),) + (HB,) * 8,
        scratch_shapes=[pltpu.VMEM((2, 128, 1024), BF16), pltpu.VMEM((5, 256, 256), F32), pltpu.SemaphoreType.DMA((8,))],
        compiler_params=pltpu.CompilerParams(vmem_limit_bytes=32 * 1024 * 1024),
        name="tail",
    )(bo, align, oa, ob, ex)


def body(
    homolog_embedding,
    pair_input_rows,
    incoming_slope,
    rescale_factor,
    probe_weights,
    lookup_weights,
    content_weights,
    sigmoid_weights,
    final_projection,
    pair_bias_matrix,
):
    rows, toks, width = homolog_embedding.shape
    align, db_own, oa, ob, extra = main(
        homolog_embedding.reshape(-1, width),
        incoming_slope.reshape(-1, width),
        rescale_factor.reshape(1, width),
        probe_weights,
        lookup_weights,
        content_weights,
        sigmoid_weights,
        final_projection,
        pair_bias_matrix.T,
        pair_input_rows,
    )
    pair_grad, align, grad_q, grad_k, grad_v, grad_g, grad_o, gain, bias = tail(
        db_own, align, oa, ob, extra
    )
    return (
        align.reshape(rows, toks, width),
        pair_grad,
        gain.reshape(width),
        grad_q,
        grad_k,
        grad_v,
        grad_g,
        grad_o,
        bias.T,
    )


def solution(mesh):
    in_specs = (
        P("seq", "res", None),
        P("res", "seq", None),
        P("seq", "res", None),
        P(),
        P(),
        P(),
        P(),
        P(),
        P(),
        P(),
    )
    out_specs = (P("seq", "res", None), P("res", "seq", None), P(), P(), P(), P(), P(), P(), P())
    return jax.shard_map(body, mesh=mesh, in_specs=in_specs, out_specs=out_specs, check_vma=False)
```
